32 devices in a mesh: fsdp: 4 (over y, core), ctx: 4 (over z), tp: 2 (over x).
Axes of the slice: x: 2, y: 2, z: 4, core: 2. Of those that a mesh axis runs over, the one named last changes fastest.
Arguments:
- tokens: bfloat16 [4, 4096, 1024], P('fsdp', 'ctx'), may hold values from -6 to 6
- cotangent: bfloat16 [4, 4096, 1024], P('fsdp', 'ctx'), may hold values from -6 to 6
- block_order: int32 [8], replicated, may hold values from 0 to 7, as said below
- positions: int32 [4, 4096], P('fsdp', 'ctx'), may hold values from 0 to 8190, as said below
- attn_gain: bfloat16 [1024], P('fsdp'), may hold values from 0.5 to 1.5
- w_query: bfloat16 [1024, 1024], P('fsdp', 'tp'), may hold values from -0.1875 to 0.1875
- key_weight: bfloat16 [1024, 512], P('fsdp', 'tp'), may hold values from -0.1875 to 0.1875
- value_weight: bfloat16 [1024, 512], P('fsdp', 'tp'), may hold values from -0.1875 to 0.1875
- query_gain: bfloat16 [64], P('fsdp'), may hold values from 0.25 to 1.75
- key_gain: bfloat16 [64], P('fsdp'), may hold values from 0.25 to 1.75
- w_out: bfloat16 [1024, 1024], P('tp', 'fsdp'), may hold values from -1.5 to 1.5
- ffn_gain: bfloat16 [1024], P('fsdp'), may hold values from 0.5 to 1.5
- w_gate: bfloat16 [1024, 4608], P('fsdp', 'tp'), may hold values from -0.1875 to 0.1875
- w_up: bfloat16 [1024, 4608], P('fsdp', 'tp'), may hold values from -0.1875 to 0.1875
- w_down: bfloat16 [4608, 1024], P('tp', 'fsdp'), may hold values from -0.09375 to 0.09375
Outputs:
- output: bfloat16 [4, 4096, 1024], P('fsdp', 'ctx')
- input_grad: float32 [4, 4096, 1024], P('fsdp', 'ctx')
- attn_gain_grad: float32 [1024], P('fsdp')
- w_query_grad: float32 [1024, 1024], P('fsdp', 'tp')
- w_key_grad: float32 [1024, 512], P('fsdp', 'tp')
- w_value_grad: float32 [1024, 512], P('fsdp', 'tp')
- query_gain_grad: float32 [64], P('fsdp')
- key_gain_grad: float32 [64], P('fsdp')
- w_out_grad: float32 [1024, 1024], P('tp', 'fsdp')
- ffn_gain_grad: float32 [1024], P('fsdp')
- w_gate_grad: float32 [1024, 4608], P('fsdp', 'tp')
- w_up_grad: float32 [1024, 4608], P('fsdp', 'tp')
- w_down_grad: float32 [4608, 1024], P('tp', 'fsdp')
The draws below stay inside these ranges and needn't reach their ends.
Inputs may be any that keep to these rules, and one draw needn't show every extreme that they name: `block_order`: every block number appears once; the slot pair 2c, 2c + 1 holds blocks b and 7 - b for some b. `positions`: in a sequence's natural token order (see block_order) the first position is 0, each next one is larger by 1, 2 or 3, and the last is 8190; stored in the slot order of tokens.
All inputs are finite; a program needn't handle non-finite values.
Results may differ from the reference program's by a relative error of at most 0.023.
Values may be sent and summed in bfloat16 or wider, within the bound.
No kernel may reach another device: no remote copies, remote signals or barrier semaphores. Data moves between devices by JAX's collectives and lax.ppermute only.
A program may use at most 192 MiB of HBM per device.

```python
import jax
import jax.numpy as jnp
from jax import lax

MODEL_WIDTH = 1024
QUERY_HEADS = 16
KEY_VALUE_HEADS = 8
HEAD_SIZE = 64
FF = 4608
SEQUENCE_LENGTH = 4096
SEQS = 4
BLOCKS = 8
N_CTX = 4


def draw_ordering(key):
    pair_count = BLOCKS // 2
    paired = jax.random.permutation(jax.random.fold_in(key, 11), pair_count).astype(jnp.int32)
    flipped = jax.random.randint(jax.random.fold_in(key, 12), (pair_count,), 0, 2).astype(jnp.int32)
    leading = jnp.where(flipped == 1, BLOCKS - 1 - paired, paired)
    second = BLOCKS - 1 - leading
    return jnp.stack([leading, second], axis=1).reshape(BLOCKS).astype(jnp.int32)


def draw_block_order(key, part):
    return draw_ordering(key)


def draw_positions(key, part):
    ordering = draw_ordering(key)
    block_len = SEQUENCE_LENGTH // BLOCKS
    dropped = jax.random.randint(jax.random.fold_in(key, 13), (SEQS, SEQUENCE_LENGTH), 0, 2).astype(jnp.int32)
    indices = jnp.arange(SEQUENCE_LENGTH, dtype=jnp.int32)
    ends = jnp.logical_or(indices == 0, indices == SEQUENCE_LENGTH - 1)
    dropped = jnp.where(ends[None, :], 0, dropped)
    natural = 2 * indices[None, :] - dropped
    slot_nat = ordering[indices // block_len] * block_len + indices % block_len
    return jnp.take(natural, slot_nat, axis=1).astype(jnp.int32)


def levels(own_key, extent, split, least, largest):
    def one(axis_at, parts):
        draws = jax.random.uniform(jax.random.fold_in(jax.random.fold_in(own_key, 6), axis_at), (parts,), jnp.float32, least / len(split), largest / len(split))
        return jnp.repeat(jnp.exp(draws), extent[axis_at] // parts).reshape((-1,) + (1,) * (len(extent) - axis_at - 1))

    level = one(*split[0])
    for cut in split[1:]:
        level = level * one(*cut)
    return level


def normal_values(own_key, extent, scale, reach, pieces=(), kind=jnp.bfloat16):
    values = jax.random.normal(own_key, extent, jnp.float32) * scale
    if len(pieces) > 0:
        values = levels(own_key, extent, pieces, -0.22, 0.18) * values
    return jnp.clip(values, min=-reach, max=reach).astype(kind)


def setup_inputs(seed: int = 0) -> dict:
    key_of = jax.random.split(jax.random.key(seed), 16)
    tokens = normal_values(key_of[0], (SEQS, SEQUENCE_LENGTH, MODEL_WIDTH), 1.0, 6.0, ((0, 4), (1, 4)))
    cotangent = normal_values(key_of[1], (SEQS, SEQUENCE_LENGTH, MODEL_WIDTH), 1.0, 6.0, ((0, 4), (1, 4)))
    block_order = draw_block_order(jax.random.fold_in(key_of[15], 71), 0)
    positions = draw_positions(jax.random.fold_in(key_of[15], 71), 0)
    attn_gain = jnp.clip(1.0 + 0.1 * jax.random.normal(key_of[4], (MODEL_WIDTH,), jnp.float32), 0.5, 1.5).astype(jnp.bfloat16)
    w_query = normal_values(key_of[5], (MODEL_WIDTH, QUERY_HEADS * HEAD_SIZE), MODEL_WIDTH ** -0.5, 0.1875, ((0, 4), (1, 2)))
    key_weight = normal_values(key_of[6], (MODEL_WIDTH, KEY_VALUE_HEADS * HEAD_SIZE), MODEL_WIDTH ** -0.5, 0.1875, ((0, 4), (1, 2)))
    value_weight = normal_values(key_of[7], (MODEL_WIDTH, KEY_VALUE_HEADS * HEAD_SIZE), MODEL_WIDTH ** -0.5, 0.1875, ((0, 4), (1, 2)))
    query_gain = jnp.clip(1.0 + 0.15 * jax.random.normal(key_of[8], (HEAD_SIZE,), jnp.float32), 0.25, 1.75).astype(jnp.bfloat16)
    key_gain = jnp.clip(1.0 + 0.15 * jax.random.normal(key_of[9], (HEAD_SIZE,), jnp.float32), 0.25, 1.75).astype(jnp.bfloat16)
    w_out = normal_values(key_of[10], (QUERY_HEADS * HEAD_SIZE, MODEL_WIDTH), (max(1, QUERY_HEADS * HEAD_SIZE * 64 // SEQUENCE_LENGTH)) ** -0.5, 1.5, ((0, 2), (1, 4)))
    ffn_gain = jnp.clip(1.0 + 0.1 * jax.random.normal(key_of[11], (MODEL_WIDTH,), jnp.float32), 0.5, 1.5).astype(jnp.bfloat16)
    w_gate = normal_values(key_of[12], (MODEL_WIDTH, FF), MODEL_WIDTH ** -0.5, 0.1875, ((0, 4), (1, 2)))
    w_up = normal_values(key_of[13], (MODEL_WIDTH, FF), MODEL_WIDTH ** -0.5, 0.1875, ((0, 4), (1, 2)))
    w_down = normal_values(key_of[14], (FF, MODEL_WIDTH), FF ** -0.5, 0.09375, ((0, 2), (1, 4)))
    return dict(tokens=tokens, cotangent=cotangent, block_order=block_order, positions=positions, attn_gain=attn_gain, w_query=w_query, key_weight=key_weight, value_weight=value_weight, query_gain=query_gain, key_gain=key_gain, w_out=w_out, ffn_gain=ffn_gain, w_gate=w_gate, w_up=w_up, w_down=w_down)


EPSILON = 1e-05
ROPE_BASE = 1000000.0
SCORE_SCALE = 0.125
PRECISE = lax.Precision.HIGHEST

@jax.custom_vjp
def lower_precision(v):
    return lax.optimization_barrier(v.astype(jnp.bfloat16)).astype(jnp.float32)

@jax.custom_vjp
def lower_precision_back(v):
    return v

def low_keep(v):
    return (lower_precision(v), None)

def low_pass(kept, grad):
    return (grad,)

def back_keep(v):
    return (v, None)

def back_low(kept, grad):
    return (lower_precision(grad),)
lower_precision.defvjp(low_keep, low_pass)
lower_precision_back.defvjp(back_keep, back_low)

def highest_product(left, right):
    return jnp.dot(left, right, precision=PRECISE, preferred_element_type=jnp.float32)

def norm_rows(value, gain):
    return value * lax.rsqrt(lax.optimization_barrier(jnp.mean(value * value, axis=-1, keepdims=True)) + EPSILON) * gain

def rotate_half(value):
    middle = value.shape[-1] // 2
    return jnp.concatenate([-value[..., middle:], value[..., :middle]], axis=-1)

def rope_tables(positions):
    middle = HEAD_SIZE // 2
    freqs = ROPE_BASE ** (-(jnp.arange(middle, dtype=jnp.float32) * 2.0) / HEAD_SIZE)
    angles = positions.astype(jnp.float32)[..., None] * freqs
    angles = jnp.concatenate([angles, angles], axis=-1)
    return (jnp.cos(angles), jnp.sin(angles))

def apply_rotary(value, cosine, sine):
    return value * cosine + rotate_half(value) * sine

def attention(query_rows, key_rows, value_tokens, natural):
    group_width = QUERY_HEADS // KEY_VALUE_HEADS
    query_block = min(512, SEQUENCE_LENGTH)
    block_count = SEQUENCE_LENGTH // query_block
    grouped_heads = query_rows.reshape(block_count, query_block, KEY_VALUE_HEADS, group_width, HEAD_SIZE)
    query_pos = natural.reshape(block_count, query_block)

    def one_block(packed):
        q_part, q_pos = packed
        scores = lower_precision_back(jnp.einsum('qgrd,kgd->grqk', q_part, key_rows, precision=PRECISE) * SCORE_SCALE)
        visible = natural[None, :] <= q_pos[:, None]
        scores = jnp.where(visible, scores, -1e+30)
        weights = lower_precision(jax.nn.softmax(scores, axis=-1))
        mixed = jnp.einsum('grqk,kgd->qgrd', weights, value_tokens, precision=PRECISE)
        return mixed.reshape(query_block, QUERY_HEADS * HEAD_SIZE)
    return lax.map(jax.checkpoint(one_block), (grouped_heads, query_pos)).reshape(SEQUENCE_LENGTH, QUERY_HEADS * HEAD_SIZE)

def sequence_forward(inputs_f, pos_seq, natural, params_f):
    gain_attn, query_mat, key_matrix, value_matrix, gain_query, gain_key, out_mat, gain_ffn, gate_mat, up_mat, down_mat = params_f
    normed_input = lower_precision(norm_rows(inputs_f, gain_attn))
    query_raw = lower_precision_back(highest_product(normed_input, query_mat)).reshape(SEQUENCE_LENGTH, QUERY_HEADS, HEAD_SIZE)
    key_unrotated = lower_precision_back(highest_product(normed_input, key_matrix)).reshape(SEQUENCE_LENGTH, KEY_VALUE_HEADS, HEAD_SIZE)
    value_tokens = lower_precision(lower_precision_back(highest_product(normed_input, value_matrix))).reshape(SEQUENCE_LENGTH, KEY_VALUE_HEADS, HEAD_SIZE)
    cosine, sine = rope_tables(pos_seq)
    cosine = cosine[:, None, :]
    sine = sine[:, None, :]
    query_rows = lower_precision(apply_rotary(norm_rows(query_raw, gain_query), cosine, sine))
    key_rows = lower_precision(apply_rotary(norm_rows(key_unrotated, gain_key), cosine, sine))
    mixed = attention(query_rows, key_rows, value_tokens, natural)
    attn_out = lower_precision_back(highest_product(lower_precision(lower_precision_back(mixed)), out_mat))
    resid = inputs_f + attn_out
    normed_two = lower_precision(norm_rows(resid, gain_ffn))
    gate_val = lower_precision_back(highest_product(normed_two, gate_mat))
    up_val = lower_precision_back(highest_product(normed_two, up_mat))
    hidden = lower_precision(jax.nn.silu(gate_val) * up_val)
    return resid + lower_precision_back(highest_product(hidden, down_mat))

def reference(tokens, cotangent, block_order, positions, attn_gain, w_query, key_weight, value_weight, query_gain, key_gain, w_out, ffn_gain, w_gate, w_up, w_down):
    params = tuple((weight_in.astype(jnp.float32) for weight_in in (attn_gain, w_query, key_weight, value_weight, query_gain, key_gain, w_out, ffn_gain, w_gate, w_up, w_down)))
    block_len = SEQUENCE_LENGTH // (2 * N_CTX)
    slot_ids = jnp.arange(SEQUENCE_LENGTH, dtype=jnp.int32)
    natural = (block_order[slot_ids // block_len] * block_len + slot_ids % block_len).astype(jnp.int32)

    def forward(inputs_all, params_f):

        def one_sequence(packed):
            return sequence_forward(packed[0], packed[1], natural, params_f)
        return lax.map(jax.checkpoint(one_sequence), (inputs_all, positions))
    outputs, pullback = jax.vjp(forward, tokens.astype(jnp.float32), params)
    input_grad, grads = pullback(cotangent.astype(jnp.float32))
    grad_attn_gain, grad_query, grad_key, grad_value, grad_query_gain, grad_key_gain, grad_out, grad_ffn_gain, grad_gate, grad_up, grad_down = grads
    return (outputs.astype(jnp.bfloat16), input_grad, grad_attn_gain, grad_query, grad_key, grad_value, grad_query_gain, grad_key_gain, grad_out, grad_ffn_gain, grad_gate, grad_up, grad_down)
```

```python
import functools

import jax
import jax.numpy as jnp
from jax import lax
from jax.experimental import pallas as pl
from jax.experimental.pallas import tpu as pltpu
from jax.sharding import PartitionSpec as P

HD = 64
EPSILON = 1e-05
ROPE_BASE = 1000000.0
LOG2E = 1.4426950408889634
SCALE2 = 0.125 * LOG2E
NT = (((1,), (1,)), ((), ()))
NN = (((1,), (0,)), ((), ()))
TN = (((0,), (0,)), ((), ()))
F32, BF16 = jnp.float32, jnp.bfloat16


def mm(a, b, dims=NN):
    return lax.dot_general(a, b, dims, preferred_element_type=F32)


def half(shape, which):
    lane = lax.broadcasted_iota(jnp.int32, shape, len(shape) - 1)
    return (lane < HD) if which == 0 else (lane >= HD)


def pieces(own, meta, block):
    at = [pl.multiple_of(meta[n], block) for n in range(4)]
    if own:
        return [(at[0], at[0], True), (at[1], at[0], False), (at[1], at[1], True)]
    return [(at[0], at[1], False), (at[2], at[3], False)]


def attend_body(own, first, last, block, meta, q_ref, kv_ref, *rest):
    rest = list(rest)
    given = None if first else rest.pop(0)
    if last:
        mixb_ref, mix_ref, lse_ref, acc = rest
    else:
        (acc,) = rest
    acc[...] = jnp.zeros_like(acc) if first else given[...]
    for q_at, k_at, diagonal in pieces(own, meta, block):
        kt = kv_ref[pl.ds(k_at, block), 0:128]
        vt = kv_ref[pl.ds(k_at, block), 128:256]
        one = jnp.ones((block, HD), BF16)
        for hh in range(2):
            kh = kt[:, HD * hh : HD * hh + HD]
            vh = vt[:, HD * hh : HD * hh + HD]
            kd = jnp.concatenate([kh, kh], axis=1)
            vx = (jnp.concatenate([vh, one], axis=1), jnp.concatenate([one, vh], axis=1))
            qt = q_ref[pl.ds(q_at, block), 128 * hh : 128 * hh + 128]
            for r in range(2):
                qr = jnp.where(half((block, 128), r), qt, jnp.zeros_like(qt))
                p = jnp.exp2(mm(qr, kd, NT) * SCALE2)
                if diagonal:
                    row = lax.broadcasted_iota(jnp.int32, p.shape, 0)
                    col = lax.broadcasted_iota(jnp.int32, p.shape, 1)
                    p = jnp.where(col <= row, p, 0.0)
                c = 256 * hh + 128 * r
                acc[pl.ds(q_at, block), c : c + 128] += mm(p.astype(BF16), vx[r])
    if last:
        rows = acc.shape[0]
        lane = lax.broadcasted_iota(jnp.int32, (8, 128), 1)
        sub = lax.broadcasted_iota(jnp.int32, (8, 128), 0)
        total = jnp.zeros((8, rows), F32)
        for hh in range(2):
            out = []
            for r in range(2):
                a = acc[:, 256 * hh + 128 * r : 256 * hh + 128 * r + 128]
                out.append(a / pltpu.roll(a, HD, 1))
                pick = jnp.where((lane == (HD if r == 0 else 0)) & (sub == 2 * hh + r), 1.0, 0.0)
                total += lax.dot_general(
                    pick, a, NT, precision=lax.Precision.HIGHEST, preferred_element_type=F32
                )
            mix = jnp.where(half((rows, 128), 0), out[0], out[1])
            mix_ref[:, 128 * hh : 128 * hh + 128] = mix
            mixb_ref[:, 128 * hh : 128 * hh + 128] = mix.astype(BF16)
        lse_ref[0] = jnp.log2(jnp.where(sub[:, 0:1] < 4, total, 1.0))


def attend(meta, q, kv, acc, own, last, block):
    rows = q.shape[0]
    pairs = kv.shape[1] // 256
    first = acc is None
    args = [meta, q, kv]
    wide = pl.BlockSpec((rows, 512), lambda g, m: (0, g))
    slim = pl.BlockSpec((rows, 256), lambda g, m: (0, g))
    in_specs = [slim, slim]
    if not first:
        in_specs.append(wide)
        args.append(acc)
    if last:
        out_shape = (
            jax.ShapeDtypeStruct((rows, pairs * 256), BF16),
            jax.ShapeDtypeStruct((rows, pairs * 256), F32),
            jax.ShapeDtypeStruct((pairs, 8, rows), F32),
        )
        out_specs = (slim, slim, pl.BlockSpec((1, 8, rows), lambda g, m: (g, 0, 0)))
        scratch = [pltpu.VMEM((rows, 512), F32)]
    else:
        out_shape = jax.ShapeDtypeStruct((rows, pairs * 512), F32)
        out_specs = wide
        scratch = []
    work = 2 * block * block * pairs * 4
    return pl.pallas_call(
        functools.partial(attend_body, own, first, last, block),
        out_shape=out_shape,
        grid_spec=pltpu.PrefetchScalarGridSpec(
            num_scalar_prefetch=1,
            grid=(pairs,),
            in_specs=in_specs,
            out_specs=out_specs,
            scratch_shapes=scratch,
        ),
        compiler_params=pltpu.CompilerParams(vmem_limit_bytes=40 << 20),
        cost_estimate=pl.CostEstimate(
            flops=work * 1024, bytes_accessed=12 << 20, transcendentals=work
        ),
        name="attend",
    )(*args)


def attend_back_body(own, first, block, meta, q_ref, do_ref, kv_ref, lse_ref, dlt_ref, *rest):
    rest = list(rest)
    given = None if first else rest.pop(0)
    dq, dkv_ref, dka, dva = rest
    dq[...] = jnp.zeros_like(dq) if first else given[...]
    dka[...] = jnp.zeros_like(dka)
    dva[...] = jnp.zeros_like(dva)
    for q_at, k_at, diagonal in pieces(own, meta, block):
        kt = kv_ref[pl.ds(k_at, block), 0:128]
        vt = kv_ref[pl.ds(k_at, block), 128:256]
        zero = jnp.zeros((block, HD), BF16)
        for hh in range(2):
            kh = kt[:, HD * hh : HD * hh + HD]
            vh = vt[:, HD * hh : HD * hh + HD]
            kx = (jnp.concatenate([kh, zero], axis=1), jnp.concatenate([zero, kh], axis=1))
            vx = (jnp.concatenate([vh, zero], axis=1), jnp.concatenate([zero, vh], axis=1))
            c = 128 * hh
            qt = q_ref[pl.ds(q_at, block), c : c + 128]
            dt = do_ref[pl.ds(q_at, block), c : c + 128]
            dvs, dks, dqs = [], [], None
            for r in range(2):
                row = 2 * hh + r
                lse = lse_ref[0, row : row + 1, pl.ds(q_at, block)]
                dlt = dlt_ref[0, row : row + 1, pl.ds(q_at, block)]
                p = jnp.exp2(mm(kx[r], qt, NT) * SCALE2 - lse)
                if diagonal:
                    key = lax.broadcasted_iota(jnp.int32, p.shape, 0)
                    query = lax.broadcasted_iota(jnp.int32, p.shape, 1)
                    p = jnp.where(key <= query, p, 0.0)
                ds = (p * (mm(vx[r], dt, NT) - dlt)).astype(BF16)
                dvs.append(mm(p.astype(BF16), dt))
                dks.append(mm(ds, qt))
                term = mm(ds, kx[r], TN)
                dqs = term if dqs is None else dqs + term
            left = half((block, 128), 0)
            dva[pl.ds(k_at, block), c : c + 128] += jnp.where(left, dvs[0], dvs[1])
            dka[pl.ds(k_at, block), c : c + 128] += jnp.where(left, dks[0], dks[1])
            dq[pl.ds(q_at, block), c : c + 128] += dqs
    for at, ref, scale in ((0, dka, 0.125), (128, dva, 1.0)):
        a = ref[...]
        a = jnp.concatenate([a[:, 0:64] + a[:, 64:128], a[:, 128:192] + a[:, 192:256]], axis=1)
        dkv_ref[:, at : at + 128] = (a * scale).astype(dkv_ref.dtype)


def attend_back(meta, q, do, kv, lse, dlt, dq, own, block):
    rows = q.shape[0]
    pairs = kv.shape[1] // 256
    first = dq is None
    slim = pl.BlockSpec((rows, 256), lambda g, m: (0, g))
    line = pl.BlockSpec((1, 8, rows), lambda g, m: (g, 0, 0))
    in_specs = [slim, slim, slim, line, line]
    args = [meta, q, do, kv, lse, dlt]
    if not first:
        in_specs.append(slim)
        args.append(dq)
    work = 2 * block * block * pairs * 4
    return pl.pallas_call(
        functools.partial(attend_back_body, own, first, block),
        out_shape=(
            jax.ShapeDtypeStruct((rows, pairs * 256), F32),
            jax.ShapeDtypeStruct((rows, pairs * 256), F32 if own else BF16),
        ),
        grid_spec=pltpu.PrefetchScalarGridSpec(
            num_scalar_prefetch=1,
            grid=(pairs,),
            in_specs=in_specs,
            out_specs=(slim, slim),
            scratch_shapes=[pltpu.VMEM((rows, 256), F32), pltpu.VMEM((rows, 256), F32)],
        ),
        compiler_params=pltpu.CompilerParams(vmem_limit_bytes=40 << 20),
        cost_estimate=pl.CostEstimate(
            flops=work * 2048, bytes_accessed=12 << 20, transcendentals=work
        ),
        name="attend_back",
    )(*args)


def head_mean(u):
    a = lax.broadcasted_iota(jnp.int32, (128, 128), 0) // HD
    b = lax.broadcasted_iota(jnp.int32, (128, 128), 1) // HD
    ones = jnp.where(a == b, 1.0, 0.0).astype(BF16)
    high = u.astype(BF16)
    low = (u - high.astype(F32)).astype(BF16)
    return (mm(high, ones) + mm(low, ones)) * (1.0 / HD)


def turn(u):
    lane = lax.broadcasted_iota(jnp.int32, u.shape, 1)
    return jnp.where(lane % HD < HD // 2, pltpu.roll(u, 96, 1), pltpu.roll(u, 32, 1))


def rope_body(q_ref, k_ref, v_ref, cos_ref, sin_ref, gain_ref, qo_ref, kv_ref):
    cos, sin = cos_ref[...], sin_ref[...]

    def one(u, gain):
        n = u * lax.rsqrt(head_mean(u * u) + EPSILON) * gain
        return (n * cos + turn(n) * sin).astype(BF16)

    for t in range(q_ref.shape[1] // 128):
        qo_ref[:, 128 * t : 128 * t + 128] = one(q_ref[:, 128 * t : 128 * t + 128], gain_ref[0:1])
    for t in range(k_ref.shape[1] // 128):
        kv_ref[:, 256 * t : 256 * t + 128] = one(k_ref[:, 128 * t : 128 * t + 128], gain_ref[1:2])
        kv_ref[:, 256 * t + 128 : 256 * t + 256] = v_ref[:, 128 * t : 128 * t + 128]


def rope(q_raw, k_raw, v, cos, sin, gains, step):
    rows, qw = q_raw.shape
    kw = k_raw.shape[1]
    spec = lambda w: pl.BlockSpec((step, w), lambda i: (i, 0))
    return pl.pallas_call(
        rope_body,
        out_shape=(
            jax.ShapeDtypeStruct((rows, qw), BF16),
            jax.ShapeDtypeStruct((rows, 2 * kw), BF16),
        ),
        grid=(rows // step,),
        in_specs=[spec(qw), spec(kw), spec(kw), spec(128), spec(128)]
        + [pl.BlockSpec((8, 128), lambda i: (0, 0))],
        out_specs=(spec(qw), spec(2 * kw)),
        cost_estimate=pl.CostEstimate(
            flops=rows * qw * 800, bytes_accessed=rows * qw * 12, transcendentals=rows * qw
        ),
        name="rope",
    )(q_raw, k_raw, v, cos, sin, gains)


def rope_back_body(terms, dq_ref, q_ref, k_ref, cos_ref, sin_ref, gain_ref, *rest):
    dkv_refs, (out_ref, gg_ref) = rest[:terms], rest[terms:]
    cos, sin = cos_ref[...], sin_ref[...]

    @pl.when(pl.program_id(0) == 0)
    def _():
        gg_ref[...] = jnp.zeros_like(gg_ref)

    def one(d, u, row):
        gain = gain_ref[row : row + 1]
        dn = d * cos + turn(d * sin)
        r = lax.rsqrt(head_mean(u * u) + EPSILON)
        gd = gain * dn
        gg_ref[row : row + 1] += jnp.sum(dn * u * r, axis=0, keepdims=True)
        return (r * gd - u * (r * r * r) * head_mean(u * gd)).astype(BF16)

    qw, kw = q_ref.shape[1], k_ref.shape[1]
    for t in range(qw // 128):
        c = slice(128 * t, 128 * t + 128)
        out_ref[:, c] = one(dq_ref[:, c] * 0.125, q_ref[:, c], 0)
    for t in range(kw // 128):
        dk = sum(ref[:, 256 * t : 256 * t + 128].astype(F32) for ref in dkv_refs)
        dv = sum(ref[:, 256 * t + 128 : 256 * t + 256].astype(F32) for ref in dkv_refs)
        out_ref[:, qw + 128 * t : qw + 128 * t + 128] = one(dk, k_ref[:, 128 * t : 128 * t + 128], 1)
        out_ref[:, qw + kw + 128 * t : qw + kw + 128 * t + 128] = dv.astype(BF16)


def rope_back(dq, q_raw, k_raw, cos, sin, gains, dkvs, step):
    rows, qw = q_raw.shape
    kw = k_raw.shape[1]
    spec = lambda w: pl.BlockSpec((step, w), lambda i: (i, 0))
    fixed = pl.BlockSpec((8, 128), lambda i: (0, 0))
    return pl.pallas_call(
        functools.partial(rope_back_body, len(dkvs)),
        out_shape=(
            jax.ShapeDtypeStruct((rows, qw + 2 * kw), BF16),
            jax.ShapeDtypeStruct((8, 128), F32),
        ),
        grid=(rows // step,),
        in_specs=[spec(qw), spec(qw), spec(kw), spec(128), spec(128), fixed]
        + [spec(2 * kw)] * len(dkvs),
        out_specs=(spec(qw + 2 * kw), fixed),
        cost_estimate=pl.CostEstimate(
            flops=rows * qw * 1600, bytes_accessed=rows * qw * 20, transcendentals=rows * qw
        ),
        name="rope_back",
    )(dq, q_raw, k_raw, cos, sin, gains, *dkvs)


def delta_body(do_ref, mix_ref, out_ref):
    lane = lax.broadcasted_iota(jnp.int32, (8, 128), 1) // HD
    sub = lax.broadcasted_iota(jnp.int32, (8, 128), 0)
    total = jnp.zeros(out_ref.shape[1:], F32)
    for hh in range(2):
        x = do_ref[:, 128 * hh : 128 * hh + 128].astype(F32) * mix_ref[:, 128 * hh : 128 * hh + 128]
        pick = jnp.where(sub == 2 * hh + lane, 1.0, 0.0)
        total += lax.dot_general(
            pick, x, NT, precision=lax.Precision.HIGHEST, preferred_element_type=F32
        )
    out_ref[0] = total


def delta_rows(do, mix):
    rows, width = do.shape
    pairs = width // 256
    slim = pl.BlockSpec((rows, 256), lambda g: (0, g))
    return pl.pallas_call(
        delta_body,
        out_shape=jax.ShapeDtypeStruct((pairs, 8, rows), F32),
        grid=(pairs,),
        in_specs=[slim, slim],
        out_specs=pl.BlockSpec((1, 8, rows), lambda g: (g, 0, 0)),
        cost_estimate=pl.CostEstimate(
            flops=rows * width * 96, bytes_accessed=rows * width * 6, transcendentals=0
        ),
        name="delta",
    )(do, mix)


def middle_body(step, n_ref, dy_ref, wg_ref, wu_ref, wd_ref, h_ref, dg_ref, du_ref):
    for at in range(0, n_ref.shape[0], step):
        rows = pl.ds(at, step)
        n = n_ref[rows, :]
        g = mm(n, wg_ref[...])
        u = mm(n, wu_ref[...])
        dh = mm(dy_ref[rows, :], wd_ref[...], NT)
        s = 1.0 / (1.0 + jnp.exp2(g * (-LOG2E)))
        act = g * s
        h_ref[rows, :] = (act * u).astype(BF16)
        du_ref[rows, :] = (dh * act).astype(BF16)
        dg_ref[rows, :] = (dh * u * s * (1.0 + g * (1.0 - s))).astype(BF16)


def middle(n, dy, wg, wu, wd):
    rows, width = n.shape
    hidden = wg.shape[1]
    tile = 256
    whole = pl.BlockSpec((rows, width), lambda j: (0, 0))
    cols = pl.BlockSpec((width, tile), lambda j: (0, j))
    outs = pl.BlockSpec((rows, tile), lambda j: (0, j))
    shape = jax.ShapeDtypeStruct((rows, hidden), BF16)
    return pl.pallas_call(
        functools.partial(middle_body, min(rows, 256)),
        out_shape=(shape, shape, shape),
        grid=(hidden // tile,),
        in_specs=[whole, whole, cols, cols, pl.BlockSpec((tile, width), lambda j: (j, 0))],
        out_specs=(outs, outs, outs),
        compiler_params=pltpu.CompilerParams(vmem_limit_bytes=40 << 20),
        cost_estimate=pl.CostEstimate(
            flops=6 * rows * width * hidden,
            bytes_accessed=6 * (rows * hidden + width * hidden),
            transcendentals=rows * hidden,
        ),
        name="middle",
    )(n, dy, wg, wu, wd)


def swap(x):
    n = lax.axis_size("tp")
    return lax.ppermute(x, "tp", [(i, i ^ 1) for i in range(n)])


def core_swap(x):
    n = lax.axis_size("fsdp")
    return lax.ppermute(x, "fsdp", [(i, i ^ 1) for i in range(n)])


def y_shift(x, s):
    n = lax.axis_size("fsdp")
    return lax.ppermute(x, "fsdp", [(i, (i + 2 * s) % n) for i in range(n)])


def gather_rows(x):
    n = lax.axis_size("fsdp")
    me = lax.axis_index("fsdp")
    y, c, ny = me // 2, me % 2, n // 2
    mine = jnp.zeros((ny,) + x.shape, x.dtype)
    mine = lax.dynamic_update_index_in_dim(mine, x, y, 0)
    for s in range(1, ny):
        mine = lax.dynamic_update_index_in_dim(mine, y_shift(x, s), (y - s) % ny, 0)
    other = core_swap(mine)
    lower = jnp.where(c == 0, mine, other)
    upper = jnp.where(c == 0, other, mine)
    return jnp.stack([lower, upper], axis=1).reshape((n * x.shape[0],) + x.shape[1:])


def scatter_rows(g):
    n = lax.axis_size("fsdp")
    me = lax.axis_index("fsdp")
    y, c, ny = me // 2, me % 2, n // 2
    parts = g.reshape((ny, 2, g.shape[0] // n) + g.shape[1:])
    keep = lax.dynamic_index_in_dim(parts, c, 1, keepdims=False)
    give = lax.dynamic_index_in_dim(parts, 1 - c, 1, keepdims=False)
    both = (keep.astype(F32) + core_swap(give).astype(F32)).astype(BF16)
    total = lax.dynamic_index_in_dim(both, y, 0, keepdims=False).astype(F32)
    for s in range(1, ny):
        send = lax.dynamic_index_in_dim(both, (y + s) % ny, 0, keepdims=False)
        total = total + y_shift(send, s).astype(F32)
    return total


def nearest(m, i, n):
    left, right = i, n - 1 - i
    near = min(left, right)
    if m == 0:
        return 0
    if m <= 2 * near:
        return (m + 1) // 2 if m % 2 else -(m // 2)
    return m - near if right > left else -(m - near)


def pick(index, choices):
    keys = list(choices)
    value = keys[0][1]
    for name, array in keys[1:]:
        here = functools.reduce(jnp.logical_or, [index == i for i in choices[(name, array)]])
        value = jnp.where(here, array, value)
    return value


def choose(index, table):
    value = table[0][0]
    for array, positions in table[1:]:
        here = functools.reduce(jnp.logical_or, [index == i for i in positions])
        value = jnp.where(here, array, value)
    return value


def line_shards(x, n):
    out = {0: x}
    for t in range(1, n):
        out[-t] = lax.ppermute(out[-(t - 1)], "ctx", [(i, i + 1) for i in range(t - 1, n - 1)])
        out[t] = lax.ppermute(out[t - 1], "ctx", [(i, i - 1) for i in range(1, n - t + 1)])
    return out


def tables(x, index, n):
    lane = jnp.arange(128)
    exponent = -((lane % (HD // 2)).astype(F32) * 2.0) / HD
    angle = x.astype(F32)[:, None] * (ROPE_BASE**exponent)[None, :]
    sign = jnp.where(lane % HD < HD // 2, -1.0, 1.0).astype(F32)
    return jnp.cos(angle), jnp.sin(angle) * sign[None, :]


def norm_rows(x, gain):
    r = lax.rsqrt(jnp.mean(x * x, axis=-1, keepdims=True) + EPSILON)
    return x * r * gain, r


def norm_back(x, r, gain, d):
    scaled = d * gain
    dx = r * scaled - x * (r * r * r) * jnp.mean(x * scaled, axis=-1, keepdims=True)
    return dx, d * x * r


def per_device(
    tokens, cotangent, block_order, positions,
    attn_gain, w_query, key_weight, value_weight, query_gain, key_gain,
    w_out, ffn_gain, w_gate, w_up, w_down,
):
    n_ctx = lax.axis_size("ctx")
    n_fsdp = lax.axis_size("fsdp")
    me = lax.axis_index("ctx")
    seqs, rows, width = tokens.shape
    x = tokens.reshape(seqs * rows, width)
    dy = cotangent.reshape(seqs * rows, width)
    block = rows // 2
    qw, kw = w_query.shape[1], key_weight.shape[1]
    gs, hs = attn_gain.shape[0], query_gain.shape[0]

    w_qkv = gather_rows(jnp.concatenate([w_query, key_weight, value_weight], axis=1))
    small = jnp.concatenate([attn_gain, ffn_gain, query_gain, key_gain])
    small = lax.all_gather(small, "fsdp", axis=0, tiled=False).astype(F32)
    gain_attn = small[:, :gs].reshape(-1)
    gain_ffn = small[:, gs : 2 * gs].reshape(-1)
    gain_q = small[:, 2 * gs : 2 * gs + hs].reshape(-1)
    gain_k = small[:, 2 * gs + hs :].reshape(-1)
    gains = jnp.stack([jnp.tile(gain_q, 2), jnp.tile(gain_k, 2)] + [jnp.zeros(128, F32)] * 6)
    w_out2 = jnp.concatenate([w_out, swap(w_out)], axis=0)
    w_out2, w_gate, w_up, w_down, w_qkv = lax.optimization_barrier(
        (w_out2, w_gate, w_up, w_down, w_qkv)
    )
    out_full = lax.all_gather(w_out2, "fsdp", axis=1, tiled=True)
    down_full = lax.all_gather(w_down, "fsdp", axis=1, tiled=True)
    gate_full = lax.all_gather(w_gate, "fsdp", axis=0, tiled=True)
    up_full = lax.all_gather(w_up, "fsdp", axis=0, tiled=True)

    xf = x.astype(F32)
    normed, inv_one = norm_rows(xf, gain_attn)
    normed_b = normed.astype(BF16)
    cos, sin = tables(positions.reshape(-1), me, n_ctx)
    k_raw = mm(normed_b, w_qkv[:, qw : qw + kw])
    v_b = mm(normed_b, w_qkv[:, qw + kw :]).astype(BF16)
    q_raw = mm(normed_b, w_qkv[:, :qw])
    q_b, kv_b = rope(q_raw, k_raw, v_b, cos, sin, gains, min(256, block))

    shards = line_shards(kv_b, n_ctx)
    first_of = block_order[0::2]
    second_of = block_order[1::2]
    low_at = jnp.where(first_of < second_of, 0, block).astype(jnp.int32)
    low_id = jnp.minimum(first_of, second_of)
    q_low, q_id = low_at[me], low_id[me]
    kvs, metas = [], []
    for m in range(n_ctx):
        table = {}
        for i in range(n_ctx):
            table.setdefault(nearest(m, i, n_ctx), []).append(i)
        kvs.append(choose(me, [(shards[d], where) for d, where in table.items()]))
        far = jnp.array([i + nearest(m, i, n_ctx) for i in range(n_ctx)], jnp.int32)[me]
        if m == 0:
            metas.append(jnp.stack([q_low, block - q_low, q_low, q_low]))
        else:
            k_low = low_at[far]
            before = low_id[far] < q_id
            metas.append(
                jnp.stack(
                    [
                        jnp.where(before, q_low, block - q_low),
                        k_low,
                        block - q_low,
                        jnp.where(before, k_low, block - k_low),
                    ]
                )
            )
    acc = None
    for m in range(n_ctx):
        acc = attend(metas[m], q_b, kvs[m], acc, m == 0, m == n_ctx - 1, block)
    mixed_b, mix, lse = acc

    half_in = mixed_b.shape[1]
    attn_out = mm(mixed_b, out_full[:half_in]) + mm(swap(mixed_b), out_full[half_in:])
    resid = xf + attn_out
    normed_two, inv_two = norm_rows(resid, gain_ffn)
    two_b = normed_two.astype(BF16)

    hidden, dgate, dup = middle(two_b, dy, gate_full, up_full, down_full)
    d_two_part = (mm(dgate, gate_full, NT) + mm(dup, up_full, NT)).astype(BF16)
    d_two_other = swap(d_two_part)
    gate_g = mm(two_b, dgate, TN).astype(BF16)
    up_g = mm(two_b, dup, TN).astype(BF16)
    down_g = mm(dy, hidden, TN).astype(BF16)
    down_part = mm(hidden, down_full).astype(BF16)
    gate_g, up_g, down_g, down_part, d_two_other = lax.optimization_barrier(
        (gate_g, up_g, down_g, down_part, d_two_other)
    )
    output = (resid + (down_part.astype(F32) + swap(down_part).astype(F32))).astype(BF16)
    d_two = d_two_part.astype(F32) + d_two_other.astype(F32)
    d_norm, ffn_term = norm_back(resid, inv_two, gain_ffn, d_two)
    ffn_gain_g = jnp.sum(ffn_term, axis=0)
    d_resid = dy.astype(F32) + d_norm
    d_resid_b = d_resid.astype(BF16)

    do = mm(d_resid_b, out_full[:half_in], NT).astype(BF16)
    dlt = delta_rows(do, mix)
    grads = [None] * n_ctx
    dq = None
    for m in reversed(range(n_ctx)):
        dq, grads[m] = attend_back(metas[m], q_b, do, kvs[m], lse, dlt, dq, m == 0, block)
    home = [grads[0]]
    for side in (1, -1):
        got = None
        for t in range(n_ctx - 1):
            away = n_ctx - 1 - t
            table = {}
            for i in range(n_ctx):
                for m in range(1, n_ctx):
                    if nearest(m, i, n_ctx) == side * away:
                        table.setdefault(m, []).append(i)
            send = choose(me, [(grads[m], where) for m, where in table.items()])
            if got is not None:
                send = (send.astype(F32) + got.astype(F32)).astype(BF16)
            senders = sorted(i for where in table.values() for i in where)
            got = lax.ppermute(send, "ctx", [(i, i + side) for i in senders])
        if got is not None:
            home.append(got)
    out_g = mm(d_resid_b, mixed_b, TN).astype(BF16)

    d_qkv, head_gain = rope_back(dq, q_raw, k_raw, cos, sin, gains, home, min(256, block))
    normed_part = mm(d_qkv, w_qkv, NT).astype(BF16)
    normed_other = swap(normed_part)
    qkv_g = mm(normed_b, d_qkv, TN).astype(BF16)
    head_gain = head_gain[:2, :HD] + head_gain[:2, HD:]
    head_gain = lax.psum(head_gain, "tp")
    d_normed = normed_part.astype(F32) + normed_other.astype(F32)
    d_input, attn_term = norm_back(xf, inv_one, gain_attn, d_normed)
    input_grad = d_resid + d_input
    attn_gain_g = jnp.sum(attn_term, axis=0)

    def total(g):
        return lax.psum(scatter_rows(g).astype(BF16), "ctx").astype(F32)

    down_s, gate_s, up_s = total(down_g), total(gate_g), total(up_g)
    out_s, qkv_s = total(out_g), total(qkv_g)
    small_g = jnp.concatenate(
        [
            attn_gain_g.reshape(n_fsdp, gs),
            ffn_gain_g.reshape(n_fsdp, gs),
            head_gain[0].reshape(n_fsdp, hs),
            head_gain[1].reshape(n_fsdp, hs),
        ],
        axis=1,
    )
    small_g = lax.psum(small_g, ("fsdp", "ctx"))
    small_g = lax.dynamic_index_in_dim(small_g, lax.axis_index("fsdp"), 0, keepdims=False)
    return (
        output.reshape(tokens.shape),
        input_grad.reshape(tokens.shape),
        small_g[:gs],
        qkv_s[:, :qw],
        qkv_s[:, qw : qw + kw],
        qkv_s[:, qw + kw :],
        small_g[2 * gs : 2 * gs + hs],
        small_g[2 * gs + hs :],
        out_s.T,
        small_g[gs : 2 * gs],
        gate_s,
        up_s,
        down_s.T,
    )


def solution(mesh):
    rows = P("fsdp", "ctx", None)
    ins = P("fsdp", "tp")
    outs = P("tp", "fsdp")
    one = P("fsdp")
    return jax.shard_map(
        per_device,
        mesh=mesh,
        in_specs=(
            rows, rows, P(), P("fsdp", "ctx"), one, ins, ins, ins, one, one, outs, one, ins, ins, outs,
        ),
        out_specs=(rows, rows, one, ins, ins, ins, one, one, outs, one, ins, ins, outs),
        check_vma=False,
    )
```

```python
import functools

import jax
import jax.numpy as jnp
from jax import lax
from jax.experimental import pallas as pl
from jax.experimental.pallas import tpu as pltpu
from jax.sharding import PartitionSpec as P

HD = 64
EPSILON = 1e-05
ROPE_BASE = 1000000.0
LOG2E = 1.4426950408889634
SCALE2 = 0.125 * LOG2E
NT = (((1,), (1,)), ((), ()))
NN = (((1,), (0,)), ((), ()))
TN = (((0,), (0,)), ((), ()))
F32, BF16 = jnp.float32, jnp.bfloat16


def mm(a, b, dims=NN):
    return lax.dot_general(a, b, dims, preferred_element_type=F32)


def cost(flops, bytes_accessed):
    return pl.CostEstimate(
        flops=flops // 64, bytes_accessed=bytes_accessed // 64, transcendentals=0
    )


def half(shape, which):
    lane = lax.broadcasted_iota(jnp.int32, shape, len(shape) - 1)
    return (lane < HD) if which == 0 else (lane >= HD)


def pieces(m, n_ctx, block, where, order):
    me = where[0]

    def low(shard):
        first, second = order[2 * shard], order[2 * shard + 1]
        return jnp.minimum(first, second), jnp.where(first < second, 0, block)

    q_id, q_low = low(me)
    q_high = block - q_low
    if m == 0:
        q_low, q_high = pl.multiple_of(q_low, block), pl.multiple_of(q_high, block)
        return [(q_low, q_low, True), (q_high, q_low, False), (q_high, q_high, True)]
    left, right = me, n_ctx - 1 - me
    beyond = m - jnp.minimum(left, right)
    inner = (m + 1) // 2 if m % 2 else -(m // 2)
    outer = jnp.where(right > left, beyond, -beyond)
    far = me + jnp.where(m <= 2 * jnp.minimum(left, right), inner, outer)
    k_id, k_low = low(far)
    before = k_id < q_id
    q_first = pl.multiple_of(jnp.where(before, q_low, q_high), block)
    k_second = pl.multiple_of(jnp.where(before, k_low, block - k_low), block)
    return [
        (q_first, pl.multiple_of(k_low, block), False),
        (pl.multiple_of(q_high, block), k_second, False),
    ]


def attend_body(m, n_ctx, first, last, block, where, order, q_ref, kv_ref, *rest):
    rest = list(rest)
    given = None if first else rest.pop(0)
    if last:
        mixb_ref, mix_ref, lse_ref, acc = rest
    else:
        (acc,) = rest
    acc[...] = jnp.zeros_like(acc) if first else given[...]
    for q_at, k_at, diagonal in pieces(m, n_ctx, block, where, order):
        kt = kv_ref[pl.ds(k_at, block), 0:128]
        vt = kv_ref[pl.ds(k_at, block), 128:256]
        one = jnp.ones((block, HD), BF16)
        for hh in range(2):
            kh = kt[:, HD * hh : HD * hh + HD]
            vh = vt[:, HD * hh : HD * hh + HD]
            kd = jnp.concatenate([kh, kh], axis=1)
            vx = (jnp.concatenate([vh, one], axis=1), jnp.concatenate([one, vh], axis=1))
            qt = q_ref[pl.ds(q_at, block), 128 * hh : 128 * hh + 128]
            for r in range(2):
                qr = jnp.where(half((block, 128), r), qt, jnp.zeros_like(qt))
                p = jnp.exp2(mm(qr, kd, NT) * SCALE2)
                if diagonal:
                    row = lax.broadcasted_iota(jnp.int32, p.shape, 0)
                    col = lax.broadcasted_iota(jnp.int32, p.shape, 1)
                    p = jnp.where(col <= row, p, 0.0)
                c = 256 * hh + 128 * r
                acc[pl.ds(q_at, block), c : c + 128] += mm(p.astype(BF16), vx[r])
    if last:
        rows = acc.shape[0]
        lane = lax.broadcasted_iota(jnp.int32, (8, 128), 1)
        sub = lax.broadcasted_iota(jnp.int32, (8, 128), 0)
        total = jnp.zeros((8, rows), F32)
        for hh in range(2):
            out = []
            for r in range(2):
                a = acc[:, 256 * hh + 128 * r : 256 * hh + 128 * r + 128]
                out.append(a / pltpu.roll(a, HD, 1))
                pick = jnp.where((lane == (HD if r == 0 else 0)) & (sub == 2 * hh + r), 1.0, 0.0)
                total += lax.dot_general(
                    pick, a, NT, precision=lax.Precision.HIGHEST, preferred_element_type=F32
                )
            mix = jnp.where(half((rows, 128), 0), out[0], out[1])
            mix_ref[:, 128 * hh : 128 * hh + 128] = mix
            mixb_ref[:, 128 * hh : 128 * hh + 128] = mix.astype(BF16)
        lse_ref[0] = jnp.log2(jnp.where(sub[:, 0:1] < 4, total, 1.0))


def attend(m, n_ctx, place, q, kv, acc, last, block, at=None):
    rows = q.shape[0]
    total = kv.shape[1] // 256
    base, pairs = (0, total) if at is None else (at, 1)
    first = acc is None
    args = [*place, q, kv]
    wide = pl.BlockSpec((rows, 512), lambda g, *_: (0, g))
    slim = pl.BlockSpec((rows, 256), lambda g, *_: (0, g))
    pair = pl.BlockSpec((rows, 256), lambda g, *_: (0, g + base))
    in_specs = [pair, pair]
    if not first:
        in_specs.append(pl.BlockSpec((rows, 512), lambda g, *_: (0, g + base)))
        args.append(acc)
    if last:
        out_shape = (
            jax.ShapeDtypeStruct((rows, pairs * 256), BF16),
            jax.ShapeDtypeStruct((rows, pairs * 256), F32),
            jax.ShapeDtypeStruct((pairs, 8, rows), F32),
        )
        out_specs = (slim, slim, pl.BlockSpec((1, 8, rows), lambda g, *_: (g, 0, 0)))
        scratch = [pltpu.VMEM((rows, 512), F32)]
    else:
        out_shape = jax.ShapeDtypeStruct((rows, pairs * 512), F32)
        out_specs = wide
        scratch = []
    work = 2 * block * block * pairs * 4
    return pl.pallas_call(
        functools.partial(attend_body, m, n_ctx, first, last, block),
        out_shape=out_shape,
        grid_spec=pltpu.PrefetchScalarGridSpec(
            num_scalar_prefetch=2,
            grid=(pairs,),
            in_specs=in_specs,
            out_specs=out_specs,
            scratch_shapes=scratch,
        ),
        compiler_params=pltpu.CompilerParams(vmem_limit_bytes=40 << 20),
        cost_estimate=cost(work * 1024, 12 << 20),
        name="attend",
    )(*args)


def attend_back_body(m, n_ctx, first, block, where, order, q_ref, do_ref, kv_ref, lse_ref, dlt_ref, *rest):
    rest = list(rest)
    given = None if first else rest.pop(0)
    dq, dkv_ref, dka, dva = rest
    dq[...] = jnp.zeros_like(dq) if first else given[...]
    dka[...] = jnp.zeros_like(dka)
    dva[...] = jnp.zeros_like(dva)
    for q_at, k_at, diagonal in pieces(m, n_ctx, block, where, order):
        kt = kv_ref[pl.ds(k_at, block), 0:128]
        vt = kv_ref[pl.ds(k_at, block), 128:256]
        zero = jnp.zeros((block, HD), BF16)
        for hh in range(2):
            kh = kt[:, HD * hh : HD * hh + HD]
            vh = vt[:, HD * hh : HD * hh + HD]
            kx = (jnp.concatenate([kh, zero], axis=1), jnp.concatenate([zero, kh], axis=1))
            vx = (jnp.concatenate([vh, zero], axis=1), jnp.concatenate([zero, vh], axis=1))
            c = 128 * hh
            qt = q_ref[pl.ds(q_at, block), c : c + 128]
            dt = do_ref[pl.ds(q_at, block), c : c + 128]
            dvs, dks, dqs = [], [], None
            for r in range(2):
                row = 2 * hh + r
                lse = lse_ref[0, row : row + 1, pl.ds(q_at, block)]
                dlt = dlt_ref[0, row : row + 1, pl.ds(q_at, block)]
                p = jnp.exp2(mm(kx[r], qt, NT) * SCALE2 - lse)
                if diagonal:
                    key = lax.broadcasted_iota(jnp.int32, p.shape, 0)
                    query = lax.broadcasted_iota(jnp.int32, p.shape, 1)
                    p = jnp.where(key <= query, p, 0.0)
                ds = (p * (mm(vx[r], dt, NT) - dlt)).astype(BF16)
                dvs.append(mm(p.astype(BF16), dt))
                dks.append(mm(ds, qt))
                term = mm(ds, kx[r], TN)
                dqs = term if dqs is None else dqs + term
            left = half((block, 128), 0)
            dva[pl.ds(k_at, block), c : c + 128] += jnp.where(left, dvs[0], dvs[1])
            dka[pl.ds(k_at, block), c : c + 128] += jnp.where(left, dks[0], dks[1])
            dq[pl.ds(q_at, block), c : c + 128] += dqs
    for at, ref, scale in ((0, dka, 0.125), (128, dva, 1.0)):
        a = ref[...]
        a = jnp.concatenate([a[:, 0:64] + a[:, 64:128], a[:, 128:192] + a[:, 192:256]], axis=1)
        dkv_ref[:, at : at + 128] = (a * scale).astype(dkv_ref.dtype)


def attend_back(m, n_ctx, place, q, do, kv, lse, dlt, dq, block):
    rows = q.shape[0]
    pairs = kv.shape[1] // 256
    first = dq is None
    slim = pl.BlockSpec((rows, 256), lambda g, *_: (0, g))
    line = pl.BlockSpec((1, 8, rows), lambda g, *_: (g, 0, 0))
    in_specs = [slim, slim, slim, line, line]
    args = [*place, q, do, kv, lse, dlt]
    if not first:
        in_specs.append(slim)
        args.append(dq)
    work = 2 * block * block * pairs * 4
    return pl.pallas_call(
        functools.partial(attend_back_body, m, n_ctx, first, block),
        out_shape=(
            jax.ShapeDtypeStruct((rows, pairs * 256), F32),
            jax.ShapeDtypeStruct((rows, pairs * 256), F32 if m == 0 else BF16),
        ),
        grid_spec=pltpu.PrefetchScalarGridSpec(
            num_scalar_prefetch=2,
            grid=(pairs,),
            in_specs=in_specs,
            out_specs=(slim, slim),
            scratch_shapes=[pltpu.VMEM((rows, 256), F32), pltpu.VMEM((rows, 256), F32)],
        ),
        compiler_params=pltpu.CompilerParams(vmem_limit_bytes=40 << 20),
        cost_estimate=cost(work * 2048, 12 << 20),
        name="attend_back",
    )(*args)


def head_mean(u):
    a = lax.broadcasted_iota(jnp.int32, (128, 128), 0) // HD
    b = lax.broadcasted_iota(jnp.int32, (128, 128), 1) // HD
    ones = jnp.where(a == b, 1.0, 0.0).astype(BF16)
    high = u.astype(BF16)
    low = (u - high.astype(F32)).astype(BF16)
    return (mm(high, ones) + mm(low, ones)) * (1.0 / HD)


def turn(u):
    lane = lax.broadcasted_iota(jnp.int32, u.shape, 1)
    return jnp.where(lane % HD < HD // 2, pltpu.roll(u, 96, 1), pltpu.roll(u, 32, 1))


def rotated(u, gain, cos, sin):
    n = u * lax.rsqrt(head_mean(u * u) + EPSILON) * gain
    return (n * cos + turn(n) * sin).astype(BF16)


def row_scale(x):
    return lax.rsqrt(jnp.mean(x * x, axis=-1, keepdims=True) + EPSILON)


def blocks_product(n, w_ref):
    count = w_ref.shape[0]
    size = w_ref.shape[1] - 16
    return sum(mm(n[:, f * size : f * size + size], w_ref[f, 0:size, :]) for f in range(count))


def key_body(x_ref, g_ref, w_ref, cos_ref, sin_ref, gain_ref, n_ref, k_ref, kv_ref):
    x = x_ref[...].astype(F32)
    n = (x * row_scale(x) * g_ref[0:1]).astype(BF16)
    n_ref[...] = n
    both = blocks_product(n, w_ref)
    width = k_ref.shape[1]
    k_ref[...] = both[:, :width]
    for t in range(width // 128):
        c = 128 * t
        kv_ref[:, 2 * c : 2 * c + 128] = rotated(
            both[:, c : c + 128], gain_ref[1:2], cos_ref[...], sin_ref[...]
        )
        kv_ref[:, 2 * c + 128 : 2 * c + 256] = both[:, width + c : width + c + 128].astype(BF16)


def query_body(n_ref, w_ref, cos_ref, sin_ref, gain_ref, u_ref, q_ref):
    u = blocks_product(n_ref[...], w_ref)
    u_ref[...] = u
    for t in range(u.shape[1] // 128):
        c = slice(128 * t, 128 * t + 128)
        q_ref[:, c] = rotated(u[:, c], gain_ref[0:1], cos_ref[...], sin_ref[...])


def row_call(body, name, step, rows, ins, outs, flops, scratch=(), aliases=None, first=0, count=None):
    spec = lambda w: pl.BlockSpec((step, w), lambda i: (i + first, 0))
    in_specs = []
    for array, kind in ins:
        if kind == "rows":
            in_specs.append(spec(array.shape[1]))
        elif kind == "part":
            in_specs.append(pl.BlockSpec((step, array.shape[1]), lambda i: (i, 0)))
        elif kind == "whole":
            in_specs.append(pl.BlockSpec(array.shape, lambda i, n=array.ndim: (0,) * n))
        else:
            in_specs.append(kind)
    return pl.pallas_call(
        body,
        out_shape=tuple(o[0] for o in outs),
        grid=(rows // step if count is None else count,),
        in_specs=in_specs,
        out_specs=tuple(spec(o[0].shape[1]) if o[1] is None else o[1] for o in outs),
        scratch_shapes=list(scratch),
        input_output_aliases=aliases or {},
        compiler_params=pltpu.CompilerParams(vmem_limit_bytes=40 << 20),
        cost_estimate=cost(flops, 1 << 20),
        name=name,
    )(*(array for array, _ in ins))


def project_keys(x, gain, packed, cos, sin, gains, kw, step):
    rows, width = x.shape
    f, r, cols = packed.shape
    shape = lambda w, t: (jax.ShapeDtypeStruct((rows, w), t), None)
    part = pl.BlockSpec((f, r, 2 * kw), lambda i: (0, 0, cols // (2 * kw) - 1))
    return row_call(
        key_body, "project_keys", step, rows,
        [(x, "rows"), (gain, "whole"), (packed, part), (cos, "rows"), (sin, "rows"), (gains, "whole")],
        [shape(width, BF16), shape(kw, F32), shape(2 * kw, BF16)],
        rows * width * kw * 4,
    )


def project_queries(n, packed, cos, sin, gains, qw, step):
    rows, width = n.shape
    f, r, _ = packed.shape
    shape = lambda w, t: (jax.ShapeDtypeStruct((rows, w), t), None)
    part = pl.BlockSpec((f, r, qw), lambda i: (0, 0, 0))
    return row_call(
        query_body, "project_queries", step, rows,
        [(n, "rows"), (packed, part), (cos, "rows"), (sin, "rows"), (gains, "whole")],
        [shape(qw, F32), shape(qw, BF16)],
        rows * width * qw * 2,
    )


def pair_product(own, other, w_ref, at):
    size = own.shape[1]
    base = w_ref.shape[1] // 2
    return jnp.concatenate(
        [
            mm(own, w_ref[f, at * size : at * size + size, :])
            + mm(other, w_ref[f, base + at * size : base + at * size + size, :])
            for f in range(w_ref.shape[0])
        ],
        axis=1,
    )


def join_body(at, own_ref, other_ref, w_ref, *refs):
    term = pair_product(own_ref[...], other_ref[...], w_ref, at)
    refs[-1][...] = term if len(refs) == 1 else refs[0][...] + term


def join_last_body(at, own_ref, other_ref, w_ref, x_ref, g_ref, *refs):
    r_ref, n_ref = refs[-2:]
    term = pair_product(own_ref[...], other_ref[...], w_ref, at)
    if len(refs) == 3:
        term = refs[0][...] + term
    r = x_ref[...].astype(F32) + term
    r_ref[...] = r
    n_ref[...] = (r * row_scale(r) * g_ref[0:1]).astype(BF16)


def join(x, gain, w, own, others, step):
    rows, width = x.shape
    shape = lambda w, t: (jax.ShapeDtypeStruct((rows, w), t), None)
    flops = rows * width * width
    so_far = []
    for at, (mine, other) in enumerate(zip(own, others)):
        ins = [(mine, "rows"), (other, "rows"), (w, "whole")]
        held = [(v, "rows") for v in so_far]
        if at < len(own) - 1:
            so_far = row_call(
                functools.partial(join_body, at), "join", step, rows, ins + held, [shape(width, F32)], flops
            )
    return row_call(
        functools.partial(join_last_body, at), "join_last", step, rows,
        ins + [(x, "rows"), (gain, "whole")] + held,
        [shape(width, F32), shape(width, BF16)],
        flops,
    )


def into_body(pairs, aliased, a_ref, b_ref, r_ref, dy_ref, g_ref, w_ref, mix_ref, *refs):
    d_ref, db_ref, do_ref, dlt_ref, gg_ref = refs[aliased:]
    gain = g_ref[0:1]
    r = r_ref[...]
    scale = row_scale(r)
    d = a_ref[...].astype(F32) + b_ref[...].astype(F32)
    scaled = d * gain
    back = scale * scaled - r * (scale * scale * scale) * jnp.mean(r * scaled, axis=-1, keepdims=True)

    @pl.when(pl.program_id(0) == 0)
    def _():
        gg_ref[...] = jnp.zeros_like(gg_ref)

    gg_ref[0:1] += jnp.sum(d * r * scale, axis=0, keepdims=True)
    out = dy_ref[...].astype(F32) + back
    d_ref[...] = out
    out = out.astype(BF16)
    db_ref[...] = out
    size = w_ref.shape[2]
    do = sum(mm(out[:, f * size : f * size + size], w_ref[f], NT) for f in range(w_ref.shape[0]))
    do = do.astype(BF16)
    do_ref[...] = do
    lane = lax.broadcasted_iota(jnp.int32, (8, 128), 1) // HD
    sub = lax.broadcasted_iota(jnp.int32, (8, 128), 0)
    for p in range(pairs):
        total = jnp.zeros((8, r.shape[0]), F32)
        for hh in range(2):
            c = slice(256 * p + 128 * hh, 256 * p + 128 * hh + 128)
            x = do[:, c].astype(F32) * mix_ref[:, c]
            total += lax.dot_general(
                jnp.where(sub == 2 * hh + lane, 1.0, 0.0), x, NT,
                precision=lax.Precision.HIGHEST, preferred_element_type=F32,
            )
        dlt_ref[p] = total


def into_attention(a, b, resid, dy, gain, w, mix, given, first, step):
    rows, width = resid.shape
    wide = w.shape[1] // 2
    pairs = wide // 256
    own_w = pl.BlockSpec((w.shape[0], wide, w.shape[2]), lambda i: (0, 0, 0))
    shape = lambda w, t: (jax.ShapeDtypeStruct((rows, w), t), None)
    hbm = pl.BlockSpec(memory_space=pl.ANY)
    base = [(a, "part"), (b, "part"), (resid, "rows"), (dy, "rows"), (gain, "whole"), (w, own_w), (mix, "rows")]
    given = list(given or ())
    return row_call(
        functools.partial(into_body, pairs, len(given)), "into_attention", step, rows,
        base + [(g, hbm) for g in given],
        [
            shape(width, F32), shape(width, BF16), shape(wide, BF16),
            (jax.ShapeDtypeStruct((pairs, 8, rows), F32), pl.BlockSpec((pairs, 8, step), lambda i: (0, 0, i + first))),
            (jax.ShapeDtypeStruct((8, width), F32), pl.BlockSpec((8, width), lambda i: (0, 0))),
        ],
        rows * width * wide,
        aliases={len(base) + k: k for k in range(len(given))},
        first=first, count=a.shape[0] // step,
    )


def leave_body(a_ref, b_ref, x_ref, g_ref, d_ref, out_ref):
    x = x_ref[...].astype(F32)
    scale = row_scale(x)
    scaled = (a_ref[...].astype(F32) + b_ref[...].astype(F32)) * g_ref[0:1]
    back = scale * scaled - x * (scale * scale * scale) * jnp.mean(x * scaled, axis=-1, keepdims=True)
    out_ref[...] = d_ref[...] + back


def leave(a, b, x, gain, d, step):
    rows, width = x.shape
    return row_call(
        leave_body, "leave", step, rows,
        [(a, "rows"), (b, "rows"), (x, "rows"), (gain, "whole"), (d, "rows")],
        [(jax.ShapeDtypeStruct((rows, width), F32), None)],
        rows * width * 16,
    )[0]


def rope_back_body(terms, dq_ref, q_ref, k_ref, cos_ref, sin_ref, gain_ref, *rest):
    dkv_refs, (out_ref, gg_ref) = rest[:terms], rest[terms:]
    cos, sin = cos_ref[...], sin_ref[...]

    @pl.when(pl.program_id(0) == 0)
    def _():
        gg_ref[...] = jnp.zeros_like(gg_ref)

    def one(d, u, row):
        gain = gain_ref[row : row + 1]
        dn = d * cos + turn(d * sin)
        r = lax.rsqrt(head_mean(u * u) + EPSILON)
        gd = gain * dn
        gg_ref[row : row + 1] += jnp.sum(dn * u * r, axis=0, keepdims=True)
        return (r * gd - u * (r * r * r) * head_mean(u * gd)).astype(BF16)

    qw, kw = q_ref.shape[1], k_ref.shape[1]
    for t in range(qw // 128):
        c = slice(128 * t, 128 * t + 128)
        out_ref[:, c] = one(dq_ref[:, c] * 0.125, q_ref[:, c], 0)
    for t in range(kw // 128):
        dk = sum(ref[:, 256 * t : 256 * t + 128].astype(F32) for ref in dkv_refs)
        dv = sum(ref[:, 256 * t + 128 : 256 * t + 256].astype(F32) for ref in dkv_refs)
        out_ref[:, qw + 128 * t : qw + 128 * t + 128] = one(dk, k_ref[:, 128 * t : 128 * t + 128], 1)
        out_ref[:, qw + kw + 128 * t : qw + kw + 128 * t + 128] = dv.astype(BF16)


def rope_back(dq, q_raw, k_raw, cos, sin, gains, dkvs, step):
    rows, qw = q_raw.shape
    kw = k_raw.shape[1]
    spec = lambda w: pl.BlockSpec((step, w), lambda i: (i, 0))
    fixed = pl.BlockSpec((8, 128), lambda i: (0, 0))
    return pl.pallas_call(
        functools.partial(rope_back_body, len(dkvs)),
        out_shape=(
            jax.ShapeDtypeStruct((rows, qw + 2 * kw), BF16),
            jax.ShapeDtypeStruct((8, 128), F32),
        ),
        grid=(rows // step,),
        in_specs=[spec(qw), spec(qw), spec(kw), spec(128), spec(128), fixed]
        + [spec(2 * kw)] * len(dkvs),
        out_specs=(spec(qw + 2 * kw), fixed),
        cost_estimate=cost(rows * qw * 1600, rows * qw * 20),
        name="rope_back",
    )(dq, q_raw, k_raw, cos, sin, gains, *dkvs)


def middle_body(step, aliased, n_ref, dy_ref, wg_ref, wu_ref, wd_ref, *refs):
    h_ref, dg_ref, du_ref, dn_ref, acc = refs[aliased:]

    @pl.when(pl.program_id(0) == 0)
    def _():
        acc[...] = jnp.zeros_like(acc)

    for at in range(0, n_ref.shape[0], step):
        rows = pl.ds(at, step)
        n = n_ref[rows, :]
        g = mm(n, wg_ref[...])
        u = mm(n, wu_ref[...])
        dh = mm(dy_ref[rows, :], wd_ref[...], NT)
        s = 1.0 / (1.0 + jnp.exp2(g * (-LOG2E)))
        act = g * s
        h_ref[rows, :] = (act * u).astype(BF16)
        du_ref[rows, :] = (dh * act).astype(BF16)
        dg_ref[rows, :] = (dh * u * s * (1.0 + g * (1.0 - s))).astype(BF16)
    acc[...] += mm(dg_ref[...], wg_ref[...], NT) + mm(du_ref[...], wu_ref[...], NT)

    @pl.when(pl.program_id(0) == pl.num_programs(0) - 1)
    def _():
        dn_ref[...] = acc[...].astype(BF16)


def middle(n, dy, both, wd, given, at, parts):
    total, width = n.shape
    rows = total // parts
    hidden = both.shape[1] // 2
    tile = 256
    whole = pl.BlockSpec((rows, width), lambda j: (at, 0))
    cols = pl.BlockSpec((width, tile), lambda j: (0, j))
    more = pl.BlockSpec((width, tile), lambda j: (0, j + hidden // tile))
    outs = pl.BlockSpec((rows, tile), lambda j: (at, j))
    shape = jax.ShapeDtypeStruct((total, hidden), BF16)
    given = list(given or ())
    return pl.pallas_call(
        functools.partial(middle_body, min(rows, 256), len(given)),
        out_shape=(shape, shape, shape, jax.ShapeDtypeStruct((rows, width), BF16)),
        grid=(hidden // tile,),
        in_specs=[whole, whole, cols, more, pl.BlockSpec((tile, width), lambda j: (j, 0))]
        + [pl.BlockSpec(memory_space=pl.ANY)] * len(given),
        out_specs=(outs, outs, outs, pl.BlockSpec((rows, width), lambda j: (0, 0))),
        scratch_shapes=[pltpu.VMEM((rows, width), F32)],
        input_output_aliases={5 + k: k for k in range(len(given))},
        compiler_params=pltpu.CompilerParams(vmem_limit_bytes=40 << 20),
        cost_estimate=cost(10 * rows * width * hidden, 6 * (rows * hidden + width * hidden)),
        name="middle",
    )(n, dy, both, both, wd, *given)


def down_body(h_ref, w_ref, out_ref):
    out_ref[...] = mm(h_ref[...], w_ref[...]).astype(BF16)


def down(h, w):
    rows, hidden = h.shape
    width = w.shape[1]
    tile = min(rows, 256)
    return pl.pallas_call(
        down_body,
        out_shape=jax.ShapeDtypeStruct((rows, width), BF16),
        grid=(rows // tile,),
        in_specs=[
            pl.BlockSpec((tile, hidden), lambda j: (j, 0)),
            pl.BlockSpec((hidden, width), lambda j: (0, 0)),
        ],
        out_specs=pl.BlockSpec((tile, width), lambda j: (j, 0)),
        compiler_params=pltpu.CompilerParams(vmem_limit_bytes=40 << 20),
        cost_estimate=cost(2 * rows * width * hidden, 2 * (rows * hidden + width * hidden)),
        name="down",
    )(h, w)


def grad_body(at_ref, a_ref, z_ref, b_ref, keep_ref, give_ref):
    keep_ref[0] = mm(a_ref[...], b_ref[...], TN).astype(BF16)
    give_ref[0] = mm(z_ref[...], b_ref[...], TN).astype(BF16)


def weight_grad(a, b, parts, core):
    rows, width = a.shape
    cols = b.shape[1]
    block = width // parts
    tile = next(t for t in (2304, 1024, 512, 256, 128) if cols % t == 0)
    shape = jax.ShapeDtypeStruct((parts // 2, block, cols), BF16)
    out = pl.BlockSpec((1, block, tile), lambda j, i, c: (i, 0, j))
    return pl.pallas_call(
        grad_body,
        out_shape=(shape, shape),
        grid_spec=pltpu.PrefetchScalarGridSpec(
            num_scalar_prefetch=1,
            grid=(cols // tile, parts // 2),
            in_specs=[
                pl.BlockSpec((rows, block), lambda j, i, c: (0, 2 * i + c[0])),
                pl.BlockSpec((rows, block), lambda j, i, c: (0, 2 * i + 1 - c[0])),
                pl.BlockSpec((rows, tile), lambda j, i, c: (0, j)),
            ],
            out_specs=(out, out),
        ),
        compiler_params=pltpu.CompilerParams(vmem_limit_bytes=40 << 20),
        cost_estimate=cost(2 * rows * width * cols, 2 * (rows * width + rows * cols + width * cols)),
        name="weight_grad",
    )(core.reshape(1), a, a, b)


def swap(x):
    n = lax.axis_size("tp")
    return lax.ppermute(x, "tp", [(i, i ^ 1) for i in range(n)])


def core_swap(x):
    n = lax.axis_size("fsdp")
    return lax.ppermute(x, "fsdp", [(i, i ^ 1) for i in range(n)])


def y_shift(x, s):
    n = lax.axis_size("fsdp")
    return lax.ppermute(x, "fsdp", [(i, (i + 2 * s) % n) for i in range(n)])


def gather_y(x):
    n = lax.axis_size("fsdp")
    y, ny = lax.axis_index("fsdp") // 2, n // 2
    mine = jnp.zeros((ny,) + x.shape, x.dtype)
    mine = lax.dynamic_update_index_in_dim(mine, x, y, 0)
    for s in range(1, ny):
        mine = lax.dynamic_update_index_in_dim(mine, y_shift(x, s), (y - s) % ny, 0)
    return mine


def gather_core(mine):
    c = lax.axis_index("fsdp") % 2
    other = core_swap(mine)
    lower = jnp.where(c == 0, mine, other)
    upper = jnp.where(c == 0, other, mine)
    return jnp.stack([lower, upper], axis=1)


def core_sums(keep, give):
    ny = keep.shape[0]
    y = lax.axis_index("fsdp") // 2
    got = core_swap(give)
    sends = [both_block(keep, got, (y + s) % ny).astype(BF16) for s in range(1, ny)]
    return keep, got, sends


def both_block(keep, got, n):
    a = lax.dynamic_index_in_dim(keep, n, 0, keepdims=False).astype(F32)
    return a + lax.dynamic_index_in_dim(got, n, 0, keepdims=False).astype(F32)


def y_sums(keep, got, sends, *after):
    parts = [y_shift(send, s + 1) for s, send in enumerate(sends)]
    keep, got, *rest = lax.optimization_barrier((keep, got, *parts, *after))
    total = both_block(keep, got, lax.axis_index("fsdp") // 2)
    for part in rest[: len(parts)]:
        total = total + part.astype(F32)
    return total.astype(BF16)


def nearest(m, i, n):
    left, right = i, n - 1 - i
    near = min(left, right)
    if m == 0:
        return 0
    if m <= 2 * near:
        return (m + 1) // 2 if m % 2 else -(m // 2)
    return m - near if right > left else -(m - near)


def choose(index, table):
    value = table[0][0]
    for array, positions in table[1:]:
        here = functools.reduce(jnp.logical_or, [index == i for i in positions])
        value = jnp.where(here, array, value)
    return value


def tie(x, *others):
    return lax.optimization_barrier((x,) + others)[0]


def tables(x):
    lane = jnp.arange(128)
    exponent = -((lane % (HD // 2)).astype(F32) * 2.0) / HD
    angle = x.astype(F32)[:, None] * (ROPE_BASE**exponent)[None, :]
    sign = jnp.where(lane % HD < HD // 2, -1.0, 1.0).astype(F32)
    return jnp.cos(angle), jnp.sin(angle) * sign[None, :]


def per_device(
    tokens, cotangent, block_order, positions,
    attn_gain, w_query, key_weight, value_weight, query_gain, key_gain,
    w_out, ffn_gain, w_gate, w_up, w_down,
):
    n_ctx = lax.axis_size("ctx")
    n_fsdp = lax.axis_size("fsdp")
    me = lax.axis_index("ctx")
    seqs, rows, width = tokens.shape
    x = tokens.reshape(seqs * rows, width)
    dy = cotangent.reshape(seqs * rows, width)
    block = rows // 2
    qw, kw = w_query.shape[1], key_weight.shape[1]
    gs, hs = attn_gain.shape[0], query_gain.shape[0]

    qkv_w = qw + 2 * kw
    small = jnp.concatenate([attn_gain, ffn_gain, query_gain, key_gain])
    small = jnp.pad(small.reshape(1, -1), ((0, 15), (0, qkv_w - 2 * (gs + hs))))
    packed = jnp.concatenate(
        [jnp.concatenate([w_query, key_weight, value_weight], axis=1), small], axis=0
    )
    mine = gather_y(packed)
    out_i = tie(w_out, packed)
    out_i = jnp.concatenate([out_i, swap(out_i)], axis=0)
    cos, sin = tables(positions.reshape(-1))
    both_i = jnp.concatenate(lax.optimization_barrier((w_gate, w_up, packed))[:2], axis=1)
    mine, out_i, cos, sin, both_i = lax.optimization_barrier((mine, out_i, cos, sin, both_i))
    both_full = lax.all_gather(both_i, "fsdp", axis=0, tiled=True)
    packed = gather_core(mine).reshape(n_fsdp, gs + 16, qkv_w)
    small = packed[:, gs].astype(F32)
    row = lambda v: jnp.broadcast_to(v.reshape(1, -1), (8, v.size))
    gain_attn = row(small[:, :gs])
    gain_ffn = row(small[:, gs : 2 * gs])
    gain_q = small[:, 2 * gs : 2 * gs + hs].reshape(-1)
    gain_k = small[:, 2 * gs + hs : 2 * (gs + hs)].reshape(-1)
    gains = jnp.stack([jnp.tile(gain_q, 2), jnp.tile(gain_k, 2)] + [jnp.zeros(128, F32)] * 6)

    step = min(256, block)
    normed_b, k_raw, kv_b = project_keys(x, gain_attn, packed, cos, sin, gains, kw, step)
    q_raw, q_b = project_queries(tie(normed_b, kv_b), packed, cos, sin, gains, qw, step)
    place = (me.astype(jnp.int32).reshape(1), block_order)
    shards = {0: kv_b}

    def shard(m):
        table = {}
        for i in range(n_ctx):
            table.setdefault(nearest(m, i, n_ctx), []).append(i)
        return choose(me, [(shards[d], where) for d, where in table.items()])

    kvs = []
    acc = None
    for t in range(1, n_ctx):
        right = [(i, i + 1) for i in range(t - 1, n_ctx - 1)]
        left = [(i, i - 1) for i in range(1, n_ctx - t + 1)]
        shards[-t] = lax.ppermute(shards[-(t - 1)], "ctx", right)
        shards[t] = lax.ppermute(shards[t - 1], "ctx", left)
        if t == 1:
            shards[-t], shards[t], q_b = lax.optimization_barrier((shards[-t], shards[t], q_b))
            out_w = lax.all_gather(tie(out_i, kv_b), "fsdp", axis=0, tiled=False)
            down_full = lax.all_gather(tie(w_down, q_b), "fsdp", axis=1, tiled=True)
            continue
        while len(kvs) < t:
            kvs.append(shard(len(kvs)))
            acc = attend(len(kvs) - 1, n_ctx, place, q_b, kvs[-1], acc, False, block)
        shards[-t], shards[t], acc = lax.optimization_barrier((shards[-t], shards[t], acc))
        if t == 2:
            acc = tie(acc, both_full)
    while len(kvs) < n_ctx - 1:
        kvs.append(shard(len(kvs)))
        acc = attend(len(kvs) - 1, n_ctx, place, q_b, kvs[-1], acc, False, block)
    m = n_ctx - 1
    kvs.append(shard(m))
    pairs = kw // 128
    mixes, others = [], []
    last_q = q_b
    for p in range(pairs):
        mixes.append(attend(m, n_ctx, place, last_q, kvs[m], acc, True, block, p))
        last_q = tie(q_b, mixes[-1][0])
        others.append(swap(mixes[-1][0]))
    mixed_b = jnp.concatenate([piece[0] for piece in mixes], axis=1)
    mix = jnp.concatenate([piece[1] for piece in mixes], axis=1)
    lse = jnp.concatenate([piece[2] for piece in mixes], axis=0)

    own = [piece[0] for piece in mixes]
    resid, two_b = join(x, gain_ffn, out_w, own, others, step)

    core = lax.axis_index("fsdp") % 2

    parts = 2
    given, d_parts, d_others = None, [], []
    two_t = two_b
    for at in range(parts):
        *given, d_part = middle(two_t, dy, both_full, down_full, given, at, parts)
        two_t = tie(two_b, d_part)
        d_parts.append(d_part)
        d_others.append(swap(d_part))
    hidden, dgate, dup = given
    down_w = weight_grad(dy, hidden, n_fsdp, core)
    two_t, hidden_t = lax.optimization_barrier((two_b, hidden, down_w, d_others[0]))[:2]
    gate_w = weight_grad(two_t, dgate, n_fsdp, core)
    up_w = weight_grad(two_t, dup, n_fsdp, core)
    down_part = down(hidden_t, down_full)
    d_others[-1], down_w, gate_w, up_w, down_part = lax.optimization_barrier(
        (d_others[-1], down_w, gate_w, up_w, down_part)
    )
    down_c, gate_c, up_c = core_sums(*down_w), core_sums(*gate_w), core_sums(*up_w)

    given, ffn_gain_g = None, 0.0
    per = rows * seqs // parts // step
    for at in range(parts):
        *given, g = into_attention(
            d_parts[at], d_others[at], resid, dy, gain_ffn, out_w, mix, given, at * per, step
        )
        ffn_gain_g = ffn_gain_g + g[0]
    d_resid, d_resid_b, do, dlt = given
    do = tie(do, *down_c[2], *gate_c[2])

    grads = [None] * n_ctx
    got = {}
    dq = None
    for m in reversed(range(n_ctx)):
        dq, grads[m] = attend_back(m, n_ctx, place, q_b, do, kvs[m], lse, dlt, dq, block)
        if m == 0:
            break
        sends = []
        for side in (1, -1):
            table = {}
            for i in range(n_ctx):
                for k in range(1, n_ctx):
                    if nearest(k, i, n_ctx) == side * m:
                        table.setdefault(k, []).append(i)
            send = choose(me, [(grads[k], where) for k, where in table.items()])
            if side in got:
                send = (send.astype(F32) + got[side].astype(F32)).astype(BF16)
            sends.append(send)
            senders = sorted(i for where in table.values() for i in where)
            got[side] = lax.ppermute(send, "ctx", [(i, i + side) for i in senders])
        if m == n_ctx - 1:
            down_other = swap(tie(down_part, dq))
            down_s = y_sums(*down_c)
            sends += [down_s] + up_c[2]
            down_s = lax.psum(down_s, "ctx")
        if m == max(n_ctx - 2, 1):
            gate_s = y_sums(*gate_c, dq)
            sends.append(gate_s)
            out_g = weight_grad(tie(d_resid_b, dq), mixed_b, n_fsdp, core)
        if m == 1:
            up_s = y_sums(*up_c, dq)
            sends += [up_s, *out_g]
            gate_s, up_s, down_s = lax.optimization_barrier((gate_s, up_s, down_s))
            gate_s, up_s = lax.psum((gate_s, up_s), "ctx")
        dq = tie(dq, *sends)
    dq, down_other = lax.optimization_barrier((dq, down_other))
    out_s = y_sums(*core_sums(*out_g))
    home = [grads[0]] + list(got.values())
    output = (tie(resid, dq) + (down_part.astype(F32) + down_other.astype(F32))).astype(BF16)

    d_qkv, head_gain = rope_back(dq, q_raw, k_raw, cos, sin, gains, home, step)
    qkv_c = core_sums(*weight_grad(normed_b, d_qkv, n_fsdp, core))
    w_qkv = packed[:, :gs].reshape(n_fsdp * gs, qkv_w)
    normed_part = mm(d_qkv, w_qkv, NT)

    head_gain = head_gain[:2, :HD] + head_gain[:2, HD:]
    xf = x.astype(F32)
    inv_one = lax.rsqrt(jnp.mean(xf * xf, axis=-1, keepdims=True) + EPSILON)
    attn_gain_g = jnp.sum(normed_part * (xf * inv_one), axis=0)
    small_g = jnp.concatenate(
        [
            attn_gain_g.reshape(n_fsdp, gs),
            0.5 * ffn_gain_g.reshape(n_fsdp, gs),
            head_gain[0].reshape(n_fsdp, hs),
            head_gain[1].reshape(n_fsdp, hs),
        ],
        axis=1,
    )
    small_g = (small_g + swap(small_g)).astype(BF16).reshape(n_fsdp // 2, 2, 1, -1)
    normed_part = tie(normed_part.astype(BF16), small_g)
    normed_other = swap(normed_part)
    small_s = y_sums(
        *core_sums(
            lax.dynamic_index_in_dim(small_g, core, 1, keepdims=False),
            lax.dynamic_index_in_dim(small_g, 1 - core, 1, keepdims=False),
        )
    )
    last = jnp.concatenate([y_sums(*qkv_c), out_s], axis=1)
    small_s = jnp.pad(small_s, ((0, 15), (0, last.shape[1] - small_s.shape[1])))
    last = jnp.concatenate([last, small_s], axis=0)
    last, gate_s, up_s = lax.optimization_barrier((last, gate_s, up_s))
    last = lax.psum(last, "ctx")
    input_grad = leave(normed_part, normed_other, x, gain_attn, d_resid, step)
    last = tie(last, input_grad)
    q_s, k_s, v_s = last[:gs, :qw], last[:gs, qw : qw + kw], last[:gs, qw + kw : qkv_w]
    out_s = last[:gs, qkv_w:]
    small_s = last[gs : gs + 1, : 2 * (gs + hs)]
    down_s, gate_s, up_s, out_s, q_s, k_s, v_s = (
        v.astype(F32) for v in (down_s, gate_s, up_s, out_s, q_s, k_s, v_s)
    )
    small_g = small_s[0].astype(F32)
    return (
        output.reshape(tokens.shape),
        input_grad.reshape(tokens.shape),
        small_g[:gs],
        q_s,
        k_s,
        v_s,
        small_g[2 * gs : 2 * gs + hs],
        small_g[2 * gs + hs :],
        out_s.T,
        small_g[gs : 2 * gs],
        gate_s,
        up_s,
        down_s.T,
    )


def solution(mesh):
    rows = P("fsdp", "ctx", None)
    ins = P("fsdp", "tp")
    outs = P("tp", "fsdp")
    one = P("fsdp")
    return jax.shard_map(
        per_device,
        mesh=mesh,
        in_specs=(
            rows, rows, P(), P("fsdp", "ctx"), one, ins, ins, ins, one, one, outs, one, ins, ins, outs,
        ),
        out_specs=(rows, rows, one, ins, ins, ins, one, one, outs, one, ins, ins, outs),
        check_vma=False,
    )
```

```python
import functools

import jax
import jax.numpy as jnp
from jax import lax
from jax.experimental import pallas as pl
from jax.experimental.pallas import tpu as pltpu
from jax.sharding import PartitionSpec as P

HD = 64
EPSILON = 1e-05
ROPE_BASE = 1000000.0
LOG2E = 1.4426950408889634
SCALE2 = 0.125 * LOG2E
NT = (((1,), (1,)), ((), ()))
NN = (((1,), (0,)), ((), ()))
TN = (((0,), (0,)), ((), ()))
F32, BF16 = jnp.float32, jnp.bfloat16


def mm(a, b, dims=NN):
    return lax.dot_general(a, b, dims, preferred_element_type=F32)


def cost(flops, bytes_accessed):
    return pl.CostEstimate(
        flops=flops // 64, bytes_accessed=bytes_accessed // 64, transcendentals=0
    )


def far(x):
    return pltpu.with_memory_space_constraint(x, pltpu.HBM)


def half(shape, which):
    lane = lax.broadcasted_iota(jnp.int32, shape, len(shape) - 1)
    return (lane < HD) if which == 0 else (lane >= HD)


def pieces(m, n_ctx, block, where, order):
    me = where[0]

    def low(shard):
        first, second = order[2 * shard], order[2 * shard + 1]
        return jnp.minimum(first, second), jnp.where(first < second, 0, block)

    q_id, q_low = low(me)
    q_high = block - q_low
    if m == 0:
        q_low, q_high = pl.multiple_of(q_low, block), pl.multiple_of(q_high, block)
        return [(q_low, q_low, True), (q_high, q_low, False), (q_high, q_high, True)]
    left, right = me, n_ctx - 1 - me
    beyond = m - jnp.minimum(left, right)
    inner = (m + 1) // 2 if m % 2 else -(m // 2)
    outer = jnp.where(right > left, beyond, -beyond)
    far = me + jnp.where(m <= 2 * jnp.minimum(left, right), inner, outer)
    k_id, k_low = low(far)
    before = k_id < q_id
    q_first = pl.multiple_of(jnp.where(before, q_low, q_high), block)
    k_second = pl.multiple_of(jnp.where(before, k_low, block - k_low), block)
    return [
        (q_first, pl.multiple_of(k_low, block), False),
        (pl.multiple_of(q_high, block), k_second, False),
    ]


def attend_body(m, n_ctx, first, last, block, where, order, q_ref, kv_ref, *rest):
    rest = list(rest)
    given = None if first else rest.pop(0)
    if last:
        mixb_ref, mix_ref, lse_ref, acc = rest
    else:
        (acc,) = rest
    acc[...] = jnp.zeros_like(acc) if first else given[...]
    for q_at, k_at, diagonal in pieces(m, n_ctx, block, where, order):
        kt = kv_ref[pl.ds(k_at, block), 0:128]
        vt = kv_ref[pl.ds(k_at, block), 128:256]
        one = jnp.ones((block, HD), BF16)
        for hh in range(2):
            kh = kt[:, HD * hh : HD * hh + HD]
            vh = vt[:, HD * hh : HD * hh + HD]
            kd = jnp.concatenate([kh, kh], axis=1)
            vx = (jnp.concatenate([vh, one], axis=1), jnp.concatenate([one, vh], axis=1))
            qt = q_ref[pl.ds(q_at, block), 128 * hh : 128 * hh + 128]
            for r in range(2):
                qr = jnp.where(half((block, 128), r), qt, jnp.zeros_like(qt))
                p = jnp.exp2(mm(qr, kd, NT) * SCALE2)
                if diagonal:
                    row = lax.broadcasted_iota(jnp.int32, p.shape, 0)
                    col = lax.broadcasted_iota(jnp.int32, p.shape, 1)
                    p = jnp.where(col <= row, p, 0.0)
                c = 256 * hh + 128 * r
                acc[pl.ds(q_at, block), c : c + 128] += mm(p.astype(BF16), vx[r])
    if last:
        rows = acc.shape[0]
        lane = lax.broadcasted_iota(jnp.int32, (8, 128), 1)
        sub = lax.broadcasted_iota(jnp.int32, (8, 128), 0)
        total = jnp.zeros((8, rows), F32)
        for hh in range(2):
            out = []
            for r in range(2):
                a = acc[:, 256 * hh + 128 * r : 256 * hh + 128 * r + 128]
                out.append(a / pltpu.roll(a, HD, 1))
                pick = jnp.where((lane == (HD if r == 0 else 0)) & (sub == 2 * hh + r), 1.0, 0.0)
                total += lax.dot_general(
                    pick, a, NT, precision=lax.Precision.HIGHEST, preferred_element_type=F32
                )
            mix = jnp.where(half((rows, 128), 0), out[0], out[1])
            mix_ref[:, 128 * hh : 128 * hh + 128] = mix
            mixb_ref[:, 128 * hh : 128 * hh + 128] = mix.astype(BF16)
        lse_ref[0] = jnp.log2(jnp.where(sub[:, 0:1] < 4, total, 1.0))


def attend(m, n_ctx, place, q, kv, acc, last, block, at=None):
    rows = q.shape[0]
    total = kv.shape[1] // 256
    base, pairs = (0, total) if at is None else (at, 1)
    first = acc is None
    args = [*place, q, kv]
    wide = pl.BlockSpec((rows, 512), lambda g, *_: (0, g))
    slim = pl.BlockSpec((rows, 256), lambda g, *_: (0, g))
    pair = pl.BlockSpec((rows, 256), lambda g, *_: (0, g + base))
    in_specs = [pair, pair]
    if not first:
        in_specs.append(pl.BlockSpec((rows, 512), lambda g, *_: (0, g + base)))
        args.append(far(acc) if m == n_ctx - 2 else acc)
    if last:
        out_shape = (
            jax.ShapeDtypeStruct((rows, pairs * 256), BF16),
            pltpu.HBM((rows, pairs * 256), F32),
            jax.ShapeDtypeStruct((pairs, 8, rows), F32),
        )
        out_specs = (slim, slim, pl.BlockSpec((1, 8, rows), lambda g, *_: (g, 0, 0)))
        scratch = [pltpu.VMEM((rows, 512), F32)]
    else:
        out_shape = (pltpu.HBM if m > 0 else jax.ShapeDtypeStruct)((rows, pairs * 512), F32)
        out_specs = wide
        scratch = []
    work = 2 * block * block * pairs * 4
    return pl.pallas_call(
        functools.partial(attend_body, m, n_ctx, first, last, block),
        out_shape=out_shape,
        grid_spec=pltpu.PrefetchScalarGridSpec(
            num_scalar_prefetch=2,
            grid=(pairs,),
            in_specs=in_specs,
            out_specs=out_specs,
            scratch_shapes=scratch,
        ),
        compiler_params=pltpu.CompilerParams(vmem_limit_bytes=24 << 20),
        cost_estimate=cost(work * 1024, 12 << 20),
        name="attend",
    )(*args)


def attend_back_body(m, n_ctx, first, block, where, order, q_ref, do_ref, kv_ref, lse_ref, dlt_ref, *rest):
    rest = list(rest)
    given = None if first else rest.pop(0)
    dq, dkv_ref, dka, dva = rest
    dq[...] = jnp.zeros_like(dq) if first else given[...]
    dka[...] = jnp.zeros_like(dka)
    dva[...] = jnp.zeros_like(dva)
    for q_at, k_at, diagonal in pieces(m, n_ctx, block, where, order):
        kt = kv_ref[pl.ds(k_at, block), 0:128]
        vt = kv_ref[pl.ds(k_at, block), 128:256]
        zero = jnp.zeros((block, HD), BF16)
        for hh in range(2):
            kh = kt[:, HD * hh : HD * hh + HD]
            vh = vt[:, HD * hh : HD * hh + HD]
            kx = (jnp.concatenate([kh, zero], axis=1), jnp.concatenate([zero, kh], axis=1))
            vx = (jnp.concatenate([vh, zero], axis=1), jnp.concatenate([zero, vh], axis=1))
            c = 128 * hh
            qt = q_ref[pl.ds(q_at, block), c : c + 128]
            dt = do_ref[pl.ds(q_at, block), c : c + 128]
            dvs, dks, dqs = [], [], None
            for r in range(2):
                row = 2 * hh + r
                lse = lse_ref[0, row : row + 1, pl.ds(q_at, block)]
                dlt = dlt_ref[0, row : row + 1, pl.ds(q_at, block)]
                p = jnp.exp2(mm(kx[r], qt, NT) * SCALE2 - lse)
                if diagonal:
                    key = lax.broadcasted_iota(jnp.int32, p.shape, 0)
                    query = lax.broadcasted_iota(jnp.int32, p.shape, 1)
                    p = jnp.where(key <= query, p, 0.0)
                ds = (p * (mm(vx[r], dt, NT) - dlt)).astype(BF16)
                dvs.append(mm(p.astype(BF16), dt))
                dks.append(mm(ds, qt))
                term = mm(ds, kx[r], TN)
                dqs = term if dqs is None else dqs + term
            left = half((block, 128), 0)
            dva[pl.ds(k_at, block), c : c + 128] += jnp.where(left, dvs[0], dvs[1])
            dka[pl.ds(k_at, block), c : c + 128] += jnp.where(left, dks[0], dks[1])
            dq[pl.ds(q_at, block), c : c + 128] += dqs
    for at, ref, scale in ((0, dka, 0.125), (128, dva, 1.0)):
        a = ref[...]
        a = jnp.concatenate([a[:, 0:64] + a[:, 64:128], a[:, 128:192] + a[:, 192:256]], axis=1)
        dkv_ref[:, at : at + 128] = (a * scale).astype(dkv_ref.dtype)


def attend_back(m, n_ctx, place, q, do, kv, lse, dlt, dq, block):
    rows = q.shape[0]
    pairs = kv.shape[1] // 256
    first = dq is None
    slim = pl.BlockSpec((rows, 256), lambda g, *_: (0, g))
    line = pl.BlockSpec((1, 8, rows), lambda g, *_: (g, 0, 0))
    in_specs = [slim, slim, slim, line, line]
    args = [*place, q, do, kv, lse, dlt]
    if not first:
        in_specs.append(slim)
        args.append(far(dq))
    work = 2 * block * block * pairs * 4
    return pl.pallas_call(
        functools.partial(attend_back_body, m, n_ctx, first, block),
        out_shape=(
            pltpu.HBM((rows, pairs * 256), F32),
            pltpu.HBM((rows, pairs * 256), F32) if m == 0 else jax.ShapeDtypeStruct((rows, pairs * 256), BF16),
        ),
        grid_spec=pltpu.PrefetchScalarGridSpec(
            num_scalar_prefetch=2,
            grid=(pairs,),
            in_specs=in_specs,
            out_specs=(slim, slim),
            scratch_shapes=[pltpu.VMEM((rows, 256), F32), pltpu.VMEM((rows, 256), F32)],
        ),
        compiler_params=pltpu.CompilerParams(vmem_limit_bytes=24 << 20),
        cost_estimate=cost(work * 2048, 12 << 20),
        name="attend_back",
    )(*args)


def head_mean(u):
    a = lax.broadcasted_iota(jnp.int32, (128, 128), 0) // HD
    b = lax.broadcasted_iota(jnp.int32, (128, 128), 1) // HD
    ones = jnp.where(a == b, 1.0, 0.0).astype(BF16)
    high = u.astype(BF16)
    low = (u - high.astype(F32)).astype(BF16)
    return (mm(high, ones) + mm(low, ones)) * (1.0 / HD)


def turn(u):
    lane = lax.broadcasted_iota(jnp.int32, u.shape, 1)
    return jnp.where(lane % HD < HD // 2, pltpu.roll(u, 96, 1), pltpu.roll(u, 32, 1))


def rotated(u, gain, cos, sin):
    n = u * lax.rsqrt(head_mean(u * u) + EPSILON) * gain
    return (n * cos + turn(n) * sin).astype(BF16)


def row_scale(x):
    return lax.rsqrt(jnp.mean(x * x, axis=-1, keepdims=True) + EPSILON)


def blocks_product(n, w_ref):
    count = w_ref.shape[0]
    size = w_ref.shape[1] - 16
    return sum(mm(n[:, f * size : f * size + size], w_ref[f, 0:size, :]) for f in range(count))


def key_body(x_ref, g_ref, w_ref, cos_ref, sin_ref, gain_ref, n_ref, k_ref, kv_ref):
    x = x_ref[...].astype(F32)
    n = (x * row_scale(x) * g_ref[0:1]).astype(BF16)
    n_ref[...] = n
    both = blocks_product(n, w_ref)
    width = k_ref.shape[1]
    k_ref[...] = both[:, :width]
    for t in range(width // 128):
        c = 128 * t
        kv_ref[:, 2 * c : 2 * c + 128] = rotated(
            both[:, c : c + 128], gain_ref[1:2], cos_ref[...], sin_ref[...]
        )
        kv_ref[:, 2 * c + 128 : 2 * c + 256] = both[:, width + c : width + c + 128].astype(BF16)


def query_body(n_ref, w_ref, cos_ref, sin_ref, gain_ref, u_ref, q_ref):
    u = blocks_product(n_ref[...], w_ref)
    u_ref[...] = u
    for t in range(u.shape[1] // 128):
        c = slice(128 * t, 128 * t + 128)
        q_ref[:, c] = rotated(u[:, c], gain_ref[0:1], cos_ref[...], sin_ref[...])


def row_call(body, name, step, rows, ins, outs, flops, scratch=(), aliases=None, first=0, count=None):
    ins = list(ins)
    spec = lambda w: pl.BlockSpec((step, w), lambda i: (i + first, 0))
    in_specs = []
    for n, (array, kind) in enumerate(ins):
        if isinstance(kind, str) and kind.startswith("far "):
            kind = kind[4:]
            ins[n] = (far(array), kind)
        if kind == "rows":
            in_specs.append(spec(array.shape[1]))
        elif kind == "part":
            in_specs.append(pl.BlockSpec((step, array.shape[1]), lambda i: (i, 0)))
        elif kind == "whole":
            in_specs.append(pl.BlockSpec(array.shape, lambda i, n=array.ndim: (0,) * n))
        else:
            in_specs.append(kind)
    return pl.pallas_call(
        body,
        out_shape=tuple(pltpu.HBM(o[0].shape, o[0].dtype) if len(o) > 2 else o[0] for o in outs),
        grid=(rows // step if count is None else count,),
        in_specs=in_specs,
        out_specs=tuple(spec(o[0].shape[1]) if o[1] is None else o[1] for o in outs),
        scratch_shapes=list(scratch),
        input_output_aliases=aliases or {},
        compiler_params=pltpu.CompilerParams(vmem_limit_bytes=24 << 20),
        cost_estimate=cost(flops, 1 << 20),
        name=name,
    )(*(array for array, _ in ins))


def project_keys(x, gain, packed, cos, sin, gains, kw, step):
    rows, width = x.shape
    f, r, cols = packed.shape
    shape = lambda w, t: (jax.ShapeDtypeStruct((rows, w), t), None)
    part = pl.BlockSpec((f, r, 2 * kw), lambda i: (0, 0, cols // (2 * kw) - 1))
    return row_call(
        key_body, "project_keys", step, rows,
        [(x, "far rows"), (gain, "whole"), (packed, part), (cos, "far rows"), (sin, "far rows"), (gains, "whole")],
        [shape(width, BF16) + ("far",), shape(kw, F32) + ("far",), shape(2 * kw, BF16) + ("far",)],
        rows * width * kw * 4,
    )


def project_queries(n, packed, cos, sin, gains, qw, step):
    rows, width = n.shape
    f, r, _ = packed.shape
    shape = lambda w, t: (jax.ShapeDtypeStruct((rows, w), t), None)
    part = pl.BlockSpec((f, r, qw), lambda i: (0, 0, 0))
    return row_call(
        query_body, "project_queries", step, rows,
        [(n, "far rows"), (packed, part), (cos, "far rows"), (sin, "far rows"), (gains, "whole")],
        [shape(qw, F32) + ("far",), shape(qw, BF16)],
        rows * width * qw * 2,
    )


def pair_product(own, other, w_ref, at):
    size = own.shape[1]
    base = w_ref.shape[1] // 2
    return jnp.concatenate(
        [
            mm(own, w_ref[f, at * size : at * size + size, :])
            + mm(other, w_ref[f, base + at * size : base + at * size + size, :])
            for f in range(w_ref.shape[0])
        ],
        axis=1,
    )


def join_body(at, own_ref, other_ref, w_ref, *refs):
    term = pair_product(own_ref[...], other_ref[...], w_ref, at)
    refs[-1][...] = term if len(refs) == 1 else refs[0][...] + term


def join_last_body(at, own_ref, other_ref, w_ref, x_ref, g_ref, *refs):
    r_ref, n_ref = refs[-2:]
    term = pair_product(own_ref[...], other_ref[...], w_ref, at)
    if len(refs) == 3:
        term = refs[0][...] + term
    r = x_ref[...].astype(F32) + term
    r_ref[...] = r
    n_ref[...] = (r * row_scale(r) * g_ref[0:1]).astype(BF16)


def join(x, gain, w, own, others, step):
    rows, width = x.shape
    shape = lambda w, t: (jax.ShapeDtypeStruct((rows, w), t), None)
    flops = rows * width * width
    so_far = []
    for at, (mine, other) in enumerate(zip(own, others)):
        ins = [(mine, "rows"), (other, "far rows"), (w, "whole")]
        held = [(v, "rows") for v in so_far]
        if at < len(own) - 1:
            so_far = row_call(
                functools.partial(join_body, at), "join", step, rows, ins + held, [shape(width, F32)], flops
            )
    return row_call(
        functools.partial(join_last_body, at), "join_last", step, rows,
        ins + [(x, "far rows"), (gain, "whole")] + held,
        [shape(width, F32) + ("far",), shape(width, BF16)],
        flops,
    )


def into_body(pairs, aliased, a_ref, b_ref, r_ref, dy_ref, g_ref, w_ref, mix_ref, *refs):
    d_ref, db_ref, do_ref, dlt_ref, gg_ref = refs[aliased:]
    gain = g_ref[0:1]
    r = r_ref[...]
    scale = row_scale(r)
    d = a_ref[...].astype(F32) + b_ref[...].astype(F32)
    scaled = d * gain
    back = scale * scaled - r * (scale * scale * scale) * jnp.mean(r * scaled, axis=-1, keepdims=True)

    @pl.when(pl.program_id(0) == 0)
    def _():
        gg_ref[...] = jnp.zeros_like(gg_ref)

    gg_ref[0:1] += jnp.sum(d * r * scale, axis=0, keepdims=True)
    out = dy_ref[...].astype(F32) + back
    d_ref[...] = out
    out = out.astype(BF16)
    db_ref[...] = out
    size = w_ref.shape[2]
    do = sum(mm(out[:, f * size : f * size + size], w_ref[f], NT) for f in range(w_ref.shape[0]))
    do = do.astype(BF16)
    do_ref[...] = do
    lane = lax.broadcasted_iota(jnp.int32, (8, 128), 1) // HD
    sub = lax.broadcasted_iota(jnp.int32, (8, 128), 0)
    for p in range(pairs):
        total = jnp.zeros((8, r.shape[0]), F32)
        for hh in range(2):
            c = slice(256 * p + 128 * hh, 256 * p + 128 * hh + 128)
            x = do[:, c].astype(F32) * mix_ref[:, c]
            total += lax.dot_general(
                jnp.where(sub == 2 * hh + lane, 1.0, 0.0), x, NT,
                precision=lax.Precision.HIGHEST, preferred_element_type=F32,
            )
        dlt_ref[p] = total


def into_attention(a, b, resid, dy, gain, w, mix, given, first, step):
    rows, width = resid.shape
    wide = w.shape[1] // 2
    pairs = wide // 256
    own_w = pl.BlockSpec((w.shape[0], wide, w.shape[2]), lambda i: (0, 0, 0))
    shape = lambda w, t: (jax.ShapeDtypeStruct((rows, w), t), None)
    hbm = pl.BlockSpec(memory_space=pl.ANY)
    base = [(a, "far part"), (b, "far part"), (resid, "far rows"), (dy, "far rows"), (gain, "whole"), (w, own_w), (mix, "far rows")]
    given = list(given or ())
    return row_call(
        functools.partial(into_body, pairs, len(given)), "into_attention", step, rows,
        base + [(g, hbm) for g in given],
        [
            shape(width, F32) + ("far",), shape(width, BF16) + ("far",), shape(wide, BF16),
            (jax.ShapeDtypeStruct((pairs, 8, rows), F32), pl.BlockSpec((pairs, 8, step), lambda i: (0, 0, i + first))),
            (jax.ShapeDtypeStruct((8, width), F32), pl.BlockSpec((8, width), lambda i: (0, 0))),
        ],
        rows * width * wide,
        aliases={len(base) + k: k for k in range(len(given))},
        first=first, count=a.shape[0] // step,
    )


def leave_body(a_ref, b_ref, x_ref, g_ref, d_ref, out_ref):
    x = x_ref[...].astype(F32)
    scale = row_scale(x)
    scaled = (a_ref[...].astype(F32) + b_ref[...].astype(F32)) * g_ref[0:1]
    back = scale * scaled - x * (scale * scale * scale) * jnp.mean(x * scaled, axis=-1, keepdims=True)
    out_ref[...] = d_ref[...] + back


def leave(a, b, x, gain, d, step):
    rows, width = x.shape
    return row_call(
        leave_body, "leave", step, rows,
        [(a, "far rows"), (b, "far rows"), (x, "far rows"), (gain, "whole"), (d, "far rows")],
        [(jax.ShapeDtypeStruct((rows, width), F32), None)],
        rows * width * 16,
    )[0]


def rope_back_body(terms, dq_ref, q_ref, k_ref, cos_ref, sin_ref, gain_ref, *rest):
    dkv_refs, (out_ref, gg_ref) = rest[:terms], rest[terms:]
    cos, sin = cos_ref[...], sin_ref[...]

    @pl.when(pl.program_id(0) == 0)
    def _():
        gg_ref[...] = jnp.zeros_like(gg_ref)

    def one(d, u, row):
        gain = gain_ref[row : row + 1]
        dn = d * cos + turn(d * sin)
        r = lax.rsqrt(head_mean(u * u) + EPSILON)
        gd = gain * dn
        gg_ref[row : row + 1] += jnp.sum(dn * u * r, axis=0, keepdims=True)
        return (r * gd - u * (r * r * r) * head_mean(u * gd)).astype(BF16)

    qw, kw = q_ref.shape[1], k_ref.shape[1]
    for t in range(qw // 128):
        c = slice(128 * t, 128 * t + 128)
        out_ref[:, c] = one(dq_ref[:, c] * 0.125, q_ref[:, c], 0)
    for t in range(kw // 128):
        dk = sum(ref[:, 256 * t : 256 * t + 128].astype(F32) for ref in dkv_refs)
        dv = sum(ref[:, 256 * t + 128 : 256 * t + 256].astype(F32) for ref in dkv_refs)
        out_ref[:, qw + 128 * t : qw + 128 * t + 128] = one(dk, k_ref[:, 128 * t : 128 * t + 128], 1)
        out_ref[:, qw + kw + 128 * t : qw + kw + 128 * t + 128] = dv.astype(BF16)


def rope_back(dq, q_raw, k_raw, cos, sin, gains, dkvs, step):
    rows, qw = q_raw.shape
    kw = k_raw.shape[1]
    spec = lambda w: pl.BlockSpec((step, w), lambda i: (i, 0))
    fixed = pl.BlockSpec((8, 128), lambda i: (0, 0))
    return pl.pallas_call(
        functools.partial(rope_back_body, len(dkvs)),
        out_shape=(
            jax.ShapeDtypeStruct((rows, qw + 2 * kw), BF16),
            jax.ShapeDtypeStruct((8, 128), F32),
        ),
        grid=(rows // step,),
        in_specs=[spec(qw), spec(qw), spec(kw), spec(128), spec(128), fixed]
        + [spec(2 * kw)] * len(dkvs),
        out_specs=(spec(qw + 2 * kw), fixed),
        compiler_params=pltpu.CompilerParams(vmem_limit_bytes=24 << 20),
        cost_estimate=cost(rows * qw * 1600, rows * qw * 20),
        name="rope_back",
    )(*map(far, (dq, q_raw, k_raw, cos, sin)), gains, far(dkvs[0]), *dkvs[1:])


def middle_body(step, aliased, n_ref, dy_ref, wg_ref, wu_ref, wd_ref, *refs):
    h_ref, dg_ref, du_ref, dn_ref, acc = refs[aliased:]

    @pl.when(pl.program_id(0) == 0)
    def _():
        acc[...] = jnp.zeros_like(acc)

    for at in range(0, n_ref.shape[0], step):
        rows = pl.ds(at, step)
        n = n_ref[rows, :]
        g = mm(n, wg_ref[...])
        u = mm(n, wu_ref[...])
        dh = mm(dy_ref[rows, :], wd_ref[...], NT)
        s = 1.0 / (1.0 + jnp.exp2(g * (-LOG2E)))
        act = g * s
        h_ref[rows, :] = (act * u).astype(BF16)
        du_ref[rows, :] = (dh * act).astype(BF16)
        dg_ref[rows, :] = (dh * u * s * (1.0 + g * (1.0 - s))).astype(BF16)
    acc[...] += mm(dg_ref[...], wg_ref[...], NT) + mm(du_ref[...], wu_ref[...], NT)

    @pl.when(pl.program_id(0) == pl.num_programs(0) - 1)
    def _():
        dn_ref[...] = acc[...].astype(BF16)


def middle(n, dy, both, wd, given, at, parts):
    total, width = n.shape
    rows = total // parts
    hidden = both.shape[1] // 2
    tile = 256
    whole = pl.BlockSpec((rows, width), lambda j: (at, 0))
    cols = pl.BlockSpec((width, tile), lambda j: (0, j))
    more = pl.BlockSpec((width, tile), lambda j: (0, j + hidden // tile))
    outs = pl.BlockSpec((rows, tile), lambda j: (at, j))
    shape = jax.ShapeDtypeStruct((total, hidden), BF16)
    given = list(given or ())
    return pl.pallas_call(
        functools.partial(middle_body, min(rows, 256), len(given)),
        out_shape=(shape, shape, shape, jax.ShapeDtypeStruct((rows, width), BF16)),
        grid=(hidden // tile,),
        in_specs=[whole, whole, cols, more, pl.BlockSpec((tile, width), lambda j: (j, 0))]
        + [pl.BlockSpec(memory_space=pl.ANY)] * len(given),
        out_specs=(outs, outs, outs, pl.BlockSpec((rows, width), lambda j: (0, 0))),
        scratch_shapes=[pltpu.VMEM((rows, width), F32)],
        input_output_aliases={5 + k: k for k in range(len(given))},
        compiler_params=pltpu.CompilerParams(vmem_limit_bytes=24 << 20),
        cost_estimate=cost(10 * rows * width * hidden, 6 * (rows * hidden + width * hidden)),
        name="middle",
    )(n, far(dy), far(both), far(both), far(wd), *given)


def down_body(h_ref, w_ref, out_ref):
    out_ref[...] = mm(h_ref[...], w_ref[...]).astype(BF16)


def down(h, w):
    rows, hidden = h.shape
    width = w.shape[1]
    tile = min(rows, 256)
    return pl.pallas_call(
        down_body,
        out_shape=jax.ShapeDtypeStruct((rows, width), BF16),
        grid=(rows // tile,),
        in_specs=[
            pl.BlockSpec((tile, hidden), lambda j: (j, 0)),
            pl.BlockSpec((hidden, width), lambda j: (0, 0)),
        ],
        out_specs=pl.BlockSpec((tile, width), lambda j: (j, 0)),
        compiler_params=pltpu.CompilerParams(vmem_limit_bytes=24 << 20),
        cost_estimate=cost(2 * rows * width * hidden, 2 * (rows * hidden + width * hidden)),
        name="down",
    )(h, w)


def grad_body(at_ref, a_ref, z_ref, b_ref, keep_ref, give_ref):
    keep_ref[0] = mm(a_ref[...], b_ref[...], TN).astype(BF16)
    give_ref[0] = mm(z_ref[...], b_ref[...], TN).astype(BF16)


def weight_grad(a, b, parts, core):
    rows, width = a.shape
    cols = b.shape[1]
    block = width // parts
    tile = next(t for t in (2304, 1024, 512, 256, 128) if cols % t == 0)
    shape = jax.ShapeDtypeStruct((parts // 2, block, cols), BF16)
    out = pl.BlockSpec((1, block, tile), lambda j, i, c: (i, 0, j))
    return pl.pallas_call(
        grad_body,
        out_shape=(pltpu.HBM(shape.shape, BF16), pltpu.HBM(shape.shape, BF16)),
        grid_spec=pltpu.PrefetchScalarGridSpec(
            num_scalar_prefetch=1,
            grid=(cols // tile, parts // 2),
            in_specs=[
                pl.BlockSpec((rows, block), lambda j, i, c: (0, 2 * i + c[0])),
                pl.BlockSpec((rows, block), lambda j, i, c: (0, 2 * i + 1 - c[0])),
                pl.BlockSpec((rows, tile), lambda j, i, c: (0, j)),
            ],
            out_specs=(out, out),
        ),
        compiler_params=pltpu.CompilerParams(vmem_limit_bytes=24 << 20),
        cost_estimate=cost(2 * rows * width * cols, 2 * (rows * width + rows * cols + width * cols)),
        name="weight_grad",
    )(core.reshape(1), a, a, b)


def swap(x):
    n = lax.axis_size("tp")
    return lax.ppermute(x, "tp", [(i, i ^ 1) for i in range(n)])


def core_swap(x):
    n = lax.axis_size("fsdp")
    return lax.ppermute(x, "fsdp", [(i, i ^ 1) for i in range(n)])


def y_shift(x, s):
    n = lax.axis_size("fsdp")
    return lax.ppermute(x, "fsdp", [(i, (i + 2 * s) % n) for i in range(n)])


def gather_y(x):
    n = lax.axis_size("fsdp")
    y, ny = lax.axis_index("fsdp") // 2, n // 2
    mine = jnp.zeros((ny,) + x.shape, x.dtype)
    mine = lax.dynamic_update_index_in_dim(mine, x, y, 0)
    for s in range(1, ny):
        mine = lax.dynamic_update_index_in_dim(mine, y_shift(x, s), (y - s) % ny, 0)
    return mine


def gather_core(mine):
    c = lax.axis_index("fsdp") % 2
    other = core_swap(mine)
    lower = jnp.where(c == 0, mine, other)
    upper = jnp.where(c == 0, other, mine)
    return jnp.stack([lower, upper], axis=1)


def core_sums(keep, give):
    ny = keep.shape[0]
    y = lax.axis_index("fsdp") // 2
    got = core_swap(give)
    sends = [both_block(keep, got, (y + s) % ny).astype(BF16) for s in range(1, ny)]
    return keep, got, sends


def both_block(keep, got, n):
    a = lax.dynamic_index_in_dim(keep, n, 0, keepdims=False).astype(F32)
    return a + lax.dynamic_index_in_dim(got, n, 0, keepdims=False).astype(F32)


def y_sums(keep, got, sends, *after):
    parts = [y_shift(send, s + 1) for s, send in enumerate(sends)]
    keep, got, *rest = lax.optimization_barrier((keep, got, *parts, *after))
    total = both_block(keep, got, lax.axis_index("fsdp") // 2)
    for part in rest[: len(parts)]:
        total = total + part.astype(F32)
    return total.astype(BF16)


def nearest(m, i, n):
    left, right = i, n - 1 - i
    near = min(left, right)
    if m == 0:
        return 0
    if m <= 2 * near:
        return (m + 1) // 2 if m % 2 else -(m // 2)
    return m - near if right > left else -(m - near)


def choose(index, table):
    value = table[0][0]
    for array, positions in table[1:]:
        here = functools.reduce(jnp.logical_or, [index == i for i in positions])
        value = jnp.where(here, array, value)
    return value


def tie(x, *others):
    return lax.optimization_barrier((x,) + others)[0]


def tables(x):
    lane = jnp.arange(128)
    exponent = -((lane % (HD // 2)).astype(F32) * 2.0) / HD
    angle = x.astype(F32)[:, None] * (ROPE_BASE**exponent)[None, :]
    sign = jnp.where(lane % HD < HD // 2, -1.0, 1.0).astype(F32)
    return jnp.cos(angle), jnp.sin(angle) * sign[None, :]


def per_device(
    tokens, cotangent, block_order, positions,
    attn_gain, w_query, key_weight, value_weight, query_gain, key_gain,
    w_out, ffn_gain, w_gate, w_up, w_down,
):
    n_ctx = lax.axis_size("ctx")
    n_fsdp = lax.axis_size("fsdp")
    me = lax.axis_index("ctx")
    seqs, rows, width = tokens.shape
    x = tokens.reshape(seqs * rows, width)
    dy = cotangent.reshape(seqs * rows, width)
    block = rows // 2
    qw, kw = w_query.shape[1], key_weight.shape[1]
    gs, hs = attn_gain.shape[0], query_gain.shape[0]

    qkv_w = qw + 2 * kw
    small = jnp.concatenate([attn_gain, ffn_gain, query_gain, key_gain])
    small = jnp.pad(small.reshape(1, -1), ((0, 15), (0, qkv_w - 2 * (gs + hs))))
    packed = jnp.concatenate(
        [jnp.concatenate([w_query, key_weight, value_weight], axis=1), small], axis=0
    )
    mine = gather_y(packed)
    out_i = tie(w_out, packed)
    out_i = jnp.concatenate([out_i, swap(out_i)], axis=0)
    cos, sin = tables(positions.reshape(-1))
    both_i = jnp.concatenate(lax.optimization_barrier((w_gate, w_up, packed))[:2], axis=1)
    mine, out_i, cos, sin, both_i = lax.optimization_barrier((mine, out_i, cos, sin, both_i))
    both_full = lax.all_gather(both_i, "fsdp", axis=0, tiled=True)
    packed = gather_core(mine).reshape(n_fsdp, gs + 16, qkv_w)
    small = packed[:, gs].astype(F32)
    row = lambda v: jnp.broadcast_to(v.reshape(1, -1), (8, v.size))
    gain_attn = row(small[:, :gs])
    gain_ffn = row(small[:, gs : 2 * gs])
    gain_q = small[:, 2 * gs : 2 * gs + hs].reshape(-1)
    gain_k = small[:, 2 * gs + hs : 2 * (gs + hs)].reshape(-1)
    gains = jnp.stack([jnp.tile(gain_q, 2), jnp.tile(gain_k, 2)] + [jnp.zeros(128, F32)] * 6)

    step = min(256, block)
    normed_b, k_raw, kv_b = project_keys(x, gain_attn, packed, cos, sin, gains, kw, step)
    q_raw, q_b = project_queries(tie(normed_b, kv_b), packed, cos, sin, gains, qw, step)
    place = (me.astype(jnp.int32).reshape(1), block_order)
    shards = {0: kv_b}

    def shard(m):
        table = {}
        for i in range(n_ctx):
            table.setdefault(nearest(m, i, n_ctx), []).append(i)
        return choose(me, [(shards[d], where) for d, where in table.items()])

    kvs = []
    acc = None
    for t in range(1, n_ctx):
        right = [(i, i + 1) for i in range(t - 1, n_ctx - 1)]
        left = [(i, i - 1) for i in range(1, n_ctx - t + 1)]
        shards[-t] = lax.ppermute(shards[-(t - 1)], "ctx", right)
        shards[t] = lax.ppermute(shards[t - 1], "ctx", left)
        if t == 1:
            shards[-t], shards[t], q_b = lax.optimization_barrier((shards[-t], shards[t], q_b))
            out_w = lax.all_gather(tie(out_i, kv_b), "fsdp", axis=0, tiled=False)
            down_full = lax.all_gather(tie(w_down, q_b), "fsdp", axis=1, tiled=True)
            continue
        while len(kvs) < t:
            kvs.append(shard(len(kvs)))
            acc = attend(len(kvs) - 1, n_ctx, place, q_b, kvs[-1], acc, False, block)
        shards[-t], shards[t], acc = lax.optimization_barrier((shards[-t], shards[t], acc))
        if t == 2:
            acc = tie(acc, both_full)
    while len(kvs) < n_ctx - 1:
        kvs.append(shard(len(kvs)))
        acc = attend(len(kvs) - 1, n_ctx, place, q_b, kvs[-1], acc, False, block)
    m = n_ctx - 1
    kvs.append(shard(m))
    pairs = kw // 128
    mixes, others = [], []
    last_q = q_b
    for p in range(pairs):
        mixes.append(attend(m, n_ctx, place, last_q, kvs[m], acc, True, block, p))
        last_q = tie(q_b, mixes[-1][0])
        others.append(swap(mixes[-1][0]))
    mixed_b = jnp.concatenate([piece[0] for piece in mixes], axis=1)
    mix = jnp.concatenate([piece[1] for piece in mixes], axis=1)
    lse = jnp.concatenate([piece[2] for piece in mixes], axis=0)

    own = [piece[0] for piece in mixes]
    resid, two_b = join(x, gain_ffn, out_w, own, others, step)

    core = lax.axis_index("fsdp") % 2

    parts = 2
    given, d_parts, d_others = None, [], []
    two_t = two_b
    for at in range(parts):
        *given, d_part = middle(two_t, dy, both_full, down_full, given, at, parts)
        two_t = tie(two_b, d_part)
        d_parts.append(d_part)
        d_others.append(swap(d_part))
    hidden, dgate, dup = given
    down_w = weight_grad(dy, hidden, n_fsdp, core)
    two_t, hidden_t = lax.optimization_barrier((two_b, hidden, down_w, d_others[0]))[:2]
    gate_w = weight_grad(two_t, dgate, n_fsdp, core)
    up_w = weight_grad(two_t, dup, n_fsdp, core)
    down_part = down(hidden_t, down_full)
    d_others[-1], down_w, gate_w, up_w, down_part = lax.optimization_barrier(
        (d_others[-1], down_w, gate_w, up_w, down_part)
    )
    down_c, gate_c, up_c = core_sums(*down_w), core_sums(*gate_w), core_sums(*up_w)

    given, ffn_gain_g = None, 0.0
    per = rows * seqs // parts // step
    for at in range(parts):
        *given, g = into_attention(
            d_parts[at], d_others[at], resid, dy, gain_ffn, out_w, mix, given, at * per, step
        )
        ffn_gain_g = ffn_gain_g + g[0]
    d_resid, d_resid_b, do, dlt = given
    do = tie(do, *down_c[2], *gate_c[2])

    grads = [None] * n_ctx
    got = {}
    dq = None
    for m in reversed(range(n_ctx)):
        dq, grads[m] = attend_back(m, n_ctx, place, q_b, do, kvs[m], lse, dlt, dq, block)
        if m == 0:
            break
        sends = []
        for side in (1, -1):
            table = {}
            for i in range(n_ctx):
                for k in range(1, n_ctx):
                    if nearest(k, i, n_ctx) == side * m:
                        table.setdefault(k, []).append(i)
            send = choose(me, [(grads[k], where) for k, where in table.items()])
            if side in got:
                send = (send.astype(F32) + got[side].astype(F32)).astype(BF16)
            sends.append(send)
            senders = sorted(i for where in table.values() for i in where)
            got[side] = lax.ppermute(send, "ctx", [(i, i + side) for i in senders])
        if m == n_ctx - 1:
            down_other = swap(tie(down_part, dq))
            down_s = y_sums(*down_c)
            sends += [down_s] + up_c[2]
            down_s = lax.psum(down_s, "ctx")
        if m == max(n_ctx - 2, 1):
            gate_s = y_sums(*gate_c, dq)
            sends.append(gate_s)
            out_g = weight_grad(tie(d_resid_b, dq), mixed_b, n_fsdp, core)
        if m == 1:
            up_s = y_sums(*up_c, dq)
            sends += [up_s, *out_g]
            gate_s, up_s, down_s = lax.optimization_barrier((gate_s, up_s, down_s))
            gate_s, up_s = lax.psum((gate_s, up_s), "ctx")
        dq = tie(dq, *sends)
    dq, down_other = lax.optimization_barrier((dq, down_other))
    out_s = y_sums(*core_sums(*out_g))
    home = [grads[0]] + list(got.values())
    output = (tie(resid, dq) + (down_part.astype(F32) + down_other.astype(F32))).astype(BF16)

    d_qkv, head_gain = rope_back(dq, q_raw, k_raw, cos, sin, gains, home, step)
    qkv_c = core_sums(*weight_grad(normed_b, d_qkv, n_fsdp, core))
    w_qkv = packed[:, :gs].reshape(n_fsdp * gs, qkv_w)
    normed_part = mm(d_qkv, w_qkv, NT)

    head_gain = head_gain[:2, :HD] + head_gain[:2, HD:]
    xf = x.astype(F32)
    inv_one = lax.rsqrt(jnp.mean(xf * xf, axis=-1, keepdims=True) + EPSILON)
    attn_gain_g = jnp.sum(normed_part * (xf * inv_one), axis=0)
    small_g = jnp.concatenate(
        [
            attn_gain_g.reshape(n_fsdp, gs),
            0.5 * ffn_gain_g.reshape(n_fsdp, gs),
            head_gain[0].reshape(n_fsdp, hs),
            head_gain[1].reshape(n_fsdp, hs),
        ],
        axis=1,
    )
    small_g = (small_g + swap(small_g)).astype(BF16).reshape(n_fsdp // 2, 2, 1, -1)
    normed_part = tie(normed_part.astype(BF16), small_g)
    normed_other = swap(normed_part)
    small_s = y_sums(
        *core_sums(
            lax.dynamic_index_in_dim(small_g, core, 1, keepdims=False),
            lax.dynamic_index_in_dim(small_g, 1 - core, 1, keepdims=False),
        )
    )
    last = jnp.concatenate([y_sums(*qkv_c), out_s], axis=1)
    small_s = jnp.pad(small_s, ((0, 15), (0, last.shape[1] - small_s.shape[1])))
    last = jnp.concatenate([last, small_s], axis=0)
    last, gate_s, up_s = lax.optimization_barrier((last, gate_s, up_s))
    last = lax.psum(last, "ctx")
    input_grad = leave(normed_part, normed_other, x, gain_attn, d_resid, step)
    last = tie(last, input_grad)
    q_s, k_s, v_s = last[:gs, :qw], last[:gs, qw : qw + kw], last[:gs, qw + kw : qkv_w]
    out_s = last[:gs, qkv_w:]
    small_s = last[gs : gs + 1, : 2 * (gs + hs)]
    down_s, gate_s, up_s, out_s, q_s, k_s, v_s = (
        v.astype(F32) for v in (down_s, gate_s, up_s, out_s, q_s, k_s, v_s)
    )
    small_g = small_s[0].astype(F32)
    return (
        output.reshape(tokens.shape),
        input_grad.reshape(tokens.shape),
        small_g[:gs],
        q_s,
        k_s,
        v_s,
        small_g[2 * gs : 2 * gs + hs],
        small_g[2 * gs + hs :],
        out_s.T,
        small_g[gs : 2 * gs],
        gate_s,
        up_s,
        down_s.T,
    )


def solution(mesh):
    rows = P("fsdp", "ctx", None)
    ins = P("fsdp", "tp")
    outs = P("tp", "fsdp")
    one = P("fsdp")
    return jax.shard_map(
        per_device,
        mesh=mesh,
        in_specs=(
            rows, rows, P(), P("fsdp", "ctx"), one, ins, ins, ins, one, one, outs, one, ins, ins, outs,
        ),
        out_specs=(rows, rows, one, ins, ins, ins, one, one, outs, one, ins, ins, outs),
        check_vma=False,
    )
```

```python
import functools

import jax
import jax.numpy as jnp
from jax import lax
from jax.experimental import pallas as pl
from jax.experimental.pallas import tpu as pltpu
from jax.sharding import PartitionSpec as P

HD = 64
EPSILON = 1e-05
ROPE_BASE = 1000000.0
LOG2E = 1.4426950408889634
SCALE2 = 0.125 * LOG2E
NT = (((1,), (1,)), ((), ()))
NN = (((1,), (0,)), ((), ()))
TN = (((0,), (0,)), ((), ()))
F32, BF16 = jnp.float32, jnp.bfloat16


def mm(a, b, dims=NN):
    return lax.dot_general(a, b, dims, preferred_element_type=F32)


def cost(flops, bytes_accessed):
    return pl.CostEstimate(
        flops=flops // 64, bytes_accessed=bytes_accessed // 64, transcendentals=0
    )


def far(x):
    return pltpu.with_memory_space_constraint(x, pltpu.HBM)


def half(shape, which):
    lane = lax.broadcasted_iota(jnp.int32, shape, len(shape) - 1)
    return (lane < HD) if which == 0 else (lane >= HD)


def pieces(m, n_ctx, block, where, order):
    me = where[0]

    def low(shard):
        first, second = order[2 * shard], order[2 * shard + 1]
        return jnp.minimum(first, second), jnp.where(first < second, 0, block)

    q_id, q_low = low(me)
    q_high = block - q_low
    if m == 0:
        q_low, q_high = pl.multiple_of(q_low, block), pl.multiple_of(q_high, block)
        return [(q_low, q_low, True), (q_high, q_low, False), (q_high, q_high, True)]
    left, right = me, n_ctx - 1 - me
    beyond = m - jnp.minimum(left, right)
    inner = (m + 1) // 2 if m % 2 else -(m // 2)
    outer = jnp.where(right > left, beyond, -beyond)
    far = me + jnp.where(m <= 2 * jnp.minimum(left, right), inner, outer)
    k_id, k_low = low(far)
    before = k_id < q_id
    q_first = pl.multiple_of(jnp.where(before, q_low, q_high), block)
    k_second = pl.multiple_of(jnp.where(before, k_low, block - k_low), block)
    return [
        (q_first, pl.multiple_of(k_low, block), False),
        (pl.multiple_of(q_high, block), k_second, False),
    ]


def attend_body(m, n_ctx, first, last, block, where, order, q_ref, kv_ref, *rest):
    rest = list(rest)
    given = None if first else rest.pop(0)
    if last:
        mixb_ref, mix_ref, lse_ref, acc = rest
    else:
        (acc,) = rest
    acc[...] = jnp.zeros_like(acc) if first else given[...]
    for q_at, k_at, diagonal in pieces(m, n_ctx, block, where, order):
        kt = kv_ref[pl.ds(k_at, block), 0:128]
        vt = kv_ref[pl.ds(k_at, block), 128:256]
        one = jnp.ones((block, HD), BF16)
        for hh in range(2):
            kh = kt[:, HD * hh : HD * hh + HD]
            vh = vt[:, HD * hh : HD * hh + HD]
            kd = jnp.concatenate([kh, kh], axis=1)
            vx = (jnp.concatenate([vh, one], axis=1), jnp.concatenate([one, vh], axis=1))
            qt = q_ref[pl.ds(q_at, block), 128 * hh : 128 * hh + 128]
            for r in range(2):
                qr = jnp.where(half((block, 128), r), qt, jnp.zeros_like(qt))
                p = jnp.exp2(mm(qr, kd, NT) * SCALE2)
                if diagonal:
                    row = lax.broadcasted_iota(jnp.int32, p.shape, 0)
                    col = lax.broadcasted_iota(jnp.int32, p.shape, 1)
                    p = jnp.where(col <= row, p, 0.0)
                c = 256 * hh + 128 * r
                acc[pl.ds(q_at, block), c : c + 128] += mm(p.astype(BF16), vx[r])
    if last:
        rows = acc.shape[0]
        lane = lax.broadcasted_iota(jnp.int32, (8, 128), 1)
        sub = lax.broadcasted_iota(jnp.int32, (8, 128), 0)
        total = jnp.zeros((8, rows), F32)
        for hh in range(2):
            out = []
            for r in range(2):
                a = acc[:, 256 * hh + 128 * r : 256 * hh + 128 * r + 128]
                out.append(a / pltpu.roll(a, HD, 1))
                pick = jnp.where((lane == (HD if r == 0 else 0)) & (sub == 2 * hh + r), 1.0, 0.0)
                total += lax.dot_general(
                    pick, a, NT, precision=lax.Precision.HIGHEST, preferred_element_type=F32
                )
            mix = jnp.where(half((rows, 128), 0), out[0], out[1])
            mix_ref[:, 128 * hh : 128 * hh + 128] = mix
            mixb_ref[:, 128 * hh : 128 * hh + 128] = mix.astype(BF16)
        lse_ref[0] = jnp.log2(jnp.where(sub[:, 0:1] < 4, total, 1.0))


def attend(m, n_ctx, place, q, kv, acc, last, block, at=None):
    rows = q.shape[0]
    total = kv.shape[1] // 256
    base, pairs = (0, total) if at is None else (at, 1)
    first = acc is None
    args = [*place, q, kv]
    wide = pl.BlockSpec((rows, 512), lambda g, *_: (0, g))
    slim = pl.BlockSpec((rows, 256), lambda g, *_: (0, g))
    pair = pl.BlockSpec((rows, 256), lambda g, *_: (0, g + base))
    in_specs = [pair, pair]
    if not first:
        in_specs.append(pl.BlockSpec((rows, 512), lambda g, *_: (0, g + base)))
        args.append(far(acc) if m == n_ctx - 2 else acc)
    if last:
        out_shape = (
            jax.ShapeDtypeStruct((rows, pairs * 256), BF16),
            pltpu.HBM((rows, pairs * 256), F32),
            jax.ShapeDtypeStruct((pairs, 8, rows), F32),
        )
        out_specs = (slim, slim, pl.BlockSpec((1, 8, rows), lambda g, *_: (g, 0, 0)))
        scratch = [pltpu.VMEM((rows, 512), F32)]
    else:
        out_shape = (pltpu.HBM if m > 0 else jax.ShapeDtypeStruct)((rows, pairs * 512), F32)
        out_specs = wide
        scratch = []
    work = 2 * block * block * pairs * 4
    return pl.pallas_call(
        functools.partial(attend_body, m, n_ctx, first, last, block),
        out_shape=out_shape,
        grid_spec=pltpu.PrefetchScalarGridSpec(
            num_scalar_prefetch=2,
            grid=(pairs,),
            in_specs=in_specs,
            out_specs=out_specs,
            scratch_shapes=scratch,
        ),
        compiler_params=pltpu.CompilerParams(vmem_limit_bytes=24 << 20),
        cost_estimate=cost(work * 1024, 12 << 20),
        name="attend",
    )(*args)


def attend_back_body(m, n_ctx, first, block, where, order, q_ref, do_ref, kv_ref, lse_ref, dlt_ref, *rest):
    rest = list(rest)
    given = None if first else rest.pop(0)
    dq, dkv_ref, dka, dva = rest
    dq[...] = jnp.zeros_like(dq) if first else given[...]
    dka[...] = jnp.zeros_like(dka)
    dva[...] = jnp.zeros_like(dva)
    for q_at, k_at, diagonal in pieces(m, n_ctx, block, where, order):
        kt = kv_ref[pl.ds(k_at, block), 0:128]
        vt = kv_ref[pl.ds(k_at, block), 128:256]
        zero = jnp.zeros((block, HD), BF16)
        for hh in range(2):
            kh = kt[:, HD * hh : HD * hh + HD]
            vh = vt[:, HD * hh : HD * hh + HD]
            kx = (jnp.concatenate([kh, zero], axis=1), jnp.concatenate([zero, kh], axis=1))
            vx = (jnp.concatenate([vh, zero], axis=1), jnp.concatenate([zero, vh], axis=1))
            c = 128 * hh
            qt = q_ref[pl.ds(q_at, block), c : c + 128]
            dt = do_ref[pl.ds(q_at, block), c : c + 128]
            dvs, dks, dqs = [], [], None
            for r in range(2):
                row = 2 * hh + r
                lse = lse_ref[0, row : row + 1, pl.ds(q_at, block)]
                dlt = dlt_ref[0, row : row + 1, pl.ds(q_at, block)]
                p = jnp.exp2(mm(kx[r], qt, NT) * SCALE2 - lse)
                if diagonal:
                    key = lax.broadcasted_iota(jnp.int32, p.shape, 0)
                    query = lax.broadcasted_iota(jnp.int32, p.shape, 1)
                    p = jnp.where(key <= query, p, 0.0)
                ds = (p * (mm(vx[r], dt, NT) - dlt)).astype(BF16)
                dvs.append(mm(p.astype(BF16), dt))
                dks.append(mm(ds, qt))
                term = mm(ds, kx[r], TN)
                dqs = term if dqs is None else dqs + term
            left = half((block, 128), 0)
            dva[pl.ds(k_at, block), c : c + 128] += jnp.where(left, dvs[0], dvs[1])
            dka[pl.ds(k_at, block), c : c + 128] += jnp.where(left, dks[0], dks[1])
            dq[pl.ds(q_at, block), c : c + 128] += dqs
    for at, ref, scale in ((0, dka, 0.125), (128, dva, 1.0)):
        a = ref[...]
        a = jnp.concatenate([a[:, 0:64] + a[:, 64:128], a[:, 128:192] + a[:, 192:256]], axis=1)
        dkv_ref[:, at : at + 128] = (a * scale).astype(dkv_ref.dtype)


def attend_back(m, n_ctx, place, q, do, kv, lse, dlt, dq, block):
    rows = q.shape[0]
    pairs = kv.shape[1] // 256
    first = dq is None
    slim = pl.BlockSpec((rows, 256), lambda g, *_: (0, g))
    line = pl.BlockSpec((1, 8, rows), lambda g, *_: (g, 0, 0))
    in_specs = [slim, slim, slim, line, line]
    args = [*place, q, do, kv, lse, dlt]
    if not first:
        in_specs.append(slim)
        args.append(far(dq))
    work = 2 * block * block * pairs * 4
    return pl.pallas_call(
        functools.partial(attend_back_body, m, n_ctx, first, block),
        out_shape=(
            pltpu.HBM((rows, pairs * 256), F32),
            pltpu.HBM((rows, pairs * 256), F32) if m == 0 else jax.ShapeDtypeStruct((rows, pairs * 256), BF16),
        ),
        grid_spec=pltpu.PrefetchScalarGridSpec(
            num_scalar_prefetch=2,
            grid=(pairs,),
            in_specs=in_specs,
            out_specs=(slim, slim),
            scratch_shapes=[pltpu.VMEM((rows, 256), F32), pltpu.VMEM((rows, 256), F32)],
        ),
        compiler_params=pltpu.CompilerParams(vmem_limit_bytes=24 << 20),
        cost_estimate=cost(work * 2048, 12 << 20),
        name="attend_back",
    )(*args)


def head_mean(u):
    a = lax.broadcasted_iota(jnp.int32, (128, 128), 0) // HD
    b = lax.broadcasted_iota(jnp.int32, (128, 128), 1) // HD
    ones = jnp.where(a == b, 1.0, 0.0).astype(BF16)
    high = u.astype(BF16)
    low = (u - high.astype(F32)).astype(BF16)
    return (mm(high, ones) + mm(low, ones)) * (1.0 / HD)


def turn(u):
    lane = lax.broadcasted_iota(jnp.int32, u.shape, 1)
    return jnp.where(lane % HD < HD // 2, pltpu.roll(u, 96, 1), pltpu.roll(u, 32, 1))


def rotated(u, gain, cos, sin):
    n = u * lax.rsqrt(head_mean(u * u) + EPSILON) * gain
    return (n * cos + turn(n) * sin).astype(BF16)


def row_scale(x):
    return lax.rsqrt(jnp.mean(x * x, axis=-1, keepdims=True) + EPSILON)


def blocks_product(n, w_ref):
    count = w_ref.shape[0]
    size = w_ref.shape[1] - 16
    return sum(mm(n[:, f * size : f * size + size], w_ref[f, 0:size, :]) for f in range(count))


def key_body(x_ref, g_ref, w_ref, cos_ref, sin_ref, gain_ref, n_ref, k_ref, kv_ref):
    x = x_ref[...].astype(F32)
    n = (x * row_scale(x) * g_ref[0:1]).astype(BF16)
    n_ref[...] = n
    both = blocks_product(n, w_ref)
    width = k_ref.shape[1]
    k_ref[...] = both[:, :width]
    for t in range(width // 128):
        c = 128 * t
        kv_ref[:, 2 * c : 2 * c + 128] = rotated(
            both[:, c : c + 128], gain_ref[1:2], cos_ref[...], sin_ref[...]
        )
        kv_ref[:, 2 * c + 128 : 2 * c + 256] = both[:, width + c : width + c + 128].astype(BF16)


def query_body(n_ref, w_ref, cos_ref, sin_ref, gain_ref, u_ref, q_ref):
    u = blocks_product(n_ref[...], w_ref)
    u_ref[...] = u
    for t in range(u.shape[1] // 128):
        c = slice(128 * t, 128 * t + 128)
        q_ref[:, c] = rotated(u[:, c], gain_ref[0:1], cos_ref[...], sin_ref[...])


def row_call(body, name, step, rows, ins, outs, flops, scratch=(), aliases=None, first=0, count=None):
    ins = list(ins)
    spec = lambda w: pl.BlockSpec((step, w), lambda i: (i + first, 0))
    in_specs = []
    for n, (array, kind) in enumerate(ins):
        if isinstance(kind, str) and kind.startswith("far "):
            kind = kind[4:]
            ins[n] = (far(array), kind)
        if kind == "rows":
            in_specs.append(spec(array.shape[1]))
        elif kind == "part":
            in_specs.append(pl.BlockSpec((step, array.shape[1]), lambda i: (i, 0)))
        elif kind == "whole":
            in_specs.append(pl.BlockSpec(array.shape, lambda i, n=array.ndim: (0,) * n))
        else:
            in_specs.append(kind)
    return pl.pallas_call(
        body,
        out_shape=tuple(pltpu.HBM(o[0].shape, o[0].dtype) if len(o) > 2 else o[0] for o in outs),
        grid=(rows // step if count is None else count,),
        in_specs=in_specs,
        out_specs=tuple(spec(o[0].shape[1]) if o[1] is None else o[1] for o in outs),
        scratch_shapes=list(scratch),
        input_output_aliases=aliases or {},
        compiler_params=pltpu.CompilerParams(vmem_limit_bytes=24 << 20),
        cost_estimate=cost(flops, 1 << 20),
        name=name,
    )(*(array for array, _ in ins))


def project_keys(x, gain, packed, cos, sin, gains, kw, step):
    rows, width = x.shape
    f, r, cols = packed.shape
    shape = lambda w, t: (jax.ShapeDtypeStruct((rows, w), t), None)
    part = pl.BlockSpec((f, r, 2 * kw), lambda i: (0, 0, cols // (2 * kw) - 1))
    return row_call(
        key_body, "project_keys", step, rows,
        [(x, "far rows"), (gain, "whole"), (packed, part), (cos, "far rows"), (sin, "far rows"), (gains, "whole")],
        [shape(width, BF16) + ("far",), shape(kw, F32) + ("far",), shape(2 * kw, BF16) + ("far",)],
        rows * width * kw * 4,
    )


def project_queries(n, packed, cos, sin, gains, qw, step):
    rows, width = n.shape
    f, r, _ = packed.shape
    shape = lambda w, t: (jax.ShapeDtypeStruct((rows, w), t), None)
    part = pl.BlockSpec((f, r, qw), lambda i: (0, 0, 0))
    return row_call(
        query_body, "project_queries", step, rows,
        [(n, "far rows"), (packed, part), (cos, "far rows"), (sin, "far rows"), (gains, "whole")],
        [shape(qw, F32) + ("far",), shape(qw, BF16)],
        rows * width * qw * 2,
    )


def pair_product(own, other, w_ref, at):
    size = own.shape[1]
    base = w_ref.shape[1] // 2
    return jnp.concatenate(
        [
            mm(own, w_ref[f, at * size : at * size + size, :])
            + mm(other, w_ref[f, base + at * size : base + at * size + size, :])
            for f in range(w_ref.shape[0])
        ],
        axis=1,
    )


def join_body(at, own_ref, other_ref, w_ref, *refs):
    term = pair_product(own_ref[...], other_ref[...], w_ref, at)
    refs[-1][...] = term if len(refs) == 1 else refs[0][...] + term


def join_last_body(at, own_ref, other_ref, w_ref, x_ref, g_ref, *refs):
    r_ref, n_ref = refs[-2:]
    term = pair_product(own_ref[...], other_ref[...], w_ref, at)
    if len(refs) == 3:
        term = refs[0][...] + term
    r = x_ref[...].astype(F32) + term
    r_ref[...] = r
    n_ref[...] = (r * row_scale(r) * g_ref[0:1]).astype(BF16)


def join(x, gain, w, own, others, step):
    rows, width = x.shape
    shape = lambda w, t: (jax.ShapeDtypeStruct((rows, w), t), None)
    flops = rows * width * width
    so_far = []
    for at, (mine, other) in enumerate(zip(own, others)):
        ins = [(mine, "rows"), (other, "far rows"), (w, "whole")]
        held = [(v, "rows") for v in so_far]
        if at < len(own) - 1:
            so_far = row_call(
                functools.partial(join_body, at), "join", step, rows, ins + held, [shape(width, F32)], flops
            )
    return row_call(
        functools.partial(join_last_body, at), "join_last", step, rows,
        ins + [(x, "far rows"), (gain, "whole")] + held,
        [shape(width, F32) + ("far",), shape(width, BF16)],
        flops,
    )


def into_body(pairs, aliased, a_ref, b_ref, r_ref, dy_ref, g_ref, w_ref, mix_ref, *refs):
    d_ref, db_ref, do_ref, dlt_ref, gg_ref = refs[aliased:]
    gain = g_ref[0:1]
    r = r_ref[...]
    scale = row_scale(r)
    d = a_ref[...].astype(F32) + b_ref[...].astype(F32)
    scaled = d * gain
    back = scale * scaled - r * (scale * scale * scale) * jnp.mean(r * scaled, axis=-1, keepdims=True)

    @pl.when(pl.program_id(0) == 0)
    def _():
        gg_ref[...] = jnp.zeros_like(gg_ref)

    gg_ref[0:1] += jnp.sum(d * r * scale, axis=0, keepdims=True)
    out = dy_ref[...].astype(F32) + back
    d_ref[...] = out
    out = out.astype(BF16)
    db_ref[...] = out
    size = w_ref.shape[2]
    do = sum(mm(out[:, f * size : f * size + size], w_ref[f], NT) for f in range(w_ref.shape[0]))
    do = do.astype(BF16)
    do_ref[...] = do
    lane = lax.broadcasted_iota(jnp.int32, (8, 128), 1) // HD
    sub = lax.broadcasted_iota(jnp.int32, (8, 128), 0)
    for p in range(pairs):
        total = jnp.zeros((8, r.shape[0]), F32)
        for hh in range(2):
            c = slice(256 * p + 128 * hh, 256 * p + 128 * hh + 128)
            x = do[:, c].astype(F32) * mix_ref[:, c]
            total += lax.dot_general(
                jnp.where(sub == 2 * hh + lane, 1.0, 0.0), x, NT,
                precision=lax.Precision.HIGHEST, preferred_element_type=F32,
            )
        dlt_ref[p] = total


def into_attention(a, b, resid, dy, gain, w, mix, given, first, step):
    rows, width = resid.shape
    wide = w.shape[1] // 2
    pairs = wide // 256
    own_w = pl.BlockSpec((w.shape[0], wide, w.shape[2]), lambda i: (0, 0, 0))
    shape = lambda w, t: (jax.ShapeDtypeStruct((rows, w), t), None)
    hbm = pl.BlockSpec(memory_space=pl.ANY)
    base = [(a, "far part"), (b, "far part"), (resid, "far rows"), (dy, "far rows"), (gain, "whole"), (w, own_w), (mix, "far rows")]
    given = list(given or ())
    return row_call(
        functools.partial(into_body, pairs, len(given)), "into_attention", step, rows,
        base + [(g, hbm) for g in given],
        [
            shape(width, F32) + ("far",), shape(width, BF16) + ("far",), shape(wide, BF16),
            (jax.ShapeDtypeStruct((pairs, 8, rows), F32), pl.BlockSpec((pairs, 8, step), lambda i: (0, 0, i + first))),
            (jax.ShapeDtypeStruct((8, width), F32), pl.BlockSpec((8, width), lambda i: (0, 0))),
        ],
        rows * width * wide,
        aliases={len(base) + k: k for k in range(len(given))},
        first=first, count=a.shape[0] // step,
    )


def leave_body(a_ref, b_ref, x_ref, g_ref, d_ref, out_ref):
    x = x_ref[...].astype(F32)
    scale = row_scale(x)
    scaled = (a_ref[...].astype(F32) + b_ref[...].astype(F32)) * g_ref[0:1]
    back = scale * scaled - x * (scale * scale * scale) * jnp.mean(x * scaled, axis=-1, keepdims=True)
    out_ref[...] = d_ref[...] + back


def leave(a, b, x, gain, d, step):
    rows, width = x.shape
    return row_call(
        leave_body, "leave", step, rows,
        [(a, "far rows"), (b, "far rows"), (x, "far rows"), (gain, "whole"), (d, "far rows")],
        [(jax.ShapeDtypeStruct((rows, width), F32), None)],
        rows * width * 16,
    )[0]


def rope_back_body(terms, dq_ref, q_ref, k_ref, cos_ref, sin_ref, gain_ref, *rest):
    dkv_refs, (out_ref, gg_ref) = rest[:terms], rest[terms:]
    cos, sin = cos_ref[...], sin_ref[...]

    @pl.when(pl.program_id(0) == 0)
    def _():
        gg_ref[...] = jnp.zeros_like(gg_ref)

    def one(d, u, row):
        gain = gain_ref[row : row + 1]
        dn = d * cos + turn(d * sin)
        r = lax.rsqrt(head_mean(u * u) + EPSILON)
        gd = gain * dn
        gg_ref[row : row + 1] += jnp.sum(dn * u * r, axis=0, keepdims=True)
        return (r * gd - u * (r * r * r) * head_mean(u * gd)).astype(BF16)

    qw, kw = q_ref.shape[1], k_ref.shape[1]
    for t in range(qw // 128):
        c = slice(128 * t, 128 * t + 128)
        out_ref[:, c] = one(dq_ref[:, c] * 0.125, q_ref[:, c], 0)
    for t in range(kw // 128):
        dk = sum(ref[:, 256 * t : 256 * t + 128].astype(F32) for ref in dkv_refs)
        dv = sum(ref[:, 256 * t + 128 : 256 * t + 256].astype(F32) for ref in dkv_refs)
        out_ref[:, qw + 128 * t : qw + 128 * t + 128] = one(dk, k_ref[:, 128 * t : 128 * t + 128], 1)
        out_ref[:, qw + kw + 128 * t : qw + kw + 128 * t + 128] = dv.astype(BF16)


def rope_back(dq, q_raw, k_raw, cos, sin, gains, dkvs, step):
    rows, qw = q_raw.shape
    kw = k_raw.shape[1]
    spec = lambda w: pl.BlockSpec((step, w), lambda i: (i, 0))
    fixed = pl.BlockSpec((8, 128), lambda i: (0, 0))
    return pl.pallas_call(
        functools.partial(rope_back_body, len(dkvs)),
        out_shape=(
            jax.ShapeDtypeStruct((rows, qw + 2 * kw), BF16),
            jax.ShapeDtypeStruct((8, 128), F32),
        ),
        grid=(rows // step,),
        in_specs=[spec(qw), spec(qw), spec(kw), spec(128), spec(128), fixed]
        + [spec(2 * kw)] * len(dkvs),
        out_specs=(spec(qw + 2 * kw), fixed),
        compiler_params=pltpu.CompilerParams(vmem_limit_bytes=24 << 20),
        cost_estimate=cost(rows * qw * 1600, rows * qw * 20),
        name="rope_back",
    )(*map(far, (dq, q_raw, k_raw, cos, sin)), gains, far(dkvs[0]), *dkvs[1:])


def middle_body(step, aliased, n_ref, dy_ref, wg_ref, wu_ref, wd_ref, *refs):
    h_ref, dg_ref, du_ref, dn_ref, acc = refs[aliased:]

    @pl.when(pl.program_id(0) == 0)
    def _():
        acc[...] = jnp.zeros_like(acc)

    for at in range(0, n_ref.shape[0], step):
        rows = pl.ds(at, step)
        n = n_ref[rows, :]
        g = mm(n, wg_ref[...])
        u = mm(n, wu_ref[...])
        dh = mm(dy_ref[rows, :], wd_ref[...], NT)
        s = 1.0 / (1.0 + jnp.exp2(g * (-LOG2E)))
        act = g * s
        h_ref[rows, :] = (act * u).astype(BF16)
        du_ref[rows, :] = (dh * act).astype(BF16)
        dg_ref[rows, :] = (dh * u * s * (1.0 + g * (1.0 - s))).astype(BF16)
    acc[...] += mm(dg_ref[...], wg_ref[...], NT) + mm(du_ref[...], wu_ref[...], NT)

    @pl.when(pl.program_id(0) == pl.num_programs(0) - 1)
    def _():
        dn_ref[...] = acc[...].astype(BF16)


def middle(n, dy, both, wd, given, at, parts):
    total, width = n.shape
    rows = total // parts
    hidden = both.shape[1] // 2
    tile = 256
    whole = pl.BlockSpec((rows, width), lambda j: (at, 0))
    cols = pl.BlockSpec((width, tile), lambda j: (0, j))
    more = pl.BlockSpec((width, tile), lambda j: (0, j + hidden // tile))
    outs = pl.BlockSpec((rows, tile), lambda j: (at, j))
    shape = jax.ShapeDtypeStruct((total, hidden), BF16)
    given = list(given or ())
    return pl.pallas_call(
        functools.partial(middle_body, min(rows, 256), len(given)),
        out_shape=(shape, shape, shape, jax.ShapeDtypeStruct((rows, width), BF16)),
        grid=(hidden // tile,),
        in_specs=[whole, whole, cols, more, pl.BlockSpec((tile, width), lambda j: (j, 0))]
        + [pl.BlockSpec(memory_space=pl.ANY)] * len(given),
        out_specs=(outs, outs, outs, pl.BlockSpec((rows, width), lambda j: (0, 0))),
        scratch_shapes=[pltpu.VMEM((rows, width), F32)],
        input_output_aliases={5 + k: k for k in range(len(given))},
        compiler_params=pltpu.CompilerParams(vmem_limit_bytes=24 << 20),
        cost_estimate=cost(10 * rows * width * hidden, 6 * (rows * hidden + width * hidden)),
        name="middle",
    )(n, far(dy), far(both), far(both), far(wd), *given)


def down_body(h_ref, w_ref, out_ref):
    out_ref[...] = mm(h_ref[...], w_ref[...]).astype(BF16)


def down(h, w):
    rows, hidden = h.shape
    width = w.shape[1]
    tile = min(rows, 256)
    return pl.pallas_call(
        down_body,
        out_shape=jax.ShapeDtypeStruct((rows, width), BF16),
        grid=(rows // tile,),
        in_specs=[
            pl.BlockSpec((tile, hidden), lambda j: (j, 0)),
            pl.BlockSpec((hidden, width), lambda j: (0, 0)),
        ],
        out_specs=pl.BlockSpec((tile, width), lambda j: (j, 0)),
        compiler_params=pltpu.CompilerParams(vmem_limit_bytes=24 << 20),
        cost_estimate=cost(2 * rows * width * hidden, 2 * (rows * hidden + width * hidden)),
        name="down",
    )(h, w)


def grad_body(at_ref, a_ref, z_ref, b_ref, keep_ref, give_ref):
    keep_ref[0] = mm(a_ref[...], b_ref[...], TN).astype(BF16)
    give_ref[0] = mm(z_ref[...], b_ref[...], TN).astype(BF16)


def weight_grad(a, b, parts, core):
    rows, width = a.shape
    cols = b.shape[1]
    block = width // parts
    tile = next(t for t in (2304, 1024, 512, 256, 128) if cols % t == 0)
    shape = jax.ShapeDtypeStruct((parts // 2, block, cols), BF16)
    out = pl.BlockSpec((1, block, tile), lambda j, i, c: (i, 0, j))
    return pl.pallas_call(
        grad_body,
        out_shape=(pltpu.HBM(shape.shape, BF16), pltpu.HBM(shape.shape, BF16)),
        grid_spec=pltpu.PrefetchScalarGridSpec(
            num_scalar_prefetch=1,
            grid=(cols // tile, parts // 2),
            in_specs=[
                pl.BlockSpec((rows, block), lambda j, i, c: (0, 2 * i + c[0])),
                pl.BlockSpec((rows, block), lambda j, i, c: (0, 2 * i + 1 - c[0])),
                pl.BlockSpec((rows, tile), lambda j, i, c: (0, j)),
            ],
            out_specs=(out, out),
        ),
        compiler_params=pltpu.CompilerParams(vmem_limit_bytes=24 << 20),
        cost_estimate=cost(2 * rows * width * cols, 2 * (rows * width + rows * cols + width * cols)),
        name="weight_grad",
    )(core.reshape(1), a, a, b)


def swap(x):
    n = lax.axis_size("tp")
    return lax.ppermute(x, "tp", [(i, i ^ 1) for i in range(n)])


def core_swap(x):
    n = lax.axis_size("fsdp")
    return lax.ppermute(x, "fsdp", [(i, i ^ 1) for i in range(n)])


def y_shift(x, s):
    n = lax.axis_size("fsdp")
    return lax.ppermute(x, "fsdp", [(i, (i + 2 * s) % n) for i in range(n)])


def gather_y(x):
    n = lax.axis_size("fsdp")
    y, ny = lax.axis_index("fsdp") // 2, n // 2
    mine = jnp.zeros((ny,) + x.shape, x.dtype)
    mine = lax.dynamic_update_index_in_dim(mine, x, y, 0)
    for s in range(1, ny):
        mine = lax.dynamic_update_index_in_dim(mine, y_shift(x, s), (y - s) % ny, 0)
    return mine


def gather_core(mine):
    c = lax.axis_index("fsdp") % 2
    other = core_swap(mine)
    lower = jnp.where(c == 0, mine, other)
    upper = jnp.where(c == 0, other, mine)
    return jnp.stack([lower, upper], axis=1)


def core_sums(keep, give):
    ny = keep.shape[0]
    y = lax.axis_index("fsdp") // 2
    got = core_swap(give)
    sends = [both_block(keep, got, (y + s) % ny).astype(BF16) for s in range(1, ny)]
    return keep, got, sends


def both_block(keep, got, n):
    a = lax.dynamic_index_in_dim(keep, n, 0, keepdims=False).astype(F32)
    return a + lax.dynamic_index_in_dim(got, n, 0, keepdims=False).astype(F32)


def y_sums(keep, got, sends, *after):
    parts = [y_shift(send, s + 1) for s, send in enumerate(sends)]
    keep, got, *rest = lax.optimization_barrier((keep, got, *parts, *after))
    total = both_block(keep, got, lax.axis_index("fsdp") // 2)
    for part in rest[: len(parts)]:
        total = total + part.astype(F32)
    return total.astype(BF16)


def nearest(m, i, n):
    left, right = i, n - 1 - i
    near = min(left, right)
    if m == 0:
        return 0
    if m <= 2 * near:
        return (m + 1) // 2 if m % 2 else -(m // 2)
    return m - near if right > left else -(m - near)


def choose(index, table):
    value = table[0][0]
    for array, positions in table[1:]:
        here = functools.reduce(jnp.logical_or, [index == i for i in positions])
        value = jnp.where(here, array, value)
    return value


def tie(x, *others):
    return lax.optimization_barrier((x,) + others)[0]


def tables(x):
    lane = jnp.arange(128)
    exponent = -((lane % (HD // 2)).astype(F32) * 2.0) / HD
    angle = x.astype(F32)[:, None] * (ROPE_BASE**exponent)[None, :]
    sign = jnp.where(lane % HD < HD // 2, -1.0, 1.0).astype(F32)
    return jnp.cos(angle), jnp.sin(angle) * sign[None, :]


def per_device(
    tokens, cotangent, block_order, positions,
    attn_gain, w_query, key_weight, value_weight, query_gain, key_gain,
    w_out, ffn_gain, w_gate, w_up, w_down,
):
    n_ctx = lax.axis_size("ctx")
    n_fsdp = lax.axis_size("fsdp")
    me = lax.axis_index("ctx")
    seqs, rows, width = tokens.shape
    x = tokens.reshape(seqs * rows, width)
    dy = cotangent.reshape(seqs * rows, width)
    block = rows // 2
    qw, kw = w_query.shape[1], key_weight.shape[1]
    gs, hs = attn_gain.shape[0], query_gain.shape[0]

    qkv_w = qw + 2 * kw
    small = jnp.concatenate([attn_gain, ffn_gain, query_gain, key_gain])
    small = jnp.pad(small.reshape(1, -1), ((0, 15), (0, qkv_w - 2 * (gs + hs))))
    packed = jnp.concatenate(
        [jnp.concatenate([w_query, key_weight, value_weight], axis=1), small], axis=0
    )
    mine = gather_y(packed)
    out_i = tie(w_out, packed)
    out_i = jnp.concatenate([out_i, swap(out_i)], axis=0)
    cos, sin = tables(positions.reshape(-1))
    both_i = jnp.concatenate(lax.optimization_barrier((w_gate, w_up, packed))[:2], axis=1)
    mine, out_i, cos, sin, both_i = lax.optimization_barrier((mine, out_i, cos, sin, both_i))
    both_full = lax.all_gather(both_i, "fsdp", axis=0, tiled=True)
    packed = gather_core(mine).reshape(n_fsdp, gs + 16, qkv_w)
    small = packed[:, gs].astype(F32)
    row = lambda v: jnp.broadcast_to(v.reshape(1, -1), (8, v.size))
    gain_attn = row(small[:, :gs])
    gain_ffn = row(small[:, gs : 2 * gs])
    gain_q = small[:, 2 * gs : 2 * gs + hs].reshape(-1)
    gain_k = small[:, 2 * gs + hs : 2 * (gs + hs)].reshape(-1)
    gains = jnp.stack([jnp.tile(gain_q, 2), jnp.tile(gain_k, 2)] + [jnp.zeros(128, F32)] * 6)

    step = min(256, block)
    normed_b, k_raw, kv_b = project_keys(x, gain_attn, packed, cos, sin, gains, kw, step)
    q_raw, q_b = project_queries(tie(normed_b, kv_b), packed, cos, sin, gains, qw, step)
    place = (me.astype(jnp.int32).reshape(1), block_order)
    shards = {0: kv_b}

    def shard(m):
        table = {}
        for i in range(n_ctx):
            table.setdefault(nearest(m, i, n_ctx), []).append(i)
        return choose(me, [(shards[d], where) for d, where in table.items()])

    kvs = []
    acc = None
    for t in range(1, n_ctx):
        right = [(i, i + 1) for i in range(t - 1, n_ctx - 1)]
        left = [(i, i - 1) for i in range(1, n_ctx - t + 1)]
        shards[-t] = lax.ppermute(shards[-(t - 1)], "ctx", right)
        shards[t] = lax.ppermute(shards[t - 1], "ctx", left)
        if t == 1:
            shards[-t], shards[t], q_b = lax.optimization_barrier((shards[-t], shards[t], q_b))
            out_w = lax.all_gather(tie(out_i, kv_b), "fsdp", axis=0, tiled=False)
            down_full = lax.all_gather(tie(w_down, q_b), "fsdp", axis=1, tiled=True)
            continue
        while len(kvs) < t:
            kvs.append(shard(len(kvs)))
            acc = attend(len(kvs) - 1, n_ctx, place, q_b, kvs[-1], acc, False, block)
        shards[-t], shards[t], acc = lax.optimization_barrier((shards[-t], shards[t], acc))
        if t == 2:
            acc = tie(acc, both_full)
    while len(kvs) < n_ctx - 1:
        kvs.append(shard(len(kvs)))
        acc = attend(len(kvs) - 1, n_ctx, place, q_b, kvs[-1], acc, False, block)
    m = n_ctx - 1
    kvs.append(shard(m))
    pairs = kw // 128
    mixes, others = [], []
    last_q = q_b
    for p in range(pairs):
        mixes.append(attend(m, n_ctx, place, last_q, kvs[m], acc, True, block, p))
        last_q = tie(q_b, mixes[-1][0])
        others.append(swap(mixes[-1][0]))
    mixed_b = jnp.concatenate([piece[0] for piece in mixes], axis=1)
    mix = jnp.concatenate([piece[1] for piece in mixes], axis=1)
    lse = jnp.concatenate([piece[2] for piece in mixes], axis=0)

    own = [piece[0] for piece in mixes]
    resid, two_b = join(x, gain_ffn, out_w, own, others, step)

    core = lax.axis_index("fsdp") % 2

    parts = 2
    given, d_parts, d_others = None, [], []
    two_t = two_b
    for at in range(parts):
        *given, d_part = middle(two_t, dy, both_full, down_full, given, at, parts)
        two_t = tie(two_b, d_part)
        d_parts.append(d_part)
        d_others.append(swap(d_part))
    hidden, dgate, dup = given
    down_w = weight_grad(dy, hidden, n_fsdp, core)
    two_t, hidden_t = lax.optimization_barrier((two_b, hidden, down_w, d_others[0]))[:2]
    gate_w = weight_grad(two_t, dgate, n_fsdp, core)
    up_w = weight_grad(two_t, dup, n_fsdp, core)
    down_part = down(hidden_t, down_full)
    d_others[-1], down_w, gate_w, up_w, down_part = lax.optimization_barrier(
        (d_others[-1], down_w, gate_w, up_w, down_part)
    )
    down_c, gate_c, up_c = core_sums(*down_w), core_sums(*gate_w), core_sums(*up_w)

    given, ffn_gain_g = None, 0.0
    per = rows * seqs // parts // step
    for at in range(parts):
        *given, g = into_attention(
            d_parts[at], d_others[at], resid, dy, gain_ffn, out_w, mix, given, at * per, step
        )
        ffn_gain_g = ffn_gain_g + g[0]
    d_resid, d_resid_b, do, dlt = given
    do = tie(do, *down_c[2], *gate_c[2])

    grads = [None] * n_ctx
    got = {}
    dq = None
    for m in reversed(range(n_ctx)):
        dq, grads[m] = attend_back(m, n_ctx, place, q_b, do, kvs[m], lse, dlt, dq, block)
        if m == 0:
            break
        sends = []
        for side in (1, -1):
            table = {}
            for i in range(n_ctx):
                for k in range(1, n_ctx):
                    if nearest(k, i, n_ctx) == side * m:
                        table.setdefault(k, []).append(i)
            send = choose(me, [(grads[k], where) for k, where in table.items()])
            if side in got:
                send = (send.astype(F32) + got[side].astype(F32)).astype(BF16)
            sends.append(send)
            senders = sorted(i for where in table.values() for i in where)
            got[side] = lax.ppermute(send, "ctx", [(i, i + side) for i in senders])
        if m == n_ctx - 1:
            down_other = swap(tie(down_part, dq))
            down_s = y_sums(*down_c)
            sends += [down_s] + up_c[2]
        if m == max(n_ctx - 2, 1):
            gate_s = y_sums(*gate_c, dq)
            sends.append(gate_s)
            out_g = weight_grad(tie(d_resid_b, dq), mixed_b, n_fsdp, core)
            down_s, gate_s = lax.psum((down_s, gate_s), "ctx")
        if m == 1:
            sends += [*out_g]
        dq = tie(dq, *sends)
    dq, down_other = lax.optimization_barrier((dq, down_other))
    out_s = y_sums(*core_sums(*out_g))
    home = [grads[0]] + list(got.values())
    output = (tie(resid, dq) + (down_part.astype(F32) + down_other.astype(F32))).astype(BF16)

    d_qkv, head_gain = rope_back(dq, q_raw, k_raw, cos, sin, gains, home, step)
    qkv_c = core_sums(*weight_grad(normed_b, d_qkv, n_fsdp, core))
    w_qkv = packed[:, :gs].reshape(n_fsdp * gs, qkv_w)
    normed_part = mm(d_qkv, w_qkv, NT)

    head_gain = head_gain[:2, :HD] + head_gain[:2, HD:]
    xf = x.astype(F32)
    inv_one = lax.rsqrt(jnp.mean(xf * xf, axis=-1, keepdims=True) + EPSILON)
    attn_gain_g = jnp.sum(normed_part * (xf * inv_one), axis=0)
    small_g = jnp.concatenate(
        [
            attn_gain_g.reshape(n_fsdp, gs),
            0.5 * ffn_gain_g.reshape(n_fsdp, gs),
            head_gain[0].reshape(n_fsdp, hs),
            head_gain[1].reshape(n_fsdp, hs),
        ],
        axis=1,
    )
    small_g = (small_g + swap(small_g)).astype(BF16).reshape(n_fsdp // 2, 2, 1, -1)
    normed_part = tie(normed_part.astype(BF16), small_g)
    normed_other = swap(normed_part)
    small_s = y_sums(
        *core_sums(
            lax.dynamic_index_in_dim(small_g, core, 1, keepdims=False),
            lax.dynamic_index_in_dim(small_g, 1 - core, 1, keepdims=False),
        )
    )
    last = jnp.concatenate([y_sums(*qkv_c), out_s], axis=1)
    small_s = jnp.pad(small_s, ((0, 15), (0, last.shape[1] - small_s.shape[1])))
    last = jnp.concatenate([last, small_s], axis=0)
    up_s = y_sums(*up_c)
    last, up_s, gate_s, down_s = lax.optimization_barrier((last, up_s, gate_s, down_s))
    last, up_s = lax.psum((last, up_s), "ctx")
    input_grad = leave(normed_part, normed_other, x, gain_attn, d_resid, step)
    last = tie(last, input_grad)
    q_s, k_s, v_s = last[:gs, :qw], last[:gs, qw : qw + kw], last[:gs, qw + kw : qkv_w]
    out_s = last[:gs, qkv_w:]
    small_s = last[gs : gs + 1, : 2 * (gs + hs)]
    down_s, gate_s, up_s, out_s, q_s, k_s, v_s = (
        v.astype(F32) for v in (down_s, gate_s, up_s, out_s, q_s, k_s, v_s)
    )
    small_g = small_s[0].astype(F32)
    return (
        output.reshape(tokens.shape),
        input_grad.reshape(tokens.shape),
        small_g[:gs],
        q_s,
        k_s,
        v_s,
        small_g[2 * gs : 2 * gs + hs],
        small_g[2 * gs + hs :],
        out_s.T,
        small_g[gs : 2 * gs],
        gate_s,
        up_s,
        down_s.T,
    )


def solution(mesh):
    rows = P("fsdp", "ctx", None)
    ins = P("fsdp", "tp")
    outs = P("tp", "fsdp")
    one = P("fsdp")
    return jax.shard_map(
        per_device,
        mesh=mesh,
        in_specs=(
            rows, rows, P(), P("fsdp", "ctx"), one, ins, ins, ins, one, one, outs, one, ins, ins, outs,
        ),
        out_specs=(rows, rows, one, ins, ins, ins, one, one, outs, one, ins, ins, outs),
        check_vma=False,
    )
```

```python
import functools

import jax
import jax.numpy as jnp
from jax import lax
from jax.experimental import pallas as pl
from jax.experimental.pallas import tpu as pltpu
from jax.sharding import PartitionSpec as P

HD = 64
EPSILON = 1e-05
ROPE_BASE = 1000000.0
LOG2E = 1.4426950408889634
SCALE2 = 0.125 * LOG2E
NT = (((1,), (1,)), ((), ()))
NN = (((1,), (0,)), ((), ()))
TN = (((0,), (0,)), ((), ()))
F32, BF16 = jnp.float32, jnp.bfloat16


def mm(a, b, dims=NN):
    return lax.dot_general(a, b, dims, preferred_element_type=F32)


def cost(flops, bytes_accessed):
    return pl.CostEstimate(
        flops=flops // 64, bytes_accessed=bytes_accessed // 64, transcendentals=0
    )


def far(x):
    return pltpu.with_memory_space_constraint(x, pltpu.HBM)


def half(shape, which):
    lane = lax.broadcasted_iota(jnp.int32, shape, len(shape) - 1)
    return (lane < HD) if which == 0 else (lane >= HD)


def pieces(m, n_ctx, block, where, order):
    me = where[0]

    def low(shard):
        first, second = order[2 * shard], order[2 * shard + 1]
        return jnp.minimum(first, second), jnp.where(first < second, 0, block)

    q_id, q_low = low(me)
    q_high = block - q_low
    if m == 0:
        q_low, q_high = pl.multiple_of(q_low, block), pl.multiple_of(q_high, block)
        return [(q_low, q_low, True), (q_high, q_low, False), (q_high, q_high, True)]
    left, right = me, n_ctx - 1 - me
    beyond = m - jnp.minimum(left, right)
    inner = (m + 1) // 2 if m % 2 else -(m // 2)
    outer = jnp.where(right > left, beyond, -beyond)
    far = me + jnp.where(m <= 2 * jnp.minimum(left, right), inner, outer)
    k_id, k_low = low(far)
    before = k_id < q_id
    q_first = pl.multiple_of(jnp.where(before, q_low, q_high), block)
    k_second = pl.multiple_of(jnp.where(before, k_low, block - k_low), block)
    return [
        (q_first, pl.multiple_of(k_low, block), False),
        (pl.multiple_of(q_high, block), k_second, False),
    ]


def attend_body(m, n_ctx, first, last, block, where, order, q_ref, kv_ref, *rest):
    rest = list(rest)
    given = None if first else rest.pop(0)
    if last:
        mixb_ref, mix_ref, lse_ref, acc = rest
    else:
        (acc,) = rest
    acc[...] = jnp.zeros_like(acc) if first else given[...]
    for q_at, k_at, diagonal in pieces(m, n_ctx, block, where, order):
        kt = kv_ref[pl.ds(k_at, block), 0:128]
        vt = kv_ref[pl.ds(k_at, block), 128:256]
        one = jnp.ones((block, HD), BF16)
        for hh in range(2):
            kh = kt[:, HD * hh : HD * hh + HD]
            vh = vt[:, HD * hh : HD * hh + HD]
            kd = jnp.concatenate([kh, kh], axis=1)
            vx = (jnp.concatenate([vh, one], axis=1), jnp.concatenate([one, vh], axis=1))
            qt = q_ref[pl.ds(q_at, block), 128 * hh : 128 * hh + 128]
            for r in range(2):
                qr = jnp.where(half((block, 128), r), qt, jnp.zeros_like(qt))
                p = jnp.exp2(mm(qr, kd, NT) * SCALE2)
                if diagonal:
                    row = lax.broadcasted_iota(jnp.int32, p.shape, 0)
                    col = lax.broadcasted_iota(jnp.int32, p.shape, 1)
                    p = jnp.where(col <= row, p, 0.0)
                c = 256 * hh + 128 * r
                acc[pl.ds(q_at, block), c : c + 128] += mm(p.astype(BF16), vx[r])
    if last:
        rows = acc.shape[0]
        lane = lax.broadcasted_iota(jnp.int32, (8, 128), 1)
        sub = lax.broadcasted_iota(jnp.int32, (8, 128), 0)
        total = jnp.zeros((8, rows), F32)
        for hh in range(2):
            out = []
            for r in range(2):
                a = acc[:, 256 * hh + 128 * r : 256 * hh + 128 * r + 128]
                out.append(a / pltpu.roll(a, HD, 1))
                pick = jnp.where((lane == (HD if r == 0 else 0)) & (sub == 2 * hh + r), 1.0, 0.0)
                total += lax.dot_general(
                    pick, a, NT, precision=lax.Precision.HIGHEST, preferred_element_type=F32
                )
            mix = jnp.where(half((rows, 128), 0), out[0], out[1])
            mix_ref[:, 128 * hh : 128 * hh + 128] = mix
            mixb_ref[:, 128 * hh : 128 * hh + 128] = mix.astype(BF16)
        lse_ref[0] = jnp.log2(jnp.where(sub[:, 0:1] < 4, total, 1.0))


def attend(m, n_ctx, place, q, kv, acc, last, block, at=None):
    rows = q.shape[0]
    total = kv.shape[1] // 256
    base, pairs = (0, total) if at is None else (at, 1)
    first = acc is None
    args = [*place, q, kv]
    wide = pl.BlockSpec((rows, 512), lambda g, *_: (0, g))
    slim = pl.BlockSpec((rows, 256), lambda g, *_: (0, g))
    pair = pl.BlockSpec((rows, 256), lambda g, *_: (0, g + base))
    in_specs = [pair, pair]
    if not first:
        in_specs.append(pl.BlockSpec((rows, 512), lambda g, *_: (0, g + base)))
        args.append(far(acc) if m == n_ctx - 2 else acc)
    if last:
        out_shape = (
            jax.ShapeDtypeStruct((rows, pairs * 256), BF16),
            pltpu.HBM((rows, pairs * 256), F32),
            jax.ShapeDtypeStruct((pairs, 8, rows), F32),
        )
        out_specs = (slim, slim, pl.BlockSpec((1, 8, rows), lambda g, *_: (g, 0, 0)))
        scratch = [pltpu.VMEM((rows, 512), F32)]
    else:
        out_shape = (pltpu.HBM if m > 0 else jax.ShapeDtypeStruct)((rows, pairs * 512), F32)
        out_specs = wide
        scratch = []
    work = 2 * block * block * pairs * 4
    return pl.pallas_call(
        functools.partial(attend_body, m, n_ctx, first, last, block),
        out_shape=out_shape,
        grid_spec=pltpu.PrefetchScalarGridSpec(
            num_scalar_prefetch=2,
            grid=(pairs,),
            in_specs=in_specs,
            out_specs=out_specs,
            scratch_shapes=scratch,
        ),
        compiler_params=pltpu.CompilerParams(vmem_limit_bytes=24 << 20),
        cost_estimate=cost(work * 1024, 12 << 20),
        name="attend",
    )(*args)


def attend_back_body(m, n_ctx, first, block, where, order, q_ref, do_ref, kv_ref, lse_ref, dlt_ref, *rest):
    rest = list(rest)
    given = None if first else rest.pop(0)
    dq, dkv_ref, dka, dva = rest
    dq[...] = jnp.zeros_like(dq) if first else given[...]
    dka[...] = jnp.zeros_like(dka)
    dva[...] = jnp.zeros_like(dva)
    for q_at, k_at, diagonal in pieces(m, n_ctx, block, where, order):
        kt = kv_ref[pl.ds(k_at, block), 0:128]
        vt = kv_ref[pl.ds(k_at, block), 128:256]
        zero = jnp.zeros((block, HD), BF16)
        for hh in range(2):
            kh = kt[:, HD * hh : HD * hh + HD]
            vh = vt[:, HD * hh : HD * hh + HD]
            kx = (jnp.concatenate([kh, zero], axis=1), jnp.concatenate([zero, kh], axis=1))
            vx = (jnp.concatenate([vh, zero], axis=1), jnp.concatenate([zero, vh], axis=1))
            c = 128 * hh
            qt = q_ref[pl.ds(q_at, block), c : c + 128]
            dt = do_ref[pl.ds(q_at, block), c : c + 128]
            dvs, dks, dqs = [], [], None
            for r in range(2):
                row = 2 * hh + r
                lse = lse_ref[0, row : row + 1, pl.ds(q_at, block)]
                dlt = dlt_ref[0, row : row + 1, pl.ds(q_at, block)]
                p = jnp.exp2(mm(kx[r], qt, NT) * SCALE2 - lse)
                if diagonal:
                    key = lax.broadcasted_iota(jnp.int32, p.shape, 0)
                    query = lax.broadcasted_iota(jnp.int32, p.shape, 1)
                    p = jnp.where(key <= query, p, 0.0)
                ds = (p * (mm(vx[r], dt, NT) - dlt)).astype(BF16)
                dvs.append(mm(p.astype(BF16), dt))
                dks.append(mm(ds, qt))
                term = mm(ds, kx[r], TN)
                dqs = term if dqs is None else dqs + term
            left = half((block, 128), 0)
            dva[pl.ds(k_at, block), c : c + 128] += jnp.where(left, dvs[0], dvs[1])
            dka[pl.ds(k_at, block), c : c + 128] += jnp.where(left, dks[0], dks[1])
            dq[pl.ds(q_at, block), c : c + 128] += dqs
    for at, ref, scale in ((0, dka, 0.125), (128, dva, 1.0)):
        a = ref[...]
        a = jnp.concatenate([a[:, 0:64] + a[:, 64:128], a[:, 128:192] + a[:, 192:256]], axis=1)
        dkv_ref[:, at : at + 128] = (a * scale).astype(dkv_ref.dtype)


def attend_back(m, n_ctx, place, q, do, kv, lse, dlt, dq, block):
    rows = q.shape[0]
    pairs = kv.shape[1] // 256
    first = dq is None
    slim = pl.BlockSpec((rows, 256), lambda g, *_: (0, g))
    line = pl.BlockSpec((1, 8, rows), lambda g, *_: (g, 0, 0))
    in_specs = [slim, slim, slim, line, line]
    args = [*place, q, do, kv, lse, dlt]
    if not first:
        in_specs.append(slim)
        args.append(far(dq))
    work = 2 * block * block * pairs * 4
    return pl.pallas_call(
        functools.partial(attend_back_body, m, n_ctx, first, block),
        out_shape=(
            pltpu.HBM((rows, pairs * 256), F32),
            pltpu.HBM((rows, pairs * 256), F32) if m == 0 else jax.ShapeDtypeStruct((rows, pairs * 256), BF16),
        ),
        grid_spec=pltpu.PrefetchScalarGridSpec(
            num_scalar_prefetch=2,
            grid=(pairs,),
            in_specs=in_specs,
            out_specs=(slim, slim),
            scratch_shapes=[pltpu.VMEM((rows, 256), F32), pltpu.VMEM((rows, 256), F32)],
        ),
        compiler_params=pltpu.CompilerParams(vmem_limit_bytes=24 << 20),
        cost_estimate=cost(work * 2048, 12 << 20),
        name="attend_back",
    )(*args)


def head_mean(u):
    a = lax.broadcasted_iota(jnp.int32, (128, 128), 0) // HD
    b = lax.broadcasted_iota(jnp.int32, (128, 128), 1) // HD
    ones = jnp.where(a == b, 1.0, 0.0).astype(BF16)
    high = u.astype(BF16)
    low = (u - high.astype(F32)).astype(BF16)
    return (mm(high, ones) + mm(low, ones)) * (1.0 / HD)


def turn(u):
    lane = lax.broadcasted_iota(jnp.int32, u.shape, 1)
    return jnp.where(lane % HD < HD // 2, pltpu.roll(u, 96, 1), pltpu.roll(u, 32, 1))


def rotated(u, gain, cos, sin):
    n = u * lax.rsqrt(head_mean(u * u) + EPSILON) * gain
    return (n * cos + turn(n) * sin).astype(BF16)


def row_scale(x):
    return lax.rsqrt(jnp.mean(x * x, axis=-1, keepdims=True) + EPSILON)


def blocks_product(n, w_ref):
    count = w_ref.shape[0]
    size = w_ref.shape[1] - 16
    return sum(mm(n[:, f * size : f * size + size], w_ref[f, 0:size, :]) for f in range(count))


def key_body(x_ref, g_ref, w_ref, cos_ref, sin_ref, gain_ref, n_ref, k_ref, kv_ref):
    x = x_ref[...].astype(F32)
    n = (x * row_scale(x) * g_ref[0:1]).astype(BF16)
    n_ref[...] = n
    both = blocks_product(n, w_ref)
    width = k_ref.shape[1]
    k_ref[...] = both[:, :width]
    for t in range(width // 128):
        c = 128 * t
        kv_ref[:, 2 * c : 2 * c + 128] = rotated(
            both[:, c : c + 128], gain_ref[1:2], cos_ref[...], sin_ref[...]
        )
        kv_ref[:, 2 * c + 128 : 2 * c + 256] = both[:, width + c : width + c + 128].astype(BF16)


def query_body(n_ref, w_ref, cos_ref, sin_ref, gain_ref, u_ref, q_ref):
    u = blocks_product(n_ref[...], w_ref)
    u_ref[...] = u
    for t in range(u.shape[1] // 128):
        c = slice(128 * t, 128 * t + 128)
        q_ref[:, c] = rotated(u[:, c], gain_ref[0:1], cos_ref[...], sin_ref[...])


def row_call(body, name, step, rows, ins, outs, flops, scratch=(), aliases=None, first=0, count=None):
    ins = list(ins)
    spec = lambda w: pl.BlockSpec((step, w), lambda i: (i + first, 0))
    in_specs = []
    for n, (array, kind) in enumerate(ins):
        if isinstance(kind, str) and kind.startswith("far "):
            kind = kind[4:]
            ins[n] = (far(array), kind)
        if kind == "rows":
            in_specs.append(spec(array.shape[1]))
        elif kind == "part":
            in_specs.append(pl.BlockSpec((step, array.shape[1]), lambda i: (i, 0)))
        elif kind == "whole":
            in_specs.append(pl.BlockSpec(array.shape, lambda i, n=array.ndim: (0,) * n))
        else:
            in_specs.append(kind)
    return pl.pallas_call(
        body,
        out_shape=tuple(pltpu.HBM(o[0].shape, o[0].dtype) if len(o) > 2 else o[0] for o in outs),
        grid=(rows // step if count is None else count,),
        in_specs=in_specs,
        out_specs=tuple(spec(o[0].shape[1]) if o[1] is None else o[1] for o in outs),
        scratch_shapes=list(scratch),
        input_output_aliases=aliases or {},
        compiler_params=pltpu.CompilerParams(vmem_limit_bytes=24 << 20),
        cost_estimate=cost(flops, 1 << 20),
        name=name,
    )(*(array for array, _ in ins))


def project_keys(x, gain, packed, cos, sin, gains, kw, step):
    rows, width = x.shape
    f, r, cols = packed.shape
    shape = lambda w, t: (jax.ShapeDtypeStruct((rows, w), t), None)
    part = pl.BlockSpec((f, r, 2 * kw), lambda i: (0, 0, cols // (2 * kw) - 1))
    return row_call(
        key_body, "project_keys", step, rows,
        [(x, "far rows"), (gain, "whole"), (packed, part), (cos, "far rows"), (sin, "far rows"), (gains, "whole")],
        [shape(width, BF16) + ("far",), shape(kw, F32) + ("far",), shape(2 * kw, BF16) + ("far",)],
        rows * width * kw * 4,
    )


def project_queries(n, packed, cos, sin, gains, qw, step):
    rows, width = n.shape
    f, r, _ = packed.shape
    shape = lambda w, t: (jax.ShapeDtypeStruct((rows, w), t), None)
    part = pl.BlockSpec((f, r, qw), lambda i: (0, 0, 0))
    return row_call(
        query_body, "project_queries", step, rows,
        [(n, "far rows"), (packed, part), (cos, "far rows"), (sin, "far rows"), (gains, "whole")],
        [shape(qw, F32) + ("far",), shape(qw, BF16)],
        rows * width * qw * 2,
    )


def pair_product(own, other, w_ref, at):
    size = own.shape[1]
    base = w_ref.shape[1] // 2
    return jnp.concatenate(
        [
            mm(own, w_ref[f, at * size : at * size + size, :])
            + mm(other, w_ref[f, base + at * size : base + at * size + size, :])
            for f in range(w_ref.shape[0])
        ],
        axis=1,
    )


def join_body(at, own_ref, other_ref, w_ref, *refs):
    term = pair_product(own_ref[...], other_ref[...], w_ref, at)
    refs[-1][...] = term if len(refs) == 1 else refs[0][...] + term


def join_last_body(at, own_ref, other_ref, w_ref, x_ref, g_ref, *refs):
    r_ref, n_ref = refs[-2:]
    term = pair_product(own_ref[...], other_ref[...], w_ref, at)
    if len(refs) == 3:
        term = refs[0][...] + term
    r = x_ref[...].astype(F32) + term
    r_ref[...] = r
    n_ref[...] = (r * row_scale(r) * g_ref[0:1]).astype(BF16)


def join(x, gain, w, own, others, step):
    rows, width = x.shape
    shape = lambda w, t: (jax.ShapeDtypeStruct((rows, w), t), None)
    flops = rows * width * width
    so_far = []
    for at, (mine, other) in enumerate(zip(own, others)):
        ins = [(mine, "rows"), (other, "far rows"), (w, "whole")]
        held = [(v, "rows") for v in so_far]
        if at < len(own) - 1:
            so_far = row_call(
                functools.partial(join_body, at), "join", step, rows, ins + held, [shape(width, F32)], flops
            )
    return row_call(
        functools.partial(join_last_body, at), "join_last", step, rows,
        ins + [(x, "far rows"), (gain, "whole")] + held,
        [shape(width, F32) + ("far",), shape(width, BF16)],
        flops,
    )


def into_body(pairs, aliased, a_ref, b_ref, r_ref, dy_ref, g_ref, w_ref, mix_ref, *refs):
    d_ref, db_ref, do_ref, dlt_ref, gg_ref = refs[aliased:]
    gain = g_ref[0:1]
    r = r_ref[...]
    scale = row_scale(r)
    d = a_ref[...].astype(F32) + b_ref[...].astype(F32)
    scaled = d * gain
    back = scale * scaled - r * (scale * scale * scale) * jnp.mean(r * scaled, axis=-1, keepdims=True)

    @pl.when(pl.program_id(0) == 0)
    def _():
        gg_ref[...] = jnp.zeros_like(gg_ref)

    gg_ref[0:1] += jnp.sum(d * r * scale, axis=0, keepdims=True)
    out = dy_ref[...].astype(F32) + back
    d_ref[...] = out
    out = out.astype(BF16)
    db_ref[...] = out
    size = w_ref.shape[2]
    do = sum(mm(out[:, f * size : f * size + size], w_ref[f], NT) for f in range(w_ref.shape[0]))
    do = do.astype(BF16)
    do_ref[...] = do
    lane = lax.broadcasted_iota(jnp.int32, (8, 128), 1) // HD
    sub = lax.broadcasted_iota(jnp.int32, (8, 128), 0)
    for p in range(pairs):
        total = jnp.zeros((8, r.shape[0]), F32)
        for hh in range(2):
            c = slice(256 * p + 128 * hh, 256 * p + 128 * hh + 128)
            x = do[:, c].astype(F32) * mix_ref[:, c]
            total += lax.dot_general(
                jnp.where(sub == 2 * hh + lane, 1.0, 0.0), x, NT,
                precision=lax.Precision.HIGHEST, preferred_element_type=F32,
            )
        dlt_ref[p] = total


def into_attention(a, b, resid, dy, gain, w, mix, given, first, step):
    rows, width = resid.shape
    wide = w.shape[1] // 2
    pairs = wide // 256
    own_w = pl.BlockSpec((w.shape[0], wide, w.shape[2]), lambda i: (0, 0, 0))
    shape = lambda w, t: (jax.ShapeDtypeStruct((rows, w), t), None)
    hbm = pl.BlockSpec(memory_space=pl.ANY)
    base = [(a, "far part"), (b, "far part"), (resid, "far rows"), (dy, "far rows"), (gain, "whole"), (w, own_w), (mix, "far rows")]
    given = list(given or ())
    return row_call(
        functools.partial(into_body, pairs, len(given)), "into_attention", step, rows,
        base + [(g, hbm) for g in given],
        [
            shape(width, F32) + ("far",), shape(width, BF16) + ("far",), shape(wide, BF16),
            (jax.ShapeDtypeStruct((pairs, 8, rows), F32), pl.BlockSpec((pairs, 8, step), lambda i: (0, 0, i + first))),
            (jax.ShapeDtypeStruct((8, width), F32), pl.BlockSpec((8, width), lambda i: (0, 0))),
        ],
        rows * width * wide,
        aliases={len(base) + k: k for k in range(len(given))},
        first=first, count=a.shape[0] // step,
    )


def leave_body(a_ref, b_ref, x_ref, g_ref, d_ref, out_ref):
    x = x_ref[...].astype(F32)
    scale = row_scale(x)
    scaled = (a_ref[...].astype(F32) + b_ref[...].astype(F32)) * g_ref[0:1]
    back = scale * scaled - x * (scale * scale * scale) * jnp.mean(x * scaled, axis=-1, keepdims=True)
    out_ref[...] = d_ref[...] + back


def leave(a, b, x, gain, d, step):
    rows, width = x.shape
    return row_call(
        leave_body, "leave", step, rows,
        [(a, "far rows"), (b, "far rows"), (x, "far rows"), (gain, "whole"), (d, "far rows")],
        [(jax.ShapeDtypeStruct((rows, width), F32), None)],
        rows * width * 16,
    )[0]


def rope_back_body(terms, dq_ref, q_ref, k_ref, cos_ref, sin_ref, gain_ref, *rest):
    dkv_refs, (out_ref, gg_ref) = rest[:terms], rest[terms:]
    cos, sin = cos_ref[...], sin_ref[...]

    @pl.when(pl.program_id(0) == 0)
    def _():
        gg_ref[...] = jnp.zeros_like(gg_ref)

    def one(d, u, row):
        gain = gain_ref[row : row + 1]
        dn = d * cos + turn(d * sin)
        r = lax.rsqrt(head_mean(u * u) + EPSILON)
        gd = gain * dn
        gg_ref[row : row + 1] += jnp.sum(dn * u * r, axis=0, keepdims=True)
        return (r * gd - u * (r * r * r) * head_mean(u * gd)).astype(BF16)

    qw, kw = q_ref.shape[1], k_ref.shape[1]
    for t in range(qw // 128):
        c = slice(128 * t, 128 * t + 128)
        out_ref[:, c] = one(dq_ref[:, c] * 0.125, q_ref[:, c], 0)
    for t in range(kw // 128):
        dk = sum(ref[:, 256 * t : 256 * t + 128].astype(F32) for ref in dkv_refs)
        dv = sum(ref[:, 256 * t + 128 : 256 * t + 256].astype(F32) for ref in dkv_refs)
        out_ref[:, qw + 128 * t : qw + 128 * t + 128] = one(dk, k_ref[:, 128 * t : 128 * t + 128], 1)
        out_ref[:, qw + kw + 128 * t : qw + kw + 128 * t + 128] = dv.astype(BF16)


def rope_back(dq, q_raw, k_raw, cos, sin, gains, dkvs, step):
    rows, qw = q_raw.shape
    kw = k_raw.shape[1]
    spec = lambda w: pl.BlockSpec((step, w), lambda i: (i, 0))
    fixed = pl.BlockSpec((8, 128), lambda i: (0, 0))
    return pl.pallas_call(
        functools.partial(rope_back_body, len(dkvs)),
        out_shape=(
            jax.ShapeDtypeStruct((rows, qw + 2 * kw), BF16),
            jax.ShapeDtypeStruct((8, 128), F32),
        ),
        grid=(rows // step,),
        in_specs=[spec(qw), spec(qw), spec(kw), spec(128), spec(128), fixed]
        + [spec(2 * kw)] * len(dkvs),
        out_specs=(spec(qw + 2 * kw), fixed),
        compiler_params=pltpu.CompilerParams(vmem_limit_bytes=24 << 20),
        cost_estimate=cost(rows * qw * 1600, rows * qw * 20),
        name="rope_back",
    )(*map(far, (dq, q_raw, k_raw, cos, sin)), gains, far(dkvs[0]), *dkvs[1:])


def middle_body(step, aliased, n_ref, dy_ref, wg_ref, wu_ref, wd_ref, *refs):
    h_ref, dg_ref, du_ref, dn_ref, acc = refs[aliased:]

    @pl.when(pl.program_id(0) == 0)
    def _():
        acc[...] = jnp.zeros_like(acc)

    for at in range(0, n_ref.shape[0], step):
        rows = pl.ds(at, step)
        n = n_ref[rows, :]
        g = mm(n, wg_ref[...])
        u = mm(n, wu_ref[...])
        dh = mm(dy_ref[rows, :], wd_ref[...], NT)
        s = 1.0 / (1.0 + jnp.exp2(g * (-LOG2E)))
        act = g * s
        h_ref[rows, :] = (act * u).astype(BF16)
        du_ref[rows, :] = (dh * act).astype(BF16)
        dg_ref[rows, :] = (dh * u * s * (1.0 + g * (1.0 - s))).astype(BF16)
    acc[...] += mm(dg_ref[...], wg_ref[...], NT) + mm(du_ref[...], wu_ref[...], NT)

    @pl.when(pl.program_id(0) == pl.num_programs(0) - 1)
    def _():
        dn_ref[...] = acc[...].astype(BF16)


def middle(n, dy, both, wd, given, at, parts):
    total, width = n.shape
    rows = total // parts
    hidden = both.shape[1] // 2
    tile = 256
    whole = pl.BlockSpec((rows, width), lambda j: (at, 0))
    cols = pl.BlockSpec((width, tile), lambda j: (0, j))
    more = pl.BlockSpec((width, tile), lambda j: (0, j + hidden // tile))
    outs = pl.BlockSpec((rows, tile), lambda j: (at, j))
    shape = jax.ShapeDtypeStruct((total, hidden), BF16)
    given = list(given or ())
    return pl.pallas_call(
        functools.partial(middle_body, min(rows, 256), len(given)),
        out_shape=(shape, shape, shape, jax.ShapeDtypeStruct((rows, width), BF16)),
        grid=(hidden // tile,),
        in_specs=[whole, whole, cols, more, pl.BlockSpec((tile, width), lambda j: (j, 0))]
        + [pl.BlockSpec(memory_space=pl.ANY)] * len(given),
        out_specs=(outs, outs, outs, pl.BlockSpec((rows, width), lambda j: (0, 0))),
        scratch_shapes=[pltpu.VMEM((rows, width), F32)],
        input_output_aliases={5 + k: k for k in range(len(given))},
        compiler_params=pltpu.CompilerParams(vmem_limit_bytes=24 << 20),
        cost_estimate=cost(10 * rows * width * hidden, 6 * (rows * hidden + width * hidden)),
        name="middle",
    )(n, far(dy), far(both), far(both), far(wd), *given)


def down_body(h_ref, w_ref, out_ref):
    out_ref[...] = mm(h_ref[...], w_ref[...]).astype(BF16)


def down(h, w):
    rows, hidden = h.shape
    width = w.shape[1]
    tile = min(rows, 256)
    return pl.pallas_call(
        down_body,
        out_shape=jax.ShapeDtypeStruct((rows, width), BF16),
        grid=(rows // tile,),
        in_specs=[
            pl.BlockSpec((tile, hidden), lambda j: (j, 0)),
            pl.BlockSpec((hidden, width), lambda j: (0, 0)),
        ],
        out_specs=pl.BlockSpec((tile, width), lambda j: (j, 0)),
        compiler_params=pltpu.CompilerParams(vmem_limit_bytes=24 << 20),
        cost_estimate=cost(2 * rows * width * hidden, 2 * (rows * hidden + width * hidden)),
        name="down",
    )(h, w)


def grad_body(at_ref, a_ref, z_ref, b_ref, keep_ref, give_ref):
    keep_ref[0] = mm(a_ref[...], b_ref[...], TN).astype(BF16)
    give_ref[0] = mm(z_ref[...], b_ref[...], TN).astype(BF16)


def weight_grad(a, b, parts, core):
    rows, width = a.shape
    cols = b.shape[1]
    block = width // parts
    tile = next(t for t in (2304, 1024, 512, 256, 128) if cols % t == 0)
    shape = jax.ShapeDtypeStruct((parts // 2, block, cols), BF16)
    out = pl.BlockSpec((1, block, tile), lambda j, i, c: (i, 0, j))
    return pl.pallas_call(
        grad_body,
        out_shape=(pltpu.HBM(shape.shape, BF16), pltpu.HBM(shape.shape, BF16)),
        grid_spec=pltpu.PrefetchScalarGridSpec(
            num_scalar_prefetch=1,
            grid=(cols // tile, parts // 2),
            in_specs=[
                pl.BlockSpec((rows, block), lambda j, i, c: (0, 2 * i + c[0])),
                pl.BlockSpec((rows, block), lambda j, i, c: (0, 2 * i + 1 - c[0])),
                pl.BlockSpec((rows, tile), lambda j, i, c: (0, j)),
            ],
            out_specs=(out, out),
        ),
        compiler_params=pltpu.CompilerParams(vmem_limit_bytes=24 << 20),
        cost_estimate=cost(2 * rows * width * cols, 2 * (rows * width + rows * cols + width * cols)),
        name="weight_grad",
    )(core.reshape(1), a, a, b)


def swap(x):
    n = lax.axis_size("tp")
    return lax.ppermute(x, "tp", [(i, i ^ 1) for i in range(n)])


def core_swap(x):
    n = lax.axis_size("fsdp")
    return lax.ppermute(x, "fsdp", [(i, i ^ 1) for i in range(n)])


def y_shift(x, s):
    n = lax.axis_size("fsdp")
    return lax.ppermute(x, "fsdp", [(i, (i + 2 * s) % n) for i in range(n)])


def gather_y(x):
    n = lax.axis_size("fsdp")
    y, ny = lax.axis_index("fsdp") // 2, n // 2
    mine = jnp.zeros((ny,) + x.shape, x.dtype)
    mine = lax.dynamic_update_index_in_dim(mine, x, y, 0)
    for s in range(1, ny):
        mine = lax.dynamic_update_index_in_dim(mine, y_shift(x, s), (y - s) % ny, 0)
    return mine


def gather_core(mine):
    c = lax.axis_index("fsdp") % 2
    other = core_swap(mine)
    lower = jnp.where(c == 0, mine, other)
    upper = jnp.where(c == 0, other, mine)
    return jnp.stack([lower, upper], axis=1)


def core_sums(keep, give):
    ny = keep.shape[0]
    y = lax.axis_index("fsdp") // 2
    got = core_swap(give)
    sends = [both_block(keep, got, (y + s) % ny).astype(BF16) for s in range(1, ny)]
    return keep, got, sends


def both_block(keep, got, n):
    a = lax.dynamic_index_in_dim(keep, n, 0, keepdims=False).astype(F32)
    return a + lax.dynamic_index_in_dim(got, n, 0, keepdims=False).astype(F32)


def y_sums(keep, got, sends, *after):
    parts = [y_shift(send, s + 1) for s, send in enumerate(sends)]
    keep, got, *rest = lax.optimization_barrier((keep, got, *parts, *after))
    total = both_block(keep, got, lax.axis_index("fsdp") // 2)
    for part in rest[: len(parts)]:
        total = total + part.astype(F32)
    return total.astype(BF16)


def nearest(m, i, n):
    left, right = i, n - 1 - i
    near = min(left, right)
    if m == 0:
        return 0
    if m <= 2 * near:
        return (m + 1) // 2 if m % 2 else -(m // 2)
    return m - near if right > left else -(m - near)


def choose(index, table):
    value = table[0][0]
    for array, positions in table[1:]:
        here = functools.reduce(jnp.logical_or, [index == i for i in positions])
        value = jnp.where(here, array, value)
    return value


def tie(x, *others):
    return lax.optimization_barrier((x,) + others)[0]


def tables(x):
    lane = jnp.arange(128)
    exponent = -((lane % (HD // 2)).astype(F32) * 2.0) / HD
    angle = x.astype(F32)[:, None] * (ROPE_BASE**exponent)[None, :]
    sign = jnp.where(lane % HD < HD // 2, -1.0, 1.0).astype(F32)
    return jnp.cos(angle), jnp.sin(angle) * sign[None, :]


def per_device(
    tokens, cotangent, block_order, positions,
    attn_gain, w_query, key_weight, value_weight, query_gain, key_gain,
    w_out, ffn_gain, w_gate, w_up, w_down,
):
    n_ctx = lax.axis_size("ctx")
    n_fsdp = lax.axis_size("fsdp")
    me = lax.axis_index("ctx")
    seqs, rows, width = tokens.shape
    x = tokens.reshape(seqs * rows, width)
    dy = cotangent.reshape(seqs * rows, width)
    block = rows // 2
    qw, kw = w_query.shape[1], key_weight.shape[1]
    gs, hs = attn_gain.shape[0], query_gain.shape[0]

    qkv_w = qw + 2 * kw
    small = jnp.concatenate([attn_gain, ffn_gain, query_gain, key_gain])
    small = jnp.pad(small.reshape(1, -1), ((0, 15), (0, qkv_w - 2 * (gs + hs))))
    packed = jnp.concatenate(
        [jnp.concatenate([w_query, key_weight, value_weight], axis=1), small], axis=0
    )
    mine = gather_y(packed)
    out_i = tie(w_out, packed)
    out_i = jnp.concatenate([out_i, swap(out_i)], axis=0)
    cos, sin = tables(positions.reshape(-1))
    both_i = jnp.concatenate(lax.optimization_barrier((w_gate, w_up, packed))[:2], axis=1)
    mine, out_i, cos, sin, both_i = lax.optimization_barrier((mine, out_i, cos, sin, both_i))
    both_full = lax.all_gather(both_i, "fsdp", axis=0, tiled=True)
    packed = gather_core(mine).reshape(n_fsdp, gs + 16, qkv_w)
    small = packed[:, gs].astype(F32)
    row = lambda v: jnp.broadcast_to(v.reshape(1, -1), (8, v.size))
    gain_attn = row(small[:, :gs])
    gain_ffn = row(small[:, gs : 2 * gs])
    gain_q = small[:, 2 * gs : 2 * gs + hs].reshape(-1)
    gain_k = small[:, 2 * gs + hs : 2 * (gs + hs)].reshape(-1)
    gains = jnp.stack([jnp.tile(gain_q, 2), jnp.tile(gain_k, 2)] + [jnp.zeros(128, F32)] * 6)

    step = min(256, block)
    normed_b, k_raw, kv_b = project_keys(x, gain_attn, packed, cos, sin, gains, kw, step)
    q_raw, q_b = project_queries(tie(normed_b, kv_b), packed, cos, sin, gains, qw, step)
    place = (me.astype(jnp.int32).reshape(1), block_order)
    shards = {0: kv_b}

    def shard(m):
        table = {}
        for i in range(n_ctx):
            table.setdefault(nearest(m, i, n_ctx), []).append(i)
        return choose(me, [(shards[d], where) for d, where in table.items()])

    kvs = []
    acc = None
    for t in range(1, n_ctx):
        right = [(i, i + 1) for i in range(t - 1, n_ctx - 1)]
        left = [(i, i - 1) for i in range(1, n_ctx - t + 1)]
        shards[-t] = lax.ppermute(shards[-(t - 1)], "ctx", right)
        shards[t] = lax.ppermute(shards[t - 1], "ctx", left)
        if t == 1:
            shards[-t], shards[t], q_b = lax.optimization_barrier((shards[-t], shards[t], q_b))
            out_w = lax.all_gather(tie(out_i, kv_b), "fsdp", axis=0, tiled=False)
            down_full = lax.all_gather(tie(w_down, q_b), "fsdp", axis=1, tiled=True)
            continue
        while len(kvs) < t:
            kvs.append(shard(len(kvs)))
            acc = attend(len(kvs) - 1, n_ctx, place, q_b, kvs[-1], acc, False, block)
        shards[-t], shards[t], acc = lax.optimization_barrier((shards[-t], shards[t], acc))
        if t == 2:
            acc = tie(acc, both_full)
    while len(kvs) < n_ctx - 1:
        kvs.append(shard(len(kvs)))
        acc = attend(len(kvs) - 1, n_ctx, place, q_b, kvs[-1], acc, False, block)
    m = n_ctx - 1
    kvs.append(shard(m))
    pairs = kw // 128
    mixes, others = [], []
    last_q = q_b
    for p in range(pairs):
        mixes.append(attend(m, n_ctx, place, last_q, kvs[m], acc, True, block, p))
        last_q = tie(q_b, mixes[-1][0])
        others.append(swap(mixes[-1][0]))
    mixed_b = jnp.concatenate([piece[0] for piece in mixes], axis=1)
    mix = jnp.concatenate([piece[1] for piece in mixes], axis=1)
    lse = jnp.concatenate([piece[2] for piece in mixes], axis=0)

    own = [piece[0] for piece in mixes]
    resid, two_b = join(x, gain_ffn, out_w, own, others, step)

    core = lax.axis_index("fsdp") % 2

    parts = 2
    given, d_parts, d_others = None, [], []
    two_t = two_b
    for at in range(parts):
        *given, d_part = middle(two_t, dy, both_full, down_full, given, at, parts)
        two_t = tie(two_b, d_part)
        d_parts.append(d_part)
        d_others.append(swap(d_part))
    hidden, dgate, dup = given
    down_w = weight_grad(dy, hidden, n_fsdp, core)
    two_t, hidden_t = lax.optimization_barrier((two_b, hidden, down_w, d_others[0]))[:2]
    gate_w = weight_grad(two_t, dgate, n_fsdp, core)
    up_w = weight_grad(two_t, dup, n_fsdp, core)
    down_part = down(hidden_t, down_full)
    d_others[-1], down_w, gate_w, up_w, down_part = lax.optimization_barrier(
        (d_others[-1], down_w, gate_w, up_w, down_part)
    )
    down_c, gate_c, up_c = core_sums(*down_w), core_sums(*gate_w), core_sums(*up_w)

    given, ffn_gain_g = None, 0.0
    per = rows * seqs // parts // step
    for at in range(parts):
        *given, g = into_attention(
            d_parts[at], d_others[at], resid, dy, gain_ffn, out_w, mix, given, at * per, step
        )
        ffn_gain_g = ffn_gain_g + g[0]
    d_resid, d_resid_b, do, dlt = given
    do = tie(do, *down_c[2], *gate_c[2])

    grads = [None] * n_ctx
    got = {}
    dq = None
    for m in reversed(range(n_ctx)):
        dq, grads[m] = attend_back(m, n_ctx, place, q_b, do, kvs[m], lse, dlt, dq, block)
        if m == 0:
            break
        sends = []
        for side in (1, -1):
            table = {}
            for i in range(n_ctx):
                for k in range(1, n_ctx):
                    if nearest(k, i, n_ctx) == side * m:
                        table.setdefault(k, []).append(i)
            send = choose(me, [(grads[k], where) for k, where in table.items()])
            if side in got:
                send = (send.astype(F32) + got[side].astype(F32)).astype(BF16)
            sends.append(send)
            senders = sorted(i for where in table.values() for i in where)
            got[side] = lax.ppermute(send, "ctx", [(i, i + side) for i in senders])
        if m == n_ctx - 1:
            down_other = swap(tie(down_part, dq))
            down_s = y_sums(*down_c)
            sends += [down_s] + up_c[2]
        if m == max(n_ctx - 2, 1):
            gate_s = y_sums(*gate_c, dq)
            sends.append(gate_s)
            out_g = weight_grad(tie(d_resid_b, dq), mixed_b, n_fsdp, core)
            down_s, gate_s = lax.psum((down_s, gate_s), "ctx")
        if m == 1:
            sends += [*out_g]
        dq = tie(dq, *sends)
    dq, down_other = lax.optimization_barrier((dq, down_other))
    out_s = y_sums(*core_sums(*out_g))
    home = [grads[0]] + list(got.values())
    output = (tie(resid, dq) + (down_part.astype(F32) + down_other.astype(F32))).astype(BF16)

    d_qkv, head_gain = rope_back(dq, q_raw, k_raw, cos, sin, gains, home, step)
    qkv_p = weight_grad(normed_b, d_qkv, n_fsdp, core)
    qkv_c = core_sums(*lax.optimization_barrier((*qkv_p, gate_s))[:2])
    w_qkv = packed[:, :gs].reshape(n_fsdp * gs, qkv_w)
    normed_part = mm(d_qkv, w_qkv, NT)

    head_gain = head_gain[:2, :HD] + head_gain[:2, HD:]
    xf = x.astype(F32)
    inv_one = lax.rsqrt(jnp.mean(xf * xf, axis=-1, keepdims=True) + EPSILON)
    attn_gain_g = jnp.sum(normed_part * (xf * inv_one), axis=0)
    small_g = jnp.concatenate(
        [
            attn_gain_g.reshape(n_fsdp, gs),
            0.5 * ffn_gain_g.reshape(n_fsdp, gs),
            head_gain[0].reshape(n_fsdp, hs),
            head_gain[1].reshape(n_fsdp, hs),
        ],
        axis=1,
    )
    small_g = (small_g + swap(small_g)).astype(BF16).reshape(n_fsdp // 2, 2, 1, -1)
    normed_part = tie(normed_part.astype(BF16), small_g)
    normed_other = swap(normed_part)
    small_s = y_sums(
        *core_sums(
            lax.dynamic_index_in_dim(small_g, core, 1, keepdims=False),
            lax.dynamic_index_in_dim(small_g, 1 - core, 1, keepdims=False),
        )
    )
    last = jnp.concatenate([y_sums(*qkv_c), out_s], axis=1)
    small_s = jnp.pad(small_s, ((0, 15), (0, last.shape[1] - small_s.shape[1])))
    last = jnp.concatenate([last, small_s], axis=0)
    up_s = y_sums(*up_c)
    last, up_s, gate_s, down_s = lax.optimization_barrier((last, up_s, gate_s, down_s))
    last, up_s = lax.psum((last, up_s), "ctx")
    input_grad = leave(normed_part, normed_other, x, gain_attn, d_resid, step)
    last = tie(last, input_grad)
    q_s, k_s, v_s = last[:gs, :qw], last[:gs, qw : qw + kw], last[:gs, qw + kw : qkv_w]
    out_s = last[:gs, qkv_w:]
    small_s = last[gs : gs + 1, : 2 * (gs + hs)]
    down_s, gate_s, up_s, out_s, q_s, k_s, v_s = (
        v.astype(F32) for v in (down_s, gate_s, up_s, out_s, q_s, k_s, v_s)
    )
    small_g = small_s[0].astype(F32)
    return (
        output.reshape(tokens.shape),
        input_grad.reshape(tokens.shape),
        small_g[:gs],
        q_s,
        k_s,
        v_s,
        small_g[2 * gs : 2 * gs + hs],
        small_g[2 * gs + hs :],
        out_s.T,
        small_g[gs : 2 * gs],
        gate_s,
        up_s,
        down_s.T,
    )


def solution(mesh):
    rows = P("fsdp", "ctx", None)
    ins = P("fsdp", "tp")
    outs = P("tp", "fsdp")
    one = P("fsdp")
    return jax.shard_map(
        per_device,
        mesh=mesh,
        in_specs=(
            rows, rows, P(), P("fsdp", "ctx"), one, ins, ins, ins, one, one, outs, one, ins, ins, outs,
        ),
        out_specs=(rows, rows, one, ins, ins, ins, one, one, outs, one, ins, ins, outs),
        check_vma=False,
    )
```

```python
import functools

import jax
import jax.numpy as jnp
from jax import lax
from jax.experimental import pallas as pl
from jax.experimental.pallas import tpu as pltpu
from jax.sharding import PartitionSpec as P

HD = 64
EPSILON = 1e-05
ROPE_BASE = 1000000.0
LOG2E = 1.4426950408889634
SCALE2 = 0.125 * LOG2E
NT = (((1,), (1,)), ((), ()))
NN = (((1,), (0,)), ((), ()))
TN = (((0,), (0,)), ((), ()))
F32, BF16 = jnp.float32, jnp.bfloat16


def mm(a, b, dims=NN):
    return lax.dot_general(a, b, dims, preferred_element_type=F32)


def cost(flops, bytes_accessed):
    return pl.CostEstimate(
        flops=flops // 64, bytes_accessed=bytes_accessed // 64, transcendentals=0
    )


def far(x):
    return pltpu.with_memory_space_constraint(x, pltpu.HBM)


def half(shape, which):
    lane = lax.broadcasted_iota(jnp.int32, shape, len(shape) - 1)
    return (lane < HD) if which == 0 else (lane >= HD)


def row_sums(pick, x):
    pick, high = pick.astype(BF16), x.astype(BF16)
    return mm(pick, high, NT) + mm(pick, (x - high.astype(F32)).astype(BF16), NT)


def pieces(m, n_ctx, block, where, order):
    me = where[0]

    def low(shard):
        first, second = order[2 * shard], order[2 * shard + 1]
        return jnp.minimum(first, second), jnp.where(first < second, 0, block)

    q_id, q_low = low(me)
    q_high = block - q_low
    if m == 0:
        q_low, q_high = pl.multiple_of(q_low, block), pl.multiple_of(q_high, block)
        return [(q_low, q_low, True), (q_high, q_low, False), (q_high, q_high, True)]
    left, right = me, n_ctx - 1 - me
    beyond = m - jnp.minimum(left, right)
    inner = (m + 1) // 2 if m % 2 else -(m // 2)
    outer = jnp.where(right > left, beyond, -beyond)
    far = me + jnp.where(m <= 2 * jnp.minimum(left, right), inner, outer)
    k_id, k_low = low(far)
    before = k_id < q_id
    q_first = pl.multiple_of(jnp.where(before, q_low, q_high), block)
    k_second = pl.multiple_of(jnp.where(before, k_low, block - k_low), block)
    return [
        (q_first, pl.multiple_of(k_low, block), False),
        (pl.multiple_of(q_high, block), k_second, False),
    ]


def attend_body(m, n_ctx, first, last, block, where, order, q_ref, kv_ref, *rest):
    rest = list(rest)
    given = None if first else rest.pop(0)
    if last:
        mixb_ref, mix_ref, lse_ref, acc = rest
    else:
        (acc,) = rest
    acc[...] = jnp.zeros_like(acc) if first else given[...]
    for q_at, k_at, diagonal in pieces(m, n_ctx, block, where, order):
        kt = kv_ref[pl.ds(k_at, block), 0:128]
        vt = kv_ref[pl.ds(k_at, block), 128:256]
        one = jnp.ones((block, HD), BF16)
        for hh in range(2):
            kh = kt[:, HD * hh : HD * hh + HD]
            vh = vt[:, HD * hh : HD * hh + HD]
            kd = jnp.concatenate([kh, kh], axis=1)
            vx = (jnp.concatenate([vh, one], axis=1), jnp.concatenate([one, vh], axis=1))
            qt = q_ref[pl.ds(q_at, block), 128 * hh : 128 * hh + 128]
            for r in range(2):
                qr = jnp.where(half((block, 128), r), qt, jnp.zeros_like(qt))
                p = jnp.exp2(mm(qr, kd, NT) * SCALE2)
                if diagonal:
                    row = lax.broadcasted_iota(jnp.int32, p.shape, 0)
                    col = lax.broadcasted_iota(jnp.int32, p.shape, 1)
                    p = jnp.where(col <= row, p, 0.0)
                c = 256 * hh + 128 * r
                acc[pl.ds(q_at, block), c : c + 128] += mm(p.astype(BF16), vx[r])
    if last:
        rows = acc.shape[0]
        lane = lax.broadcasted_iota(jnp.int32, (8, 128), 1)
        sub = lax.broadcasted_iota(jnp.int32, (8, 128), 0)
        total = jnp.zeros((8, rows), F32)
        for hh in range(2):
            out = []
            for r in range(2):
                a = acc[:, 256 * hh + 128 * r : 256 * hh + 128 * r + 128]
                out.append(a / pltpu.roll(a, HD, 1))
                pick = jnp.where((lane == (HD if r == 0 else 0)) & (sub == 2 * hh + r), 1.0, 0.0)
                total += row_sums(pick, a)
            mix = jnp.where(half((rows, 128), 0), out[0], out[1])
            mix_ref[:, 128 * hh : 128 * hh + 128] = mix
            mixb_ref[:, 128 * hh : 128 * hh + 128] = mix.astype(BF16)
        lse_ref[0] = jnp.log2(jnp.where(sub[:, 0:1] < 4, total, 1.0))


def attend(m, n_ctx, place, q, kv, acc, last, block, at=None):
    rows = q.shape[0]
    total = kv.shape[1] // 256
    base, pairs = (0, total) if at is None else (at, 1)
    first = acc is None
    args = [*place, q, kv]
    wide = pl.BlockSpec((rows, 512), lambda g, *_: (0, g))
    slim = pl.BlockSpec((rows, 256), lambda g, *_: (0, g))
    pair = pl.BlockSpec((rows, 256), lambda g, *_: (0, g + base))
    in_specs = [pair, pair]
    if not first:
        in_specs.append(pl.BlockSpec((rows, 512), lambda g, *_: (0, g + base)))
        args.append(far(acc) if m == n_ctx - 2 else acc)
    if last:
        out_shape = (
            jax.ShapeDtypeStruct((rows, pairs * 256), BF16),
            pltpu.HBM((rows, pairs * 256), F32),
            jax.ShapeDtypeStruct((pairs, 8, rows), F32),
        )
        out_specs = (slim, slim, pl.BlockSpec((1, 8, rows), lambda g, *_: (g, 0, 0)))
        scratch = [pltpu.VMEM((rows, 512), F32)]
    else:
        out_shape = (pltpu.HBM if m > 0 else jax.ShapeDtypeStruct)((rows, pairs * 512), F32)
        out_specs = wide
        scratch = []
    work = 2 * block * block * pairs * 4
    return pl.pallas_call(
        functools.partial(attend_body, m, n_ctx, first, last, block),
        out_shape=out_shape,
        grid_spec=pltpu.PrefetchScalarGridSpec(
            num_scalar_prefetch=2,
            grid=(pairs,),
            in_specs=in_specs,
            out_specs=out_specs,
            scratch_shapes=scratch,
        ),
        compiler_params=pltpu.CompilerParams(vmem_limit_bytes=24 << 20),
        cost_estimate=cost(work * 1024, 12 << 20),
        name="attend",
    )(*args)


def attend_back_body(m, n_ctx, first, block, where, order, q_ref, do_ref, kv_ref, lse_ref, dlt_ref, *rest):
    rest = list(rest)
    given = None if first else rest.pop(0)
    dq, dkv_ref, dka, dva = rest
    dq[...] = jnp.zeros_like(dq) if first else given[...]
    dka[...] = jnp.zeros_like(dka)
    dva[...] = jnp.zeros_like(dva)
    for q_at, k_at, diagonal in pieces(m, n_ctx, block, where, order):
        kt = kv_ref[pl.ds(k_at, block), 0:128]
        vt = kv_ref[pl.ds(k_at, block), 128:256]
        zero = jnp.zeros((block, HD), BF16)
        for hh in range(2):
            kh = kt[:, HD * hh : HD * hh + HD]
            vh = vt[:, HD * hh : HD * hh + HD]
            kx = (jnp.concatenate([kh, zero], axis=1), jnp.concatenate([zero, kh], axis=1))
            vx = (jnp.concatenate([vh, zero], axis=1), jnp.concatenate([zero, vh], axis=1))
            c = 128 * hh
            qt = q_ref[pl.ds(q_at, block), c : c + 128]
            dt = do_ref[pl.ds(q_at, block), c : c + 128]
            dvs, dks, dqs = [], [], None
            for r in range(2):
                row = 2 * hh + r
                lse = lse_ref[0, row : row + 1, pl.ds(q_at, block)]
                dlt = dlt_ref[0, row : row + 1, pl.ds(q_at, block)]
                p = jnp.exp2(mm(kx[r], qt, NT) * SCALE2 - lse)
                if diagonal:
                    key = lax.broadcasted_iota(jnp.int32, p.shape, 0)
                    query = lax.broadcasted_iota(jnp.int32, p.shape, 1)
                    p = jnp.where(key <= query, p, 0.0)
                ds = (p * (mm(vx[r], dt, NT) - dlt)).astype(BF16)
                dvs.append(mm(p.astype(BF16), dt))
                dks.append(mm(ds, qt))
                term = mm(ds, kx[r], TN)
                dqs = term if dqs is None else dqs + term
            left = half((block, 128), 0)
            dva[pl.ds(k_at, block), c : c + 128] += jnp.where(left, dvs[0], dvs[1])
            dka[pl.ds(k_at, block), c : c + 128] += jnp.where(left, dks[0], dks[1])
            dq[pl.ds(q_at, block), c : c + 128] += dqs
    for at, ref, scale in ((0, dka, 0.125), (128, dva, 1.0)):
        a = ref[...]
        a = jnp.concatenate([a[:, 0:64] + a[:, 64:128], a[:, 128:192] + a[:, 192:256]], axis=1)
        dkv_ref[:, at : at + 128] = (a * scale).astype(dkv_ref.dtype)


def attend_back(m, n_ctx, place, q, do, kv, lse, dlt, dq, block):
    rows = q.shape[0]
    pairs = kv.shape[1] // 256
    first = dq is None
    slim = pl.BlockSpec((rows, 256), lambda g, *_: (0, g))
    line = pl.BlockSpec((1, 8, rows), lambda g, *_: (g, 0, 0))
    in_specs = [slim, slim, slim, line, line]
    args = [*place, q, do, kv, lse, dlt]
    if not first:
        in_specs.append(slim)
        args.append(far(dq))
    work = 2 * block * block * pairs * 4
    return pl.pallas_call(
        functools.partial(attend_back_body, m, n_ctx, first, block),
        out_shape=(
            pltpu.HBM((rows, pairs * 256), F32),
            pltpu.HBM((rows, pairs * 256), F32) if m == 0 else jax.ShapeDtypeStruct((rows, pairs * 256), BF16),
        ),
        grid_spec=pltpu.PrefetchScalarGridSpec(
            num_scalar_prefetch=2,
            grid=(pairs,),
            in_specs=in_specs,
            out_specs=(slim, slim),
            scratch_shapes=[pltpu.VMEM((rows, 256), F32), pltpu.VMEM((rows, 256), F32)],
        ),
        compiler_params=pltpu.CompilerParams(vmem_limit_bytes=24 << 20),
        cost_estimate=cost(work * 2048, 12 << 20),
        name="attend_back",
    )(*args)


def head_mean(u):
    a = lax.broadcasted_iota(jnp.int32, (128, 128), 0) // HD
    b = lax.broadcasted_iota(jnp.int32, (128, 128), 1) // HD
    ones = jnp.where(a == b, 1.0, 0.0).astype(BF16)
    high = u.astype(BF16)
    low = (u - high.astype(F32)).astype(BF16)
    return (mm(high, ones) + mm(low, ones)) * (1.0 / HD)


def turn(u):
    lane = lax.broadcasted_iota(jnp.int32, u.shape, 1)
    return jnp.where(lane % HD < HD // 2, pltpu.roll(u, 96, 1), pltpu.roll(u, 32, 1))


def rotated(u, gain, cos, sin):
    n = u * lax.rsqrt(head_mean(u * u) + EPSILON) * gain
    return (n * cos + turn(n) * sin).astype(BF16)


def row_scale(x):
    return lax.rsqrt(jnp.mean(x * x, axis=-1, keepdims=True) + EPSILON)


def blocks_product(n, w_ref):
    count = w_ref.shape[0]
    size = w_ref.shape[1] - 16
    return sum(mm(n[:, f * size : f * size + size], w_ref[f, 0:size, :]) for f in range(count))


def key_body(x_ref, g_ref, w_ref, cos_ref, sin_ref, gain_ref, n_ref, k_ref, kv_ref):
    x = x_ref[...].astype(F32)
    n = (x * row_scale(x) * g_ref[0:1]).astype(BF16)
    n_ref[...] = n
    both = blocks_product(n, w_ref)
    width = k_ref.shape[1]
    k_ref[...] = both[:, :width]
    for t in range(width // 128):
        c = 128 * t
        kv_ref[:, 2 * c : 2 * c + 128] = rotated(
            both[:, c : c + 128], gain_ref[1:2], cos_ref[...], sin_ref[...]
        )
        kv_ref[:, 2 * c + 128 : 2 * c + 256] = both[:, width + c : width + c + 128].astype(BF16)


def query_body(n_ref, w_ref, cos_ref, sin_ref, gain_ref, u_ref, q_ref):
    u = blocks_product(n_ref[...], w_ref)
    u_ref[...] = u
    for t in range(u.shape[1] // 128):
        c = slice(128 * t, 128 * t + 128)
        q_ref[:, c] = rotated(u[:, c], gain_ref[0:1], cos_ref[...], sin_ref[...])


def row_call(body, name, step, rows, ins, outs, flops, scratch=(), aliases=None, first=0, count=None):
    ins = list(ins)
    spec = lambda w: pl.BlockSpec((step, w), lambda i: (i + first, 0))
    in_specs = []
    for n, (array, kind) in enumerate(ins):
        if isinstance(kind, str) and kind.startswith("far "):
            kind = kind[4:]
            ins[n] = (far(array), kind)
        if kind == "rows":
            in_specs.append(spec(array.shape[1]))
        elif kind == "part":
            in_specs.append(pl.BlockSpec((step, array.shape[1]), lambda i: (i, 0)))
        elif kind == "whole":
            in_specs.append(pl.BlockSpec(array.shape, lambda i, n=array.ndim: (0,) * n))
        else:
            in_specs.append(kind)
    return pl.pallas_call(
        body,
        out_shape=tuple(pltpu.HBM(o[0].shape, o[0].dtype) if len(o) > 2 else o[0] for o in outs),
        grid=(rows // step if count is None else count,),
        in_specs=in_specs,
        out_specs=tuple(spec(o[0].shape[1]) if o[1] is None else o[1] for o in outs),
        scratch_shapes=list(scratch),
        input_output_aliases=aliases or {},
        compiler_params=pltpu.CompilerParams(vmem_limit_bytes=24 << 20),
        cost_estimate=cost(flops, 1 << 20),
        name=name,
    )(*(array for array, _ in ins))


def project_keys(x, gain, packed, cos, sin, gains, kw, step):
    rows, width = x.shape
    f, r, cols = packed.shape
    shape = lambda w, t: (jax.ShapeDtypeStruct((rows, w), t), None)
    part = pl.BlockSpec((f, r, 2 * kw), lambda i: (0, 0, cols // (2 * kw) - 1))
    return row_call(
        key_body, "project_keys", step, rows,
        [(x, "far rows"), (gain, "whole"), (packed, part), (cos, "far rows"), (sin, "far rows"), (gains, "whole")],
        [shape(width, BF16) + ("far",), shape(kw, F32) + ("far",), shape(2 * kw, BF16) + ("far",)],
        rows * width * kw * 4,
    )


def project_queries(n, packed, cos, sin, gains, qw, step):
    rows, width = n.shape
    f, r, _ = packed.shape
    shape = lambda w, t: (jax.ShapeDtypeStruct((rows, w), t), None)
    part = pl.BlockSpec((f, r, qw), lambda i: (0, 0, 0))
    return row_call(
        query_body, "project_queries", step, rows,
        [(n, "far rows"), (packed, part), (cos, "far rows"), (sin, "far rows"), (gains, "whole")],
        [shape(qw, F32) + ("far",), shape(qw, BF16)],
        rows * width * qw * 2,
    )


def pair_product(own, other, w_ref, at):
    size = own.shape[1]
    base = w_ref.shape[1] // 2
    return jnp.concatenate(
        [
            mm(own, w_ref[f, at * size : at * size + size, :])
            + mm(other, w_ref[f, base + at * size : base + at * size + size, :])
            for f in range(w_ref.shape[0])
        ],
        axis=1,
    )


def join_body(at, own_ref, other_ref, w_ref, *refs):
    term = pair_product(own_ref[...], other_ref[...], w_ref, at)
    refs[-1][...] = term if len(refs) == 1 else refs[0][...] + term


def join_last_body(at, own_ref, other_ref, w_ref, x_ref, g_ref, *refs):
    r_ref, n_ref = refs[-2:]
    term = pair_product(own_ref[...], other_ref[...], w_ref, at)
    if len(refs) == 3:
        term = refs[0][...] + term
    r = x_ref[...].astype(F32) + term
    r_ref[...] = r
    n_ref[...] = (r * row_scale(r) * g_ref[0:1]).astype(BF16)


def join(x, gain, w, own, others, step):
    rows, width = x.shape
    shape = lambda w, t: (jax.ShapeDtypeStruct((rows, w), t), None)
    flops = rows * width * width
    so_far = []
    for at, (mine, other) in enumerate(zip(own, others)):
        ins = [(mine, "rows"), (other, "far rows"), (w, "whole")]
        held = [(v, "rows") for v in so_far]
        if at < len(own) - 1:
            so_far = row_call(
                functools.partial(join_body, at), "join", step, rows, ins + held, [shape(width, F32)], flops
            )
    return row_call(
        functools.partial(join_last_body, at), "join_last", step, rows,
        ins + [(x, "far rows"), (gain, "whole")] + held,
        [shape(width, F32) + ("far",), shape(width, BF16)],
        flops,
    )


def into_body(pairs, aliased, a_ref, b_ref, r_ref, dy_ref, g_ref, w_ref, mix_ref, *refs):
    d_ref, db_ref, do_ref, dlt_ref, gg_ref = refs[aliased:]
    gain = g_ref[0:1]
    r = r_ref[...]
    scale = row_scale(r)
    d = a_ref[...].astype(F32) + b_ref[...].astype(F32)
    scaled = d * gain
    back = scale * scaled - r * (scale * scale * scale) * jnp.mean(r * scaled, axis=-1, keepdims=True)

    @pl.when(pl.program_id(0) == 0)
    def _():
        gg_ref[...] = jnp.zeros_like(gg_ref)

    gg_ref[0:1] += jnp.sum(d * r * scale, axis=0, keepdims=True)
    out = dy_ref[...].astype(F32) + back
    d_ref[...] = out
    out = out.astype(BF16)
    db_ref[...] = out
    size = w_ref.shape[2]
    do = sum(mm(out[:, f * size : f * size + size], w_ref[f], NT) for f in range(w_ref.shape[0]))
    do = do.astype(BF16)
    do_ref[...] = do
    lane = lax.broadcasted_iota(jnp.int32, (8, 128), 1) // HD
    sub = lax.broadcasted_iota(jnp.int32, (8, 128), 0)
    for p in range(pairs):
        total = jnp.zeros((8, r.shape[0]), F32)
        for hh in range(2):
            c = slice(256 * p + 128 * hh, 256 * p + 128 * hh + 128)
            x = do[:, c].astype(F32) * mix_ref[:, c]
            total += row_sums(jnp.where(sub == 2 * hh + lane, 1.0, 0.0), x)
        dlt_ref[p] = total


def into_attention(a, b, resid, dy, gain, w, mix, given, first, step):
    rows, width = resid.shape
    wide = w.shape[1] // 2
    pairs = wide // 256
    own_w = pl.BlockSpec((w.shape[0], wide, w.shape[2]), lambda i: (0, 0, 0))
    shape = lambda w, t: (jax.ShapeDtypeStruct((rows, w), t), None)
    hbm = pl.BlockSpec(memory_space=pl.ANY)
    base = [(a, "far part"), (b, "far part"), (resid, "far rows"), (dy, "far rows"), (gain, "whole"), (w, own_w), (mix, "far rows")]
    given = list(given or ())
    return row_call(
        functools.partial(into_body, pairs, len(given)), "into_attention", step, rows,
        base + [(g, hbm) for g in given],
        [
            shape(width, F32) + ("far",), shape(width, BF16) + ("far",), shape(wide, BF16),
            (jax.ShapeDtypeStruct((pairs, 8, rows), F32), pl.BlockSpec((pairs, 8, step), lambda i: (0, 0, i + first))),
            (jax.ShapeDtypeStruct((8, width), F32), pl.BlockSpec((8, width), lambda i: (0, 0))),
        ],
        rows * width * wide,
        aliases={len(base) + k: k for k in range(len(given))},
        first=first, count=a.shape[0] // step,
    )


def leave_body(a_ref, b_ref, x_ref, g_ref, d_ref, out_ref):
    x = x_ref[...].astype(F32)
    scale = row_scale(x)
    scaled = (a_ref[...].astype(F32) + b_ref[...].astype(F32)) * g_ref[0:1]
    back = scale * scaled - x * (scale * scale * scale) * jnp.mean(x * scaled, axis=-1, keepdims=True)
    out_ref[...] = d_ref[...] + back


def leave(a, b, x, gain, d, step):
    rows, width = x.shape
    return row_call(
        leave_body, "leave", step, rows,
        [(a, "far rows"), (b, "far rows"), (x, "far rows"), (gain, "whole"), (d, "far rows")],
        [(jax.ShapeDtypeStruct((rows, width), F32), None)],
        rows * width * 16,
    )[0]


def rope_back_body(terms, dq_ref, q_ref, k_ref, cos_ref, sin_ref, gain_ref, *rest):
    dkv_refs, (out_ref, gg_ref) = rest[:terms], rest[terms:]
    cos, sin = cos_ref[...], sin_ref[...]

    @pl.when(pl.program_id(0) == 0)
    def _():
        gg_ref[...] = jnp.zeros_like(gg_ref)

    def one(d, u, row):
        gain = gain_ref[row : row + 1]
        dn = d * cos + turn(d * sin)
        r = lax.rsqrt(head_mean(u * u) + EPSILON)
        gd = gain * dn
        gg_ref[row : row + 1] += jnp.sum(dn * u * r, axis=0, keepdims=True)
        return (r * gd - u * (r * r * r) * head_mean(u * gd)).astype(BF16)

    qw, kw = q_ref.shape[1], k_ref.shape[1]
    for t in range(qw // 128):
        c = slice(128 * t, 128 * t + 128)
        out_ref[:, c] = one(dq_ref[:, c] * 0.125, q_ref[:, c], 0)
    for t in range(kw // 128):
        dk = sum(ref[:, 256 * t : 256 * t + 128].astype(F32) for ref in dkv_refs)
        dv = sum(ref[:, 256 * t + 128 : 256 * t + 256].astype(F32) for ref in dkv_refs)
        out_ref[:, qw + 128 * t : qw + 128 * t + 128] = one(dk, k_ref[:, 128 * t : 128 * t + 128], 1)
        out_ref[:, qw + kw + 128 * t : qw + kw + 128 * t + 128] = dv.astype(BF16)


def rope_back(dq, q_raw, k_raw, cos, sin, gains, dkvs, step):
    rows, qw = q_raw.shape
    kw = k_raw.shape[1]
    spec = lambda w: pl.BlockSpec((step, w), lambda i: (i, 0))
    fixed = pl.BlockSpec((8, 128), lambda i: (0, 0))
    return pl.pallas_call(
        functools.partial(rope_back_body, len(dkvs)),
        out_shape=(
            jax.ShapeDtypeStruct((rows, qw + 2 * kw), BF16),
            jax.ShapeDtypeStruct((8, 128), F32),
        ),
        grid=(rows // step,),
        in_specs=[spec(qw), spec(qw), spec(kw), spec(128), spec(128), fixed]
        + [spec(2 * kw)] * len(dkvs),
        out_specs=(spec(qw + 2 * kw), fixed),
        compiler_params=pltpu.CompilerParams(vmem_limit_bytes=24 << 20),
        cost_estimate=cost(rows * qw * 1600, rows * qw * 20),
        name="rope_back",
    )(*map(far, (dq, q_raw, k_raw, cos, sin)), gains, far(dkvs[0]), *dkvs[1:])


def middle_body(step, aliased, n_ref, dy_ref, wg_ref, wu_ref, wd_ref, *refs):
    h_ref, dg_ref, du_ref, dn_ref, acc = refs[aliased:]

    @pl.when(pl.program_id(0) == 0)
    def _():
        acc[...] = jnp.zeros_like(acc)

    for at in range(0, n_ref.shape[0], step):
        rows = pl.ds(at, step)
        n = n_ref[rows, :]
        g = mm(n, wg_ref[...])
        u = mm(n, wu_ref[...])
        dh = mm(dy_ref[rows, :], wd_ref[...], NT)
        s = 1.0 / (1.0 + jnp.exp2(g * (-LOG2E)))
        act = g * s
        h_ref[rows, :] = (act * u).astype(BF16)
        du_ref[rows, :] = (dh * act).astype(BF16)
        dg_ref[rows, :] = (dh * u * s * (1.0 + g * (1.0 - s))).astype(BF16)
    acc[...] += mm(dg_ref[...], wg_ref[...], NT) + mm(du_ref[...], wu_ref[...], NT)

    @pl.when(pl.program_id(0) == pl.num_programs(0) - 1)
    def _():
        dn_ref[...] = acc[...].astype(BF16)


def middle(n, dy, both, wd, given, at, parts):
    total, width = n.shape
    rows = total // parts
    hidden = both.shape[1] // 2
    tile = 256
    whole = pl.BlockSpec((rows, width), lambda j: (at, 0))
    cols = pl.BlockSpec((width, tile), lambda j: (0, j))
    more = pl.BlockSpec((width, tile), lambda j: (0, j + hidden // tile))
    outs = pl.BlockSpec((rows, tile), lambda j: (at, j))
    shape = jax.ShapeDtypeStruct((total, hidden), BF16)
    given = list(given or ())
    return pl.pallas_call(
        functools.partial(middle_body, min(rows, 256), len(given)),
        out_shape=(shape, shape, shape, jax.ShapeDtypeStruct((rows, width), BF16)),
        grid=(hidden // tile,),
        in_specs=[whole, whole, cols, more, pl.BlockSpec((tile, width), lambda j: (j, 0))]
        + [pl.BlockSpec(memory_space=pl.ANY)] * len(given),
        out_specs=(outs, outs, outs, pl.BlockSpec((rows, width), lambda j: (0, 0))),
        scratch_shapes=[pltpu.VMEM((rows, width), F32)],
        input_output_aliases={5 + k: k for k in range(len(given))},
        compiler_params=pltpu.CompilerParams(vmem_limit_bytes=24 << 20),
        cost_estimate=cost(10 * rows * width * hidden, 6 * (rows * hidden + width * hidden)),
        name="middle",
    )(n, far(dy), far(both), far(both), far(wd), *given)


def down_body(h_ref, w_ref, out_ref):
    out_ref[...] = mm(h_ref[...], w_ref[...]).astype(BF16)


def down(h, w):
    rows, hidden = h.shape
    width = w.shape[1]
    tile = min(rows, 256)
    return pl.pallas_call(
        down_body,
        out_shape=jax.ShapeDtypeStruct((rows, width), BF16),
        grid=(rows // tile,),
        in_specs=[
            pl.BlockSpec((tile, hidden), lambda j: (j, 0)),
            pl.BlockSpec((hidden, width), lambda j: (0, 0)),
        ],
        out_specs=pl.BlockSpec((tile, width), lambda j: (j, 0)),
        compiler_params=pltpu.CompilerParams(vmem_limit_bytes=24 << 20),
        cost_estimate=cost(2 * rows * width * hidden, 2 * (rows * hidden + width * hidden)),
        name="down",
    )(h, w)


def grad_body(at_ref, a_ref, z_ref, b_ref, keep_ref, give_ref):
    keep_ref[0] = mm(a_ref[...], b_ref[...], TN).astype(BF16)
    give_ref[0] = mm(z_ref[...], b_ref[...], TN).astype(BF16)


def weight_grad(a, b, parts, core):
    rows, width = a.shape
    cols = b.shape[1]
    block = width // parts
    tile = next(t for t in (2304, 1024, 512, 256, 128) if cols % t == 0)
    shape = jax.ShapeDtypeStruct((parts // 2, block, cols), BF16)
    out = pl.BlockSpec((1, block, tile), lambda j, i, c: (i, 0, j))
    return pl.pallas_call(
        grad_body,
        out_shape=(pltpu.HBM(shape.shape, BF16), pltpu.HBM(shape.shape, BF16)),
        grid_spec=pltpu.PrefetchScalarGridSpec(
            num_scalar_prefetch=1,
            grid=(cols // tile, parts // 2),
            in_specs=[
                pl.BlockSpec((rows, block), lambda j, i, c: (0, 2 * i + c[0])),
                pl.BlockSpec((rows, block), lambda j, i, c: (0, 2 * i + 1 - c[0])),
                pl.BlockSpec((rows, tile), lambda j, i, c: (0, j)),
            ],
            out_specs=(out, out),
        ),
        compiler_params=pltpu.CompilerParams(vmem_limit_bytes=24 << 20),
        cost_estimate=cost(2 * rows * width * cols, 2 * (rows * width + rows * cols + width * cols)),
        name="weight_grad",
    )(core.reshape(1), a, a, b)


def swap(x):
    n = lax.axis_size("tp")
    return lax.ppermute(x, "tp", [(i, i ^ 1) for i in range(n)])


def core_swap(x):
    n = lax.axis_size("fsdp")
    return lax.ppermute(x, "fsdp", [(i, i ^ 1) for i in range(n)])


def y_shift(x, s):
    n = lax.axis_size("fsdp")
    return lax.ppermute(x, "fsdp", [(i, (i + 2 * s) % n) for i in range(n)])


def gather_y(x):
    n = lax.axis_size("fsdp")
    y, ny = lax.axis_index("fsdp") // 2, n // 2
    mine = jnp.zeros((ny,) + x.shape, x.dtype)
    mine = lax.dynamic_update_index_in_dim(mine, x, y, 0)
    for s in range(1, ny):
        mine = lax.dynamic_update_index_in_dim(mine, y_shift(x, s), (y - s) % ny, 0)
    return mine


def gather_core(mine):
    c = lax.axis_index("fsdp") % 2
    other = core_swap(mine)
    lower = jnp.where(c == 0, mine, other)
    upper = jnp.where(c == 0, other, mine)
    return jnp.stack([lower, upper], axis=1)


def core_sums(keep, give):
    ny = keep.shape[0]
    y = lax.axis_index("fsdp") // 2
    got = core_swap(give)
    sends = [both_block(keep, got, (y + s) % ny).astype(BF16) for s in range(1, ny)]
    return keep, got, sends


def both_block(keep, got, n):
    a = lax.dynamic_index_in_dim(keep, n, 0, keepdims=False).astype(F32)
    return a + lax.dynamic_index_in_dim(got, n, 0, keepdims=False).astype(F32)


def y_sums(keep, got, sends, *after):
    parts = [y_shift(send, s + 1) for s, send in enumerate(sends)]
    keep, got, *rest = lax.optimization_barrier((keep, got, *parts, *after))
    total = both_block(keep, got, lax.axis_index("fsdp") // 2)
    for part in rest[: len(parts)]:
        total = total + part.astype(F32)
    return total.astype(BF16)


def nearest(m, i, n):
    left, right = i, n - 1 - i
    near = min(left, right)
    if m == 0:
        return 0
    if m <= 2 * near:
        return (m + 1) // 2 if m % 2 else -(m // 2)
    return m - near if right > left else -(m - near)


def choose(index, table):
    value = table[0][0]
    for array, positions in table[1:]:
        here = functools.reduce(jnp.logical_or, [index == i for i in positions])
        value = jnp.where(here, array, value)
    return value


def tie(x, *others):
    return lax.optimization_barrier((x,) + others)[0]


def tables(x):
    lane = jnp.arange(128)
    exponent = -((lane % (HD // 2)).astype(F32) * 2.0) / HD
    angle = x.astype(F32)[:, None] * (ROPE_BASE**exponent)[None, :]
    sign = jnp.where(lane % HD < HD // 2, -1.0, 1.0).astype(F32)
    return jnp.cos(angle), jnp.sin(angle) * sign[None, :]


def per_device(
    tokens, cotangent, block_order, positions,
    attn_gain, w_query, key_weight, value_weight, query_gain, key_gain,
    w_out, ffn_gain, w_gate, w_up, w_down,
):
    n_ctx = lax.axis_size("ctx")
    n_fsdp = lax.axis_size("fsdp")
    me = lax.axis_index("ctx")
    seqs, rows, width = tokens.shape
    x = tokens.reshape(seqs * rows, width)
    dy = cotangent.reshape(seqs * rows, width)
    block = rows // 2
    qw, kw = w_query.shape[1], key_weight.shape[1]
    gs, hs = attn_gain.shape[0], query_gain.shape[0]

    qkv_w = qw + 2 * kw
    small = jnp.concatenate([attn_gain, ffn_gain, query_gain, key_gain])
    small = jnp.pad(small.reshape(1, -1), ((0, 15), (0, qkv_w - 2 * (gs + hs))))
    packed = jnp.concatenate(
        [jnp.concatenate([w_query, key_weight, value_weight], axis=1), small], axis=0
    )
    mine = gather_y(packed)
    out_i = tie(w_out, packed)
    out_i = jnp.concatenate([out_i, swap(out_i)], axis=0)
    cos, sin = tables(positions.reshape(-1))
    both_i = jnp.concatenate(lax.optimization_barrier((w_gate, w_up, packed))[:2], axis=1)
    mine, out_i, cos, sin, both_i = lax.optimization_barrier((mine, out_i, cos, sin, both_i))
    both_full = lax.all_gather(both_i, "fsdp", axis=0, tiled=True)
    packed = gather_core(mine).reshape(n_fsdp, gs + 16, qkv_w)
    small = packed[:, gs].astype(F32)
    row = lambda v: jnp.broadcast_to(v.reshape(1, -1), (8, v.size))
    gain_attn = row(small[:, :gs])
    gain_ffn = row(small[:, gs : 2 * gs])
    gain_q = small[:, 2 * gs : 2 * gs + hs].reshape(-1)
    gain_k = small[:, 2 * gs + hs : 2 * (gs + hs)].reshape(-1)
    gains = jnp.stack([jnp.tile(gain_q, 2), jnp.tile(gain_k, 2)] + [jnp.zeros(128, F32)] * 6)

    step = min(256, block)
    normed_b, k_raw, kv_b = project_keys(x, gain_attn, packed, cos, sin, gains, kw, step)
    q_raw, q_b = project_queries(tie(normed_b, kv_b), packed, cos, sin, gains, qw, step)
    place = (me.astype(jnp.int32).reshape(1), block_order)
    shards = {0: kv_b}

    def shard(m):
        table = {}
        for i in range(n_ctx):
            table.setdefault(nearest(m, i, n_ctx), []).append(i)
        return choose(me, [(shards[d], where) for d, where in table.items()])

    kvs = []
    acc = None
    for t in range(1, n_ctx):
        right = [(i, i + 1) for i in range(t - 1, n_ctx - 1)]
        left = [(i, i - 1) for i in range(1, n_ctx - t + 1)]
        shards[-t] = lax.ppermute(shards[-(t - 1)], "ctx", right)
        shards[t] = lax.ppermute(shards[t - 1], "ctx", left)
        if t == 1:
            shards[-t], shards[t], q_b = lax.optimization_barrier((shards[-t], shards[t], q_b))
            out_w = lax.all_gather(tie(out_i, kv_b), "fsdp", axis=0, tiled=False)
            down_full = lax.all_gather(tie(w_down, q_b), "fsdp", axis=1, tiled=True)
            continue
        while len(kvs) < t:
            kvs.append(shard(len(kvs)))
            acc = attend(len(kvs) - 1, n_ctx, place, q_b, kvs[-1], acc, False, block)
        shards[-t], shards[t], acc = lax.optimization_barrier((shards[-t], shards[t], acc))
        if t == 2:
            acc = tie(acc, both_full)
    while len(kvs) < n_ctx - 1:
        kvs.append(shard(len(kvs)))
        acc = attend(len(kvs) - 1, n_ctx, place, q_b, kvs[-1], acc, False, block)
    m = n_ctx - 1
    kvs.append(shard(m))
    pairs = kw // 128
    mixes, others = [], []
    last_q = q_b
    for p in range(pairs):
        mixes.append(attend(m, n_ctx, place, last_q, kvs[m], acc, True, block, p))
        last_q = tie(q_b, mixes[-1][0])
        others.append(swap(mixes[-1][0]))
    mixed_b = jnp.concatenate([piece[0] for piece in mixes], axis=1)
    mix = jnp.concatenate([piece[1] for piece in mixes], axis=1)
    lse = jnp.concatenate([piece[2] for piece in mixes], axis=0)

    own = [piece[0] for piece in mixes]
    resid, two_b = join(x, gain_ffn, out_w, own, others, step)

    core = lax.axis_index("fsdp") % 2

    parts = 2
    given, d_parts, d_others = None, [], []
    two_t = two_b
    for at in range(parts):
        *given, d_part = middle(two_t, dy, both_full, down_full, given, at, parts)
        two_t = tie(two_b, d_part)
        d_parts.append(d_part)
        d_others.append(swap(d_part))
    hidden, dgate, dup = given
    down_w = weight_grad(dy, hidden, n_fsdp, core)
    two_t, hidden_t = lax.optimization_barrier((two_b, hidden, down_w, d_others[0]))[:2]
    gate_w = weight_grad(two_t, dgate, n_fsdp, core)
    up_w = weight_grad(two_t, dup, n_fsdp, core)
    down_part = down(hidden_t, down_full)
    d_others[-1], down_w, gate_w, up_w, down_part = lax.optimization_barrier(
        (d_others[-1], down_w, gate_w, up_w, down_part)
    )
    down_c, gate_c, up_c = core_sums(*down_w), core_sums(*gate_w), core_sums(*up_w)

    given, ffn_gain_g = None, 0.0
    per = rows * seqs // parts // step
    for at in range(parts):
        *given, g = into_attention(
            d_parts[at], d_others[at], resid, dy, gain_ffn, out_w, mix, given, at * per, step
        )
        ffn_gain_g = ffn_gain_g + g[0]
    d_resid, d_resid_b, do, dlt = given
    do = tie(do, *down_c[2], *gate_c[2])

    grads = [None] * n_ctx
    got = {}
    dq = None
    for m in reversed(range(n_ctx)):
        dq, grads[m] = attend_back(m, n_ctx, place, q_b, do, kvs[m], lse, dlt, dq, block)
        if m == 0:
            break
        sends = []
        for side in (1, -1):
            table = {}
            for i in range(n_ctx):
                for k in range(1, n_ctx):
                    if nearest(k, i, n_ctx) == side * m:
                        table.setdefault(k, []).append(i)
            send = choose(me, [(grads[k], where) for k, where in table.items()])
            if side in got:
                send = (send.astype(F32) + got[side].astype(F32)).astype(BF16)
            sends.append(send)
            senders = sorted(i for where in table.values() for i in where)
            got[side] = lax.ppermute(send, "ctx", [(i, i + side) for i in senders])
        if m == n_ctx - 1:
            down_other = swap(tie(down_part, dq))
            down_s = y_sums(*down_c)
            sends += [down_s] + up_c[2]
        if m == max(n_ctx - 2, 1):
            gate_s = y_sums(*gate_c, dq)
            sends.append(gate_s)
            out_g = weight_grad(tie(d_resid_b, dq), mixed_b, n_fsdp, core)
            down_s, gate_s = lax.psum((down_s, gate_s), "ctx")
        if m == 1:
            sends += [*out_g]
        dq = tie(dq, *sends)
    dq, down_other = lax.optimization_barrier((dq, down_other))
    out_s = y_sums(*core_sums(*out_g))
    home = [grads[0]] + list(got.values())
    output = (tie(resid, dq) + (down_part.astype(F32) + down_other.astype(F32))).astype(BF16)

    d_qkv, head_gain = rope_back(dq, q_raw, k_raw, cos, sin, gains, home, step)
    qkv_p = weight_grad(normed_b, d_qkv, n_fsdp, core)
    qkv_c = core_sums(*lax.optimization_barrier((*qkv_p, gate_s))[:2])
    w_qkv = packed[:, :gs].reshape(n_fsdp * gs, qkv_w)
    normed_part = mm(d_qkv, w_qkv, NT)

    head_gain = head_gain[:2, :HD] + head_gain[:2, HD:]
    xf = x.astype(F32)
    inv_one = lax.rsqrt(jnp.mean(xf * xf, axis=-1, keepdims=True) + EPSILON)
    attn_gain_g = jnp.sum(normed_part * (xf * inv_one), axis=0)
    small_g = jnp.concatenate(
        [
            attn_gain_g.reshape(n_fsdp, gs),
            0.5 * ffn_gain_g.reshape(n_fsdp, gs),
            head_gain[0].reshape(n_fsdp, hs),
            head_gain[1].reshape(n_fsdp, hs),
        ],
        axis=1,
    )
    small_g = (small_g + swap(small_g)).astype(BF16).reshape(n_fsdp // 2, 2, 1, -1)
    normed_part = tie(normed_part.astype(BF16), small_g)
    normed_other = swap(normed_part)
    small_s = y_sums(
        *core_sums(
            lax.dynamic_index_in_dim(small_g, core, 1, keepdims=False),
            lax.dynamic_index_in_dim(small_g, 1 - core, 1, keepdims=False),
        )
    )
    last = jnp.concatenate([y_sums(*qkv_c), out_s], axis=1)
    small_s = jnp.pad(small_s, ((0, 15), (0, last.shape[1] - small_s.shape[1])))
    last = jnp.concatenate([last, small_s], axis=0)
    up_s = y_sums(*up_c)
    last, up_s, gate_s, down_s = lax.optimization_barrier((last, up_s, gate_s, down_s))
    last, up_s = lax.psum((last, up_s), "ctx")
    input_grad = leave(normed_part, normed_other, x, gain_attn, d_resid, step)
    last = tie(last, input_grad)
    q_s, k_s, v_s = last[:gs, :qw], last[:gs, qw : qw + kw], last[:gs, qw + kw : qkv_w]
    out_s = last[:gs, qkv_w:]
    small_s = last[gs : gs + 1, : 2 * (gs + hs)]
    down_s, gate_s, up_s, out_s, q_s, k_s, v_s = (
        v.astype(F32) for v in (down_s, gate_s, up_s, out_s, q_s, k_s, v_s)
    )
    small_g = small_s[0].astype(F32)
    return (
        output.reshape(tokens.shape),
        input_grad.reshape(tokens.shape),
        small_g[:gs],
        q_s,
        k_s,
        v_s,
        small_g[2 * gs : 2 * gs + hs],
        small_g[2 * gs + hs :],
        out_s.T,
        small_g[gs : 2 * gs],
        gate_s,
        up_s,
        down_s.T,
    )


def solution(mesh):
    rows = P("fsdp", "ctx", None)
    ins = P("fsdp", "tp")
    outs = P("tp", "fsdp")
    one = P("fsdp")
    return jax.shard_map(
        per_device,
        mesh=mesh,
        in_specs=(
            rows, rows, P(), P("fsdp", "ctx"), one, ins, ins, ins, one, one, outs, one, ins, ins, outs,
        ),
        out_specs=(rows, rows, one, ins, ins, ins, one, one, outs, one, ins, ins, outs),
        check_vma=False,
    )
```
